128 devices in a mesh: seq: 128 (over x, y, z, core).
Axes of the slice: x: 4, y: 4, z: 4, core: 2. Of those that a mesh axis runs over, the one named last changes fastest.
Arguments:
- tokens: bfloat16 [65536, 2048], P('seq'), may hold values from -48 to 48
- w_row: bfloat16 [2048, 3072], replicated, may hold values from -0.21875 to 0.21875
- w_column: bfloat16 [2048, 3072], replicated, may hold values from -0.21875 to 0.21875
Outputs:
- attended: bfloat16 [65536, 2048], P('seq')
The draws below stay inside these ranges and needn't reach their ends.
All inputs are finite; a program needn't handle non-finite values.
Results may differ from the reference program's by a relative error of at most 0.011.
The reference program's roundings to bfloat16 on the way count: a program that leaves them out, or rounds other values in their place, can miss the bound.
Values may be sent and summed in bfloat16 or wider, within the bound.
No kernel may reach another device: no remote copies, remote signals or barrier semaphores. Data moves between devices by JAX's collectives and lax.ppermute only.
A program may use at most 128 MiB of HBM per device.

```python
import jax
import jax.numpy as jnp
from jax import lax

D = 2048
HEAD = 128
HEADS = 8
STRIDE = 1024
TOKENS = 65536
ROWS = 64


def draw_tokens(key, part):
    base = jnp.clip(jax.random.normal(key, (TOKENS, D), jnp.float32), -6.0, 6.0)
    return base.astype(jnp.bfloat16)


def bell_draw(own_key, shape, deviation, bound, held_as=jnp.bfloat16):
    entries = deviation * jax.random.normal(own_key, shape, jnp.float32)
    return jnp.clip(entries, min=-bound, max=bound).astype(held_as)


def setup_inputs(seed: int = 0) -> dict:
    splits = jax.random.split(jax.random.key(seed), 4)
    return {
        "tokens": draw_tokens(jax.random.fold_in(splits[3], 71), 0),
        "w_row": bell_draw(splits[1], (D, 3 * HEADS * HEAD), (D // 3) ** -0.5, 0.21875),
        "w_column": bell_draw(splits[2], (D, 3 * HEADS * HEAD), (D // 3) ** -0.5, 0.21875),
    }


def softmax_rounded(scores):
    top = jnp.max(scores, axis=-1, keepdims=True)
    expd = jnp.exp(scores - top)
    return (expd / jnp.sum(expd, axis=-1, keepdims=True)).astype(jnp.bfloat16)


def reference(tokens, w_row, w_column):
    width = HEADS * HEAD
    scale = 1.0 / (HEAD ** 0.5)
    row_proj = jnp.dot(tokens, w_row, preferred_element_type=jnp.float32).astype(jnp.bfloat16)
    col_proj = jnp.dot(tokens, w_column, preferred_element_type=jnp.float32).astype(jnp.bfloat16)
    query = row_proj[:, :width]
    keyval = jnp.concatenate([jnp.zeros((STRIDE, 2 * width), jnp.bfloat16), row_proj[:, width:]], axis=0)
    block = STRIDE

    def band_block(index):
        start = (index * block).astype(jnp.int32)
        qpart = lax.dynamic_slice_in_dim(query, start, block, 0).reshape(block, HEADS, HEAD).astype(jnp.float32)
        kvpart = lax.dynamic_slice_in_dim(keyval, start, STRIDE + block, 0)
        keys = kvpart[:, :width].reshape(-1, HEADS, HEAD).astype(jnp.float32)
        values = kvpart[:, width:].reshape(-1, HEADS, HEAD).astype(jnp.float32)
        scores = jnp.einsum('thd,uhd->htu', qpart, keys) * scale
        tpos = jnp.arange(block, dtype=jnp.int32)[:, None]
        upos = jnp.arange(STRIDE + block, dtype=jnp.int32)[None, :]
        diff = tpos + STRIDE - upos
        keypos = start - STRIDE + upos
        allowed = (diff >= 0) & (diff <= STRIDE - 1) & (keypos >= 0)
        scores = jnp.where(allowed[None], scores, -jnp.inf)
        weights = softmax_rounded(scores).astype(jnp.float32)
        out = jnp.einsum('htu,uhd->thd', weights, values)
        return out.astype(jnp.bfloat16).reshape(block, width)

    band_out = lax.map(band_block, jnp.arange(TOKENS // block, dtype=jnp.int32)).reshape(TOKENS, width)

    group = min(64, STRIDE)
    columns = col_proj.reshape(ROWS, STRIDE, 3 * width).transpose(1, 0, 2)
    columns = columns.reshape(STRIDE // group, group, ROWS, 3 * width)

    def column_block(part):
        qpart = part[:, :, :width].reshape(group, ROWS, HEADS, HEAD).astype(jnp.float32)
        keys = part[:, :, width:2 * width].reshape(group, ROWS, HEADS, HEAD).astype(jnp.float32)
        values = part[:, :, 2 * width:].reshape(group, ROWS, HEADS, HEAD).astype(jnp.float32)
        scores = jnp.einsum('crhd,cshd->chrs', qpart, keys) * scale
        rpos = jnp.arange(ROWS, dtype=jnp.int32)
        allowed = rpos[None, :] <= rpos[:, None]
        scores = jnp.where(allowed[None, None], scores, -jnp.inf)
        weights = softmax_rounded(scores).astype(jnp.float32)
        out = jnp.einsum('chrs,cshd->crhd', weights, values)
        return out.astype(jnp.bfloat16).reshape(group, ROWS, width)

    col_out = lax.map(column_block, columns).reshape(STRIDE, ROWS, width)
    col_out = col_out.transpose(1, 0, 2).reshape(TOKENS, width)
    return jnp.concatenate([band_out, col_out], axis=1)
```

```python
import functools

import jax
import jax.numpy as jnp
from jax import lax
from jax.experimental import pallas as pl
from jax.experimental.pallas import tpu as pltpu
from jax.sharding import PartitionSpec as P

HEAD = 128
HEADS = 8
STRIDE = 1024
HALF = 512
SCALE = 1.0 / HEAD**0.5
NEG = -1e30
VMEM_LIMIT = 48 << 20
STAT_ROWS = 32
PAYLOAD = HALF + STAT_ROWS


def params():
    return pltpu.CompilerParams(vmem_limit_bytes=VMEM_LIMIT)


def cost(flops, data):
    return pl.CostEstimate(flops=flops, bytes_accessed=data, transcendentals=0)


def project_kernel(core_ref, x_ref, w_ref, *refs):
    q_ref, kv_ref = refs[-2:]
    part = pl.program_id(0)
    value = jnp.dot(x_ref[...], w_ref[...], preferred_element_type=jnp.float32)
    value = value.astype(jnp.bfloat16)

    @pl.when(part == 0)
    def _():
        q_ref[...] = value

    @pl.when(part > 0)
    def _():
        kv_ref[...] = value


def project_band(core, tokens, w_row, own, before=None):
    depth = tokens.shape[1]
    half = (lambda c: c[0]) if own else (lambda c: 1 - c[0])
    aliased = [] if before is None else list(before)
    return pl.pallas_call(
        project_kernel,
        grid_spec=pltpu.PrefetchScalarGridSpec(
            num_scalar_prefetch=1,
            grid=(3,),
            in_specs=[
                pl.BlockSpec((HALF, depth), lambda j, c: (0, 0)),
                pl.BlockSpec((depth, HALF), lambda j, c: (0, 2 * j + c[0])),
            ]
            + [pl.BlockSpec(memory_space=pl.ANY)] * len(aliased),
            out_specs=[
                pl.BlockSpec((HALF, HALF), lambda j, c: (half(c), 0)),
                pl.BlockSpec((HALF, HALF), lambda j, c: (half(c), jnp.maximum(j - 1, 0))),
            ],
        ),
        out_shape=[
            jax.ShapeDtypeStruct((STRIDE, HALF), jnp.bfloat16),
            jax.ShapeDtypeStruct((STRIDE, STRIDE), jnp.bfloat16),
        ],
        input_output_aliases={3 + i: i for i in range(len(aliased))},
        compiler_params=params(),
        cost_estimate=cost(2 * HALF * depth * 3 * HALF, (HALF * depth + depth * 3 * HALF + HALF * 3 * HALF) * 2),
        name="project_band",
    )(core, tokens, w_row, *aliased)


def attend(queries, keys, values_t, allowed):
    scores = lax.dot_general(
        keys, queries, (((1,), (1,)), ((), ())), preferred_element_type=jnp.float32
    )
    if allowed is not None:
        scores = jnp.where(allowed, scores, NEG)
    top = jnp.max(scores, axis=0, keepdims=True)
    expd = jnp.exp((scores - top) * SCALE)
    total = jnp.sum(expd, axis=0, keepdims=True)
    out = jnp.dot(values_t, expd.astype(jnp.bfloat16), preferred_element_type=jnp.float32)
    return out * (1.0 / total), top, total


def split3(value):
    high = value.astype(jnp.bfloat16).astype(jnp.float32)
    rest = value - high
    mid = rest.astype(jnp.bfloat16).astype(jnp.float32)
    return high, mid, rest - mid


def band_kernel(earlier, core_ref, q_ref, k_ref, v_ref, same_ref, cross_ref, stat_ref):
    head = pl.program_id(0)
    core = core_ref[0]
    block = 256
    values_t = v_ref[...].astype(jnp.float32).T.astype(jnp.bfloat16)
    for part in range(STRIDE // block):
        low, high = (part * block, STRIDE) if earlier else (0, (part + 1) * block)
        shape = (high - low, block)
        kpos = low + lax.broadcasted_iota(jnp.int32, shape, 0)
        qpos = part * block + lax.broadcasted_iota(jnp.int32, shape, 1)
        allowed = kpos > qpos if earlier else kpos <= qpos
        out, top, total = attend(
            q_ref[part * block : (part + 1) * block, :],
            k_ref[low:high, :],
            values_t[:, low:high],
            allowed,
        )
        out = out.astype(jnp.bfloat16)
        half, column = divmod(part * block, HALF)
        rows = pl.ds(pl.multiple_of(head * HEAD, HEAD), HEAD)

        @pl.when(core == half)
        def _():
            same_ref[rows, column : column + block] = out

        @pl.when(core != half)
        def _():
            cross_ref[rows, column : column + block] = out

        stats = jnp.concatenate(
            list(split3(top)) + list(split3(total)) + [jnp.zeros((2, block), jnp.float32)], axis=0
        )
        stat_ref[head, :, part * block : (part + 1) * block] = stats

    @pl.when(head == 3)
    def _():
        stats = jnp.concatenate([stat_ref[h] for h in range(4)], axis=0).astype(jnp.bfloat16)
        for half in range(2):
            piece = stats[:, half * HALF : (half + 1) * HALF]

            @pl.when(core == half)
            def _():
                same_ref[HALF:PAYLOAD, :] = piece

            @pl.when(core != half)
            def _():
                cross_ref[HALF:PAYLOAD, :] = piece


def band_part(earlier, core, query, keyval):
    whole = pl.BlockSpec((PAYLOAD, HALF), lambda h, c: (0, 0))
    return pl.pallas_call(
        functools.partial(band_kernel, earlier),
        grid_spec=pltpu.PrefetchScalarGridSpec(
            num_scalar_prefetch=1,
            grid=(4,),
            in_specs=[
                pl.BlockSpec((STRIDE, HEAD), lambda h, c: (0, h)),
                pl.BlockSpec((STRIDE, HEAD), lambda h, c: (0, h)),
                pl.BlockSpec((STRIDE, HEAD), lambda h, c: (0, 4 + h)),
            ],
            out_specs=[whole, whole],
            scratch_shapes=[pltpu.VMEM((4, 8, STRIDE), jnp.float32)],
        ),
        out_shape=[jax.ShapeDtypeStruct((PAYLOAD, HALF), jnp.bfloat16)] * 2,
        compiler_params=params(),
        cost_estimate=cost(5 * 10**9, 8 << 20),
        name="band_earlier" if earlier else "band_local",
    )(core, query, keyval, keyval)


def column_kernel(q_ref, k_ref, v_ref, o_ref, *, group):
    rows = q_ref.shape[0]
    block = 256
    values_t = v_ref[...].astype(jnp.float32).T.astype(jnp.bfloat16)
    for part in range(rows // block):
        high = (part + 1) * block
        shape = (high, block)
        kpos = lax.broadcasted_iota(jnp.int32, shape, 0)
        qpos = part * block + lax.broadcasted_iota(jnp.int32, shape, 1)
        allowed = (kpos <= qpos) & (((qpos - kpos) & (group - 1)) == 0)
        out, _, _ = attend(
            q_ref[part * block : high, :], k_ref[:high, :], values_t[:, :high], allowed
        )
        o_ref[part * block : high, :] = out.T.astype(jnp.bfloat16)


def column_attention(projected, group):
    rows = projected.shape[0]
    spec = lambda third: pl.BlockSpec((rows, HEAD), lambda h: (0, third * HEADS + h))
    return pl.pallas_call(
        functools.partial(column_kernel, group=group),
        grid=(HEADS,),
        in_specs=[spec(0), spec(1), spec(2)],
        out_specs=pl.BlockSpec((rows, HEAD), lambda h: (0, h)),
        out_shape=jax.ShapeDtypeStruct((rows, HEADS * HEAD), jnp.bfloat16),
        compiler_params=params(),
        cost_estimate=cost(3 * 10**9, 4 << 20),
        name="column_attention",
    )(projected, projected, projected)


def merge_kernel(flags_ref, local_ref, earlier_ref, o_ref):
    has_earlier = flags_ref[1] > 0
    for head in range(4):
        def stats(ref):
            s = ref[0, HALF : HALF + STAT_ROWS, :].astype(jnp.float32)[8 * head : 8 * head + 8]
            return s[0:1] + s[1:2] + s[2:3], s[3:4] + s[4:5] + s[5:6]

        top_l, sum_l = stats(local_ref)
        top_e, sum_e = stats(earlier_ref)
        top_e = jnp.where(has_earlier, top_e, NEG)
        top = jnp.maximum(top_l, top_e)
        weight_l = jnp.exp((top_l - top) * SCALE) * sum_l
        weight_e = jnp.exp((top_e - top) * SCALE) * sum_e
        weight_e = jnp.where(has_earlier, weight_e, 0.0)
        inverse = 1.0 / (weight_l + weight_e)
        rows = slice(head * HEAD, (head + 1) * HEAD)
        out_l = local_ref[0, rows, :].astype(jnp.float32)
        out_e = earlier_ref[0, rows, :].astype(jnp.float32)
        out = out_l * (weight_l * inverse) + out_e * (weight_e * inverse)
        o_ref[:, rows] = out.T.astype(jnp.bfloat16)


def merge_band(flags, local, earlier):
    return pl.pallas_call(
        merge_kernel,
        grid_spec=pltpu.PrefetchScalarGridSpec(
            num_scalar_prefetch=1,
            grid=(2,),
            in_specs=[
                pl.BlockSpec((1, PAYLOAD, HALF), lambda j, c: (j, 0, 0)),
                pl.BlockSpec((1, PAYLOAD, HALF), lambda j, c: (j, 0, 0)),
            ],
            out_specs=pl.BlockSpec((HALF, HALF), lambda j, c: (0, j + c[0] - 2 * j * c[0])),
        ),
        out_shape=jax.ShapeDtypeStruct((HALF, 2 * HALF), jnp.bfloat16),
        compiler_params=params(),
        cost_estimate=cost(10**7, 4 << 20),
        name="merge_band",
    )(flags, local, earlier)


def on_device(tokens, w_row, w_column):
    count = lax.axis_size("seq")
    chips = count // 2
    rank = lax.axis_index("seq")
    core = (rank % 2).astype(jnp.int32)
    core_arr = core.reshape(1)
    flags = jnp.stack([core, (rank >= 2).astype(jnp.int32)])
    group = HALF // chips
    same_core = [list(range(0, count, 2)), list(range(1, count, 2))]
    swap = [(d, d ^ 1) for d in range(count)]

    def exchange(value):
        width = value.shape[1]
        value = lax.all_to_all(
            value.reshape(chips, group, width), "seq", split_axis=0, concat_axis=0,
            axis_index_groups=same_core, tiled=True,
        )
        return value.reshape(HALF, width)

    columns = exchange(tokens)
    sibling = lax.ppermute(tokens, "seq", swap)

    projected = project_band(core_arr, tokens, w_row, True)
    query, keyval = project_band(core_arr, sibling, w_row, False, projected)
    next_query = lax.ppermute(query, "seq", [(d, d - 2) for d in range(2, count)])
    local_same, local_cross = band_part(False, core_arr, query, keyval)
    local_cross = lax.ppermute(local_cross, "seq", swap)
    early_same, early_cross = band_part(True, core_arr, next_query, keyval)
    early_same = lax.ppermute(early_same, "seq", [(d, d + 2) for d in range(count - 2)])
    early_cross = lax.ppermute(
        early_cross, "seq", [(d, (d + 2) ^ 1) for d in range(count - 2)]
    )

    col_proj = jnp.dot(columns, w_column, preferred_element_type=jnp.float32).astype(jnp.bfloat16)
    col_out = exchange(column_attention(col_proj, group))
    band_out = merge_band(
        flags, jnp.stack([local_same, local_cross]), jnp.stack([early_same, early_cross])
    )
    return jnp.concatenate([band_out, col_out], axis=1)


def solution(mesh):
    in_specs = (P("seq", None), P(), P())
    out_specs = P("seq", None)
    return jax.shard_map(
        on_device, mesh=mesh, in_specs=in_specs, out_specs=out_specs, check_vma=False
    )
```

```python
import functools
import math

import jax
import jax.numpy as jnp
from jax import lax
from jax.experimental import pallas as pl
from jax.experimental.pallas import tpu as pltpu
from jax.sharding import PartitionSpec as P

HEAD = 128
HEADS = 8
STRIDE = 1024
HALF = 512
BLOCK = 256
SCALE2 = math.log2(math.e) / math.sqrt(HEAD)
NEG = -1e30
VMEM_LIMIT = 28 << 20


def params():
    return pltpu.CompilerParams(vmem_limit_bytes=VMEM_LIMIT)


def cost(us):
    return pl.CostEstimate(flops=int(us * 10**9), bytes_accessed=1 << 14, transcendentals=0)


def halves(core, own_ref, sibling_ref, w, store):
    for place, ref in ((core, own_ref), (1 - core, sibling_ref)):
        value = jnp.dot(ref[...], w, preferred_element_type=jnp.float32)
        store(pl.ds(pl.multiple_of(place * HALF, HALF), HALF), value)


def query_kernel(core_ref, own_ref, sibling_ref, w_ref, a_ref, b_ref):
    for step, ref in enumerate((a_ref, b_ref)):
        @pl.when(pl.program_id(0) == step)
        def _():
            def store(rows, value):
                ref[rows, :] = value.astype(jnp.bfloat16)

            halves(core_ref[0], own_ref, sibling_ref, w_ref[...], store)


def keyval_kernel(core_ref, own_ref, sibling_ref, w_ref, k_ref, vt_ref):
    @pl.when(pl.program_id(0) < 2)
    def _():
        def store(rows, value):
            k_ref[rows, :] = value.astype(jnp.bfloat16)

        halves(core_ref[0], own_ref, sibling_ref, w_ref[...], store)

    @pl.when(pl.program_id(0) >= 2)
    def _():
        def store(rows, value):
            vt_ref[:, rows] = value.T.astype(jnp.bfloat16)

        halves(core_ref[0], own_ref, sibling_ref, w_ref[...], store)


def project(kernel, steps, first, core, tokens, sibling, w_row, out_specs, out_shape, name):
    depth = tokens.shape[1]
    whole = pl.BlockSpec((HALF, depth), lambda j, c: (0, 0))
    weights = pl.BlockSpec(
        (depth, BLOCK), lambda j, c: (0, 4 * (first + j // 2) + 2 * c[0] + j % 2)
    )
    return pl.pallas_call(
        kernel,
        grid_spec=pltpu.PrefetchScalarGridSpec(
            num_scalar_prefetch=1,
            grid=(steps,),
            in_specs=[whole, whole, weights],
            out_specs=out_specs,
        ),
        out_shape=out_shape,
        compiler_params=params(),
        cost_estimate=cost(1.3 * steps),
        name=name,
    )(core, tokens, sibling, w_row)


def project_query(core, tokens, sibling, w_row):
    spec = pl.BlockSpec((STRIDE, BLOCK), lambda j, c: (0, 0))
    shape = jax.ShapeDtypeStruct((STRIDE, BLOCK), jnp.bfloat16)
    return project(
        query_kernel, 2, 0, core, tokens, sibling, w_row, [spec, spec], [shape, shape], "query"
    )


def project_keyval(core, tokens, sibling, w_row):
    return project(
        keyval_kernel, 4, 1, core, tokens, sibling, w_row,
        [
            pl.BlockSpec((STRIDE, BLOCK), lambda j, c: (0, jnp.minimum(j, 1))),
            pl.BlockSpec((BLOCK, STRIDE), lambda j, c: (jnp.maximum(j - 2, 0), 0)),
        ],
        [
            jax.ShapeDtypeStruct((STRIDE, HALF), jnp.bfloat16),
            jax.ShapeDtypeStruct((HALF, STRIDE), jnp.bfloat16),
        ],
        "keyval",
    )


def score_blocks(query, key_ref, columns, spans):
    return [
        lax.dot_general(
            key_ref[low:high, columns], query, (((1,), (1,)), ((), ())),
            preferred_element_type=jnp.float32,
        )
        for low, high in spans
    ]


def softmax_out(scores, biases, value_t_blocks):
    scores = [s if b is None else s + b for s, b in zip(scores, biases)]
    top = functools.reduce(jnp.maximum, [jnp.max(s, axis=0, keepdims=True) for s in scores])
    expd = [jnp.exp2((s - top) * SCALE2) for s in scores]
    total = sum(jnp.sum(e, axis=0, keepdims=True) for e in expd)
    out = sum(
        jnp.dot(v, e.astype(jnp.bfloat16), preferred_element_type=jnp.float32)
        for v, e in zip(value_t_blocks, expd)
    )
    return out * (1.0 / total), top, total


def pipelined(jobs, ahead, start, finish):
    pending, results = [], {}
    for job in jobs:
        pending.append((job, start(*job)))
        if len(pending) > ahead:
            first, value = pending.pop(0)
            results[first] = finish(*first, value)
    for first, value in pending:
        results[first] = finish(*first, value)
    return results


def split3(value):
    high = value.astype(jnp.bfloat16).astype(jnp.float32)
    rest = value - high
    mid = rest.astype(jnp.bfloat16).astype(jnp.float32)
    return [high, mid, rest - mid]


def band_kernel(
    earlier, heads, ahead, core_ref, q_ref, k_ref, vt_ref, same_ref, cross_ref, stat_ref, bias_ref
):
    step = pl.program_id(0)
    core = core_ref[0]
    parts = STRIDE // BLOCK

    @pl.when(step == 0)
    def _():
        kpos = lax.broadcasted_iota(jnp.int32, (BLOCK, BLOCK), 0)
        qpos = lax.broadcasted_iota(jnp.int32, (BLOCK, BLOCK), 1)
        allowed = kpos > qpos if earlier else kpos <= qpos
        bias_ref[...] = jnp.where(allowed, 0.0, NEG)

    def spans(part):
        low, high = part * BLOCK, (part + 1) * BLOCK
        rest = (high, STRIDE) if earlier else (0, low)
        return [(low, high)] + ([rest] if rest[0] < rest[1] else [])

    def columns(head):
        return slice(head * HEAD, (head + 1) * HEAD)

    def start(part, head):
        query = q_ref[part * BLOCK : (part + 1) * BLOCK, columns(head)]
        return score_blocks(query, k_ref, columns(head), spans(part))

    def finish(part, head, scores):
        values = [vt_ref[columns(head), low:high] for low, high in spans(part)]
        out, top, total = softmax_out(scores, [bias_ref[...], None], values)
        return out.astype(jnp.bfloat16), top, total

    jobs = [(part, head) for part in range(parts) for head in range(2)]
    results = pipelined(jobs, ahead, start, finish)
    for head in range(2):
        stats = [
            jnp.concatenate(
                split3(results[part, head][1])
                + split3(results[part, head][2])
                + [jnp.zeros((2, BLOCK), jnp.float32)],
                axis=0,
            )
            for part in range(parts)
        ]
        stat_ref[step * 2 + head] = jnp.concatenate(stats, axis=1)
    rows = pl.ds(pl.multiple_of(step * 2 * HEAD, 2 * HEAD), 2 * HEAD)
    for half in range(2):
        piece = jnp.concatenate(
            [
                jnp.concatenate([results[2 * half + part, head][0] for part in range(2)], axis=1)
                for head in range(2)
            ],
            axis=0,
        )

        @pl.when(core == half)
        def _():
            same_ref[rows, :] = piece

        @pl.when(core != half)
        def _():
            cross_ref[rows, :] = piece

    @pl.when(step == heads // 2 - 1)
    def _():
        stats = jnp.concatenate([stat_ref[h] for h in range(heads)], axis=0).astype(jnp.bfloat16)
        for half in range(2):
            piece = stats[:, half * HALF : (half + 1) * HALF]

            @pl.when(core == half)
            def _():
                same_ref[heads * HEAD :, :] = piece

            @pl.when(core != half)
            def _():
                cross_ref[heads * HEAD :, :] = piece


def band_part(earlier, core, query, keys, values_t, first=0):
    heads = query.shape[1] // HEAD
    payload = heads * (HEAD + 8)
    whole = pl.BlockSpec((payload, HALF), lambda h, c: (0, 0))
    return pl.pallas_call(
        functools.partial(band_kernel, earlier, heads, 2 if earlier else 4),
        grid_spec=pltpu.PrefetchScalarGridSpec(
            num_scalar_prefetch=1,
            grid=(heads // 2,),
            in_specs=[
                pl.BlockSpec((STRIDE, 2 * HEAD), lambda h, c: (0, h)),
                pl.BlockSpec((STRIDE, 2 * HEAD), lambda h, c: (0, first + h)),
                pl.BlockSpec((2 * HEAD, STRIDE), lambda h, c: (first + h, 0)),
            ],
            out_specs=[whole, whole],
            scratch_shapes=[
                pltpu.VMEM((heads, 8, STRIDE), jnp.float32),
                pltpu.VMEM((BLOCK, BLOCK), jnp.float32),
            ],
        ),
        out_shape=[jax.ShapeDtypeStruct((payload, HALF), jnp.bfloat16)] * 2,
        compiler_params=params(),
        cost_estimate=cost(1.7 * heads),
        name="band_earlier" if earlier else "band_local",
    )(core, query, keys, values_t)


def column_kernel(group, x_ref, wq_ref, wk_ref, wv_ref, o_ref, k_ref, bias_ref):
    parts = HALF // BLOCK

    @pl.when(pl.program_id(0) == 0)
    def _():
        kpos = lax.broadcasted_iota(jnp.int32, (BLOCK, BLOCK), 0)
        qpos = lax.broadcasted_iota(jnp.int32, (BLOCK, BLOCK), 1)
        column = ((qpos - kpos) & (group - 1)) == 0
        bias_ref[0] = jnp.where(column, 0.0, NEG)
        bias_ref[1] = jnp.where(column & (kpos <= qpos), 0.0, NEG)

    x = x_ref[...]
    query = jnp.dot(x, wq_ref[...], preferred_element_type=jnp.float32).astype(jnp.bfloat16)
    keys = jnp.dot(x, wk_ref[...], preferred_element_type=jnp.float32).astype(jnp.bfloat16)
    k_ref[...] = keys
    values_t = jnp.dot(x, wv_ref[...], preferred_element_type=jnp.float32).T.astype(jnp.bfloat16)

    def spans(part):
        return [(block * BLOCK, (block + 1) * BLOCK) for block in range(part + 1)]

    def columns(head):
        return slice(head * HEAD, (head + 1) * HEAD)

    def start(part, head):
        part_query = query[part * BLOCK : (part + 1) * BLOCK, columns(head)]
        return score_blocks(part_query, k_ref, columns(head), spans(part))

    def finish(part, head, scores):
        values = [values_t[columns(head), low:high] for low, high in spans(part)]
        biases = [bias_ref[1 if block == part else 0] for block in range(part + 1)]
        out = softmax_out(scores, biases, values)[0]
        o_ref[part * BLOCK : (part + 1) * BLOCK, columns(head)] = out.T.astype(jnp.bfloat16)

    pipelined([(part, head) for part in range(parts) for head in range(2)], 2, start, finish)


def column_attention(x, w_column, group):
    rows, depth = x.shape
    pairs = HEADS // 2
    weights = lambda third: pl.BlockSpec((depth, 2 * HEAD), lambda j: (0, third * pairs + j))
    return pl.pallas_call(
        functools.partial(column_kernel, group),
        grid=(pairs,),
        in_specs=[pl.BlockSpec((rows, depth), lambda j: (0, 0)), weights(0), weights(1), weights(2)],
        out_specs=pl.BlockSpec((rows, 2 * HEAD), lambda j: (0, j)),
        out_shape=jax.ShapeDtypeStruct((rows, HEADS * HEAD), jnp.bfloat16),
        scratch_shapes=[
            pltpu.VMEM((rows, 2 * HEAD), jnp.bfloat16),
            pltpu.VMEM((2, BLOCK, BLOCK), jnp.float32),
        ],
        compiler_params=params(),
        cost_estimate=cost(10),
        name="column_attention",
    )(x, w_column, w_column, w_column)


def merge_heads(has_earlier, local_ref, earlier_refs, o_ref):
    local_heads, part_heads = 4, 2
    for head in range(local_heads):
        def stats(ref, heads, index):
            start = heads * HEAD
            rows = ref[start : start + 8 * heads, :].astype(jnp.float32)
            rows = rows[8 * index : 8 * index + 8]
            return rows[0:1] + rows[1:2] + rows[2:3], rows[3:4] + rows[4:5] + rows[5:6]

        earlier_ref, index = earlier_refs[head // part_heads], head % part_heads
        top_l, sum_l = stats(local_ref, local_heads, head)
        top_e, sum_e = stats(earlier_ref, part_heads, index)
        top_e = jnp.where(has_earlier, top_e, NEG)
        top = jnp.maximum(top_l, top_e)
        weight_l = jnp.exp2((top_l - top) * SCALE2) * sum_l
        weight_e = jnp.exp2((top_e - top) * SCALE2) * sum_e
        weight_e = jnp.where(has_earlier, weight_e, 0.0)
        inverse = 1.0 / (weight_l + weight_e)
        out_l = local_ref[head * HEAD : (head + 1) * HEAD, :].astype(jnp.float32)
        out_e = earlier_ref[index * HEAD : (index + 1) * HEAD, :].astype(jnp.float32)
        out = out_l * (weight_l * inverse) + out_e * (weight_e * inverse)
        o_ref[:, head * HEAD : (head + 1) * HEAD] = out.T.astype(jnp.bfloat16)


def finish_kernel(
    flags_ref, local_same, local_cross, same_a, same_b, cross_a, cross_b, col_ref, o_ref
):
    step = pl.program_id(0)
    has_earlier = flags_ref[1] > 0

    @pl.when(step < 2)
    def _():
        o_ref[...] = col_ref[...]

    @pl.when(step == 2)
    def _():
        merge_heads(has_earlier, local_same, (same_a, same_b), o_ref)

    @pl.when(step == 3)
    def _():
        merge_heads(has_earlier, local_cross, (cross_a, cross_b), o_ref)


def finish(flags, local_same, local_cross, same_a, same_b, cross_a, cross_b, col_out):
    bands = [local_same, local_cross, same_a, same_b, cross_a, cross_b]

    def out_block(j, c):
        core = c[0]
        return (0, jnp.where(j < 2, 2 + j, jnp.where(j == 2, core, 1 - core)))

    return pl.pallas_call(
        finish_kernel,
        grid_spec=pltpu.PrefetchScalarGridSpec(
            num_scalar_prefetch=1,
            grid=(4,),
            in_specs=[pl.BlockSpec(b.shape, lambda j, c: (0, 0)) for b in bands]
            + [pl.BlockSpec((HALF, HALF), lambda j, c: (0, jnp.minimum(j, 1)))],
            out_specs=pl.BlockSpec((HALF, HALF), out_block),
        ),
        out_shape=jax.ShapeDtypeStruct((HALF, 2 * HEADS * HEAD), jnp.bfloat16),
        compiler_params=params(),
        cost_estimate=cost(3),
        name="merge",
    )(flags, *bands, col_out)


def after(value, *others):
    return lax.optimization_barrier((value,) + others)[0]


def on_device(tokens, w_row, w_column):
    count = lax.axis_size("seq")
    chips = count // 2
    rank = lax.axis_index("seq")
    core = (rank % 2).astype(jnp.int32)
    core_arr = core.reshape(1)
    flags = jnp.stack([core, (rank >= 2).astype(jnp.int32)])
    group = HALF // chips
    same_core = [list(range(0, count, 2)), list(range(1, count, 2))]

    def exchange(value):
        width = value.shape[1]
        value = lax.all_to_all(
            value.reshape(chips, group, width), "seq", split_axis=0, concat_axis=0,
            axis_index_groups=same_core, tiled=True,
        )
        return value.reshape(HALF, width)

    def swapped(value):
        return lax.ppermute(value, "seq", [(d, d ^ 1) for d in range(count)])

    def to_previous(value):
        return lax.ppermute(value, "seq", [(d, d - 2) for d in range(2, count)])

    def to_next(same, cross):
        same = lax.ppermute(same, "seq", [(d, d + 2) for d in range(count - 2)])
        cross = lax.ppermute(cross, "seq", [(d, (d + 2) ^ 1) for d in range(count - 2)])
        return same, cross

    w_row = pltpu.with_memory_space_constraint(w_row, pltpu.HBM)
    w_column = pltpu.with_memory_space_constraint(w_column, pltpu.HBM)
    columns = exchange(tokens)
    sibling = swapped(tokens)
    query_a, query_b = project_query(core_arr, tokens, sibling, w_row)
    next_a, next_b = to_previous(query_a), to_previous(query_b)
    keys, values_t = project_keyval(core_arr, tokens, sibling, w_row)
    local_same, local_cross = band_part(
        False, core_arr, jnp.concatenate([query_a, query_b], axis=1), keys, values_t
    )
    parts_a = band_part(True, core_arr, after(next_a, local_same), keys, values_t, 0)
    same_a, cross_a = to_next(*parts_a)
    col_out = column_attention(after(columns, parts_a[0]), w_column, group)
    parts_b = band_part(True, core_arr, after(next_b, col_out), keys, values_t, 1)
    same_b, cross_b = to_next(*parts_b)
    return finish(
        flags, local_same, swapped(local_cross), same_a, same_b, cross_a, cross_b,
        exchange(after(col_out, same_a, cross_a)),
    )


def solution(mesh):
    in_specs = (P("seq", None), P(), P())
    out_specs = P("seq", None)
    return jax.shard_map(
        on_device, mesh=mesh, in_specs=in_specs, out_specs=out_specs, check_vma=False
    )
```

```python
import functools
import math

import jax
import jax.numpy as jnp
from jax import lax
from jax.experimental import pallas as pl
from jax.experimental.pallas import tpu as pltpu
from jax.sharding import PartitionSpec as P

HEAD = 128
HEADS = 8
STRIDE = 1024
HALF = 512
BLOCK = 256
SCALE2 = math.log2(math.e) / math.sqrt(HEAD)
NEG = -1e30
VMEM_LIMIT = 28 << 20


def params():
    return pltpu.CompilerParams(vmem_limit_bytes=VMEM_LIMIT)


def cost(us):
    return pl.CostEstimate(flops=int(us * 10**9), bytes_accessed=1 << 14, transcendentals=0)


def project_kernel(parts, core_ref, x_ref, w_ref, *refs):
    outs = refs[-len(parts) :]
    value = jnp.dot(x_ref[...], w_ref[...], preferred_element_type=jnp.float32)
    for index, (part, out_ref) in enumerate(zip(parts, outs)):

        @pl.when(pl.program_id(0) // 2 == index)
        def _():
            out_ref[...] = (value.T if part == 2 else value).astype(jnp.bfloat16)


def project(parts, own, core, x, w_row, before=()):
    depth = x.shape[1]
    half = (lambda c: c[0]) if own else (lambda c: 1 - c[0])

    def weight_block(j, c):
        return (0, 4 * (parts[0] + j // 2) + 2 * c[0] + j % 2)

    def spec(index, part):
        block = lambda j: jnp.clip(j - 2 * index, 0, 1)
        if part == 2:
            return pl.BlockSpec((BLOCK, HALF), lambda j, c: (block(j), half(c)))
        return pl.BlockSpec((HALF, BLOCK), lambda j, c: (half(c), block(j)))

    shapes = [(HALF, STRIDE) if part == 2 else (STRIDE, HALF) for part in parts]
    return pl.pallas_call(
        functools.partial(project_kernel, parts),
        grid_spec=pltpu.PrefetchScalarGridSpec(
            num_scalar_prefetch=1,
            grid=(2 * len(parts),),
            in_specs=[
                pl.BlockSpec((HALF, depth), lambda j, c: (0, 0)),
                pl.BlockSpec((depth, BLOCK), weight_block),
            ]
            + [pl.BlockSpec(memory_space=pl.ANY)] * len(before),
            out_specs=[spec(index, part) for index, part in enumerate(parts)],
        ),
        out_shape=[jax.ShapeDtypeStruct(shape, jnp.bfloat16) for shape in shapes],
        input_output_aliases={3 + index: index for index in range(len(before))},
        compiler_params=params(),
        cost_estimate=cost(0.2 * len(parts)),
        name="project",
    )(core, x, w_row, *before)


def score_blocks(query, key_ref, columns, spans):
    return [
        lax.dot_general(
            key_ref[low:high, columns], query, (((1,), (1,)), ((), ())),
            preferred_element_type=jnp.float32,
        )
        for low, high in spans
    ]


def softmax_out(scores, biases, value_t_blocks):
    scores = [s if b is None else s + b for s, b in zip(scores, biases)]
    top = functools.reduce(jnp.maximum, [jnp.max(s, axis=0, keepdims=True) for s in scores])
    expd = [jnp.exp2((s - top) * SCALE2) for s in scores]
    total = sum(jnp.sum(e, axis=0, keepdims=True) for e in expd)
    out = sum(
        jnp.dot(v, e.astype(jnp.bfloat16), preferred_element_type=jnp.float32)
        for v, e in zip(value_t_blocks, expd)
    )
    return out * (1.0 / total), top, total


def pipelined(jobs, ahead, start, finish):
    pending, results = [], {}
    for job in jobs:
        pending.append((job, start(*job)))
        if len(pending) > ahead:
            first, value = pending.pop(0)
            results[first] = finish(*first, value)
    for first, value in pending:
        results[first] = finish(*first, value)
    return results


def split3(value):
    high = value.astype(jnp.bfloat16).astype(jnp.float32)
    rest = value - high
    mid = rest.astype(jnp.bfloat16).astype(jnp.float32)
    return [high, mid, rest - mid]


def band_kernel(
    earlier, heads, ahead, core_ref, q_ref, k_ref, vt_ref, same_ref, cross_ref, stat_ref, bias_ref
):
    step = pl.program_id(0)
    core = core_ref[0]
    parts = STRIDE // BLOCK

    @pl.when(step == 0)
    def _():
        kpos = lax.broadcasted_iota(jnp.int32, (BLOCK, BLOCK), 0)
        qpos = lax.broadcasted_iota(jnp.int32, (BLOCK, BLOCK), 1)
        allowed = kpos > qpos if earlier else kpos <= qpos
        bias_ref[...] = jnp.where(allowed, 0.0, NEG)

    def spans(part):
        low, high = part * BLOCK, (part + 1) * BLOCK
        rest = (high, STRIDE) if earlier else (0, low)
        return [(low, high)] + ([rest] if rest[0] < rest[1] else [])

    def columns(head):
        return slice(head * HEAD, (head + 1) * HEAD)

    def start(part, head):
        query = q_ref[part * BLOCK : (part + 1) * BLOCK, columns(head)]
        return score_blocks(query, k_ref, columns(head), spans(part))

    def finish(part, head, scores):
        values = [vt_ref[columns(head), low:high] for low, high in spans(part)]
        out, top, total = softmax_out(scores, [bias_ref[...], None], values)
        return out.astype(jnp.bfloat16), top, total

    jobs = [(part, head) for part in range(parts) for head in range(2)]
    results = pipelined(jobs, ahead, start, finish)
    for head in range(2):
        stats = [
            jnp.concatenate(
                split3(results[part, head][1])
                + split3(results[part, head][2])
                + [jnp.zeros((2, BLOCK), jnp.float32)],
                axis=0,
            )
            for part in range(parts)
        ]
        stat_ref[step * 2 + head] = jnp.concatenate(stats, axis=1)
    rows = pl.ds(pl.multiple_of(step * 2 * HEAD, 2 * HEAD), 2 * HEAD)
    for half in range(2):
        piece = jnp.concatenate(
            [
                jnp.concatenate([results[2 * half + part, head][0] for part in range(2)], axis=1)
                for head in range(2)
            ],
            axis=0,
        )

        @pl.when(core == half)
        def _():
            same_ref[rows, :] = piece

        @pl.when(core != half)
        def _():
            cross_ref[rows, :] = piece

    @pl.when(step == heads // 2 - 1)
    def _():
        stats = jnp.concatenate([stat_ref[h] for h in range(heads)], axis=0).astype(jnp.bfloat16)
        for half in range(2):
            piece = stats[:, half * HALF : (half + 1) * HALF]

            @pl.when(core == half)
            def _():
                same_ref[heads * HEAD :, :] = piece

            @pl.when(core != half)
            def _():
                cross_ref[heads * HEAD :, :] = piece


def band_part(earlier, core, query, keys, values_t, first=0):
    heads = query.shape[1] // HEAD
    payload = heads * (HEAD + 8)
    whole = pl.BlockSpec((payload, HALF), lambda h, c: (0, 0))
    return pl.pallas_call(
        functools.partial(band_kernel, earlier, heads, 2 if earlier else 4),
        grid_spec=pltpu.PrefetchScalarGridSpec(
            num_scalar_prefetch=1,
            grid=(heads // 2,),
            in_specs=[
                pl.BlockSpec((STRIDE, 2 * HEAD), lambda h, c: (0, h)),
                pl.BlockSpec((STRIDE, 2 * HEAD), lambda h, c: (0, first + h)),
                pl.BlockSpec((2 * HEAD, STRIDE), lambda h, c: (first + h, 0)),
            ],
            out_specs=[whole, whole],
            scratch_shapes=[
                pltpu.VMEM((heads, 8, STRIDE), jnp.float32),
                pltpu.VMEM((BLOCK, BLOCK), jnp.float32),
            ],
        ),
        out_shape=[jax.ShapeDtypeStruct((payload, HALF), jnp.bfloat16)] * 2,
        compiler_params=params(),
        cost_estimate=cost(20 if earlier else 0.2),
        name="band_earlier" if earlier else "band_local",
    )(core, query, keys, values_t)


def column_kernel(group, q_ref, k_ref, v_ref, o_ref, bias_ref):
    parts = HALF // BLOCK
    heads = q_ref.shape[1] // HEAD

    @pl.when(pl.program_id(0) == 0)
    def _():
        kpos = lax.broadcasted_iota(jnp.int32, (BLOCK, BLOCK), 0)
        qpos = lax.broadcasted_iota(jnp.int32, (BLOCK, BLOCK), 1)
        column = ((qpos - kpos) & (group - 1)) == 0
        bias_ref[0] = jnp.where(column, 0.0, NEG)
        bias_ref[1] = jnp.where(column & (kpos <= qpos), 0.0, NEG)

    values_t = v_ref[...].astype(jnp.float32).T.astype(jnp.bfloat16)

    def spans(part):
        return [(block * BLOCK, (block + 1) * BLOCK) for block in range(part + 1)]

    def columns(head):
        return slice(head * HEAD, (head + 1) * HEAD)

    def start(part, head):
        query = q_ref[part * BLOCK : (part + 1) * BLOCK, columns(head)]
        return score_blocks(query, k_ref, columns(head), spans(part))

    def finish(part, head, scores):
        values = [values_t[columns(head), low:high] for low, high in spans(part)]
        biases = [bias_ref[1 if block == part else 0] for block in range(part + 1)]
        out = softmax_out(scores, biases, values)[0]
        o_ref[part * BLOCK : (part + 1) * BLOCK, columns(head)] = out.T.astype(jnp.bfloat16)

    pipelined([(part, head) for part in range(parts) for head in range(heads)], 2, start, finish)


def column_attention(projected, group):
    rows = projected.shape[0]
    heads = 4
    steps = HEADS // heads
    spec = lambda third: pl.BlockSpec((rows, heads * HEAD), lambda j: (0, third * steps + j))
    return pl.pallas_call(
        functools.partial(column_kernel, group),
        grid=(steps,),
        in_specs=[spec(0), spec(1), spec(2)],
        out_specs=pl.BlockSpec((rows, heads * HEAD), lambda j: (0, j)),
        out_shape=jax.ShapeDtypeStruct((rows, HEADS * HEAD), jnp.bfloat16),
        scratch_shapes=[pltpu.VMEM((2, BLOCK, BLOCK), jnp.float32)],
        compiler_params=params(),
        cost_estimate=cost(6),
        name="column_attention",
    )(projected, projected, projected)


def merge_kernel(flags_ref, local_same, local_cross, earlier_same, earlier_cross, o_ref):
    has_earlier = flags_ref[1] > 0

    def stats(ref, head):
        rows = ref[HALF:, :].astype(jnp.float32)[8 * head : 8 * head + 8]
        return rows[0:1] + rows[1:2] + rows[2:3], rows[3:4] + rows[4:5] + rows[5:6]

    def merge(local_ref, earlier_ref):
        for head in range(4):
            top_l, sum_l = stats(local_ref, head)
            top_e, sum_e = stats(earlier_ref, head)
            top_e = jnp.where(has_earlier, top_e, NEG)
            top = jnp.maximum(top_l, top_e)
            weight_l = jnp.exp2((top_l - top) * SCALE2) * sum_l
            weight_e = jnp.exp2((top_e - top) * SCALE2) * sum_e
            weight_e = jnp.where(has_earlier, weight_e, 0.0)
            inverse = 1.0 / (weight_l + weight_e)
            columns = slice(head * HEAD, (head + 1) * HEAD)
            out_l = local_ref[columns, :].astype(jnp.float32)
            out_e = earlier_ref[columns, :].astype(jnp.float32)
            out = out_l * (weight_l * inverse) + out_e * (weight_e * inverse)
            o_ref[:, columns] = out.T.astype(jnp.bfloat16)

    @pl.when(pl.program_id(0) == 0)
    def _():
        merge(local_same, earlier_same)

    @pl.when(pl.program_id(0) == 1)
    def _():
        merge(local_cross, earlier_cross)


def merge_band(flags, *payloads):
    def out_block(j, c):
        return (0, jnp.where(j == 0, c[0], 1 - c[0]))

    return pl.pallas_call(
        merge_kernel,
        grid_spec=pltpu.PrefetchScalarGridSpec(
            num_scalar_prefetch=1,
            grid=(2,),
            in_specs=[pl.BlockSpec(p.shape, lambda j, c: (0, 0)) for p in payloads],
            out_specs=pl.BlockSpec((HALF, HALF), out_block),
        ),
        out_shape=jax.ShapeDtypeStruct((HALF, 2 * HEADS * HEAD), jnp.bfloat16),
        compiler_params=params(),
        cost_estimate=cost(60),
        name="merge_band",
    )(flags, *payloads)


def place_kernel(columns_ref, _, o_ref):
    o_ref[...] = columns_ref[...]


def place_columns(band_out, col_out):
    width = col_out.shape[1]
    return pl.pallas_call(
        place_kernel,
        grid=(4,),
        in_specs=[
            pl.BlockSpec((HALF // 4, width), lambda j: (j, 0)),
            pl.BlockSpec(memory_space=pl.ANY),
        ],
        out_specs=pl.BlockSpec((HALF // 4, width), lambda j: (j, 1)),
        out_shape=jax.ShapeDtypeStruct(band_out.shape, jnp.bfloat16),
        input_output_aliases={1: 0},
        compiler_params=params(),
        cost_estimate=cost(1),
        name="place_columns",
    )(col_out, band_out)


def in_hbm(value):
    return pltpu.with_memory_space_constraint(value, pltpu.HBM)


def after(value, *others):
    return lax.optimization_barrier((value,) + others)[0]


def on_device(tokens, w_row, w_column):
    count = lax.axis_size("seq")
    chips = count // 2
    rank = lax.axis_index("seq")
    core = (rank % 2).astype(jnp.int32)
    core_arr = core.reshape(1)
    flags = jnp.stack([core, (rank >= 2).astype(jnp.int32)])
    group = HALF // chips
    same_core = [list(range(0, count, 2)), list(range(1, count, 2))]

    def exchange(value):
        width = value.shape[1]
        value = lax.all_to_all(
            value.reshape(chips, group, width), "seq", split_axis=0, concat_axis=0,
            axis_index_groups=same_core, tiled=True,
        )
        return value.reshape(HALF, width)

    def swapped(value):
        return lax.ppermute(value, "seq", [(d, d ^ 1) for d in range(count)])

    def to_previous(value):
        return lax.ppermute(value, "seq", [(d, d - 2) for d in range(2, count)])

    def to_next(same, cross):
        same = lax.ppermute(same, "seq", [(d, d + 2) for d in range(count - 2)])
        cross = lax.ppermute(cross, "seq", [(d, (d + 2) ^ 1) for d in range(count - 2)])
        return same, cross

    w_row = in_hbm(w_row)
    sibling = swapped(tokens)
    query, keys, values_t = project((0, 1, 2), True, core_arr, tokens, w_row)
    query, keys, values_t = in_hbm(query), in_hbm(keys), in_hbm(values_t)
    (query,) = project((0,), False, core_arr, sibling, w_row, (query,))
    next_query = to_previous(query)
    columns = exchange(after(tokens, query))
    keys, values_t = project((1, 2), False, core_arr, sibling, w_row, (keys, values_t))
    query, keys, values_t = in_hbm(query), in_hbm(keys), in_hbm(values_t)
    local_same, local_cross = band_part(False, core_arr, query, keys, values_t)
    earlier = band_part(True, core_arr, after(next_query, local_same), keys, values_t)
    same, cross = to_next(*earlier)
    columns = after(columns, earlier[0])
    col_proj = jnp.dot(columns, w_column, preferred_element_type=jnp.float32).astype(jnp.bfloat16)
    col_out = exchange(column_attention(col_proj, group))
    band_out = merge_band(flags, local_same, swapped(local_cross), same, cross)
    return place_columns(band_out, col_out)


def solution(mesh):
    in_specs = (P("seq", None), P(), P())
    out_specs = P("seq", None)
    return jax.shard_map(
        on_device, mesh=mesh, in_specs=in_specs, out_specs=out_specs, check_vma=False
    )
```

```python
import functools
import math

import jax
import jax.numpy as jnp
from jax import lax
from jax.experimental import pallas as pl
from jax.experimental.pallas import tpu as pltpu
from jax.sharding import PartitionSpec as P

HEAD = 128
HEADS = 8
STRIDE = 1024
HALF = 512
BLOCK = 256
SCALE2 = math.log2(math.e) / math.sqrt(HEAD)
NEG = -1e30
VMEM_LIMIT = 28 << 20
PROJECT_COST, LOCAL_COST, A_COST, B_COST, MERGE_COST = 0.5, 0.5, 20, 0.5, 2


def params():
    return pltpu.CompilerParams(vmem_limit_bytes=VMEM_LIMIT)


def cost(us):
    return pl.CostEstimate(flops=int(us * 10**9), bytes_accessed=1 << 14, transcendentals=0)


def project_kernel(core_ref, own_ref, sibling_ref, w_ref, kv_a, kv_b, q_a, q_b):
    core = core_ref[0]
    for step, (kind, ref) in enumerate(PROJECT_ORDER):
        ref = {"kv_a": kv_a, "kv_b": kv_b, "q_a": q_a, "q_b": q_b}[ref]

        @pl.when(pl.program_id(0) == step)
        def _():
            for place, x_ref in ((core, own_ref), (1 - core, sibling_ref)):
                value = jnp.dot(x_ref[...], w_ref[...], preferred_element_type=jnp.float32)
                row = pl.multiple_of(place * HALF, HALF)
                if kind == 2:
                    value = value.T.astype(jnp.bfloat16)
                    for block in range(HALF // BLOCK):
                        rows = pl.ds(STRIDE + row + block * BLOCK, BLOCK)
                        ref[rows, :] = value[:, block * BLOCK : (block + 1) * BLOCK]
                else:
                    ref[pl.ds(row, HALF), :] = value.astype(jnp.bfloat16)


PROJECT_ORDER = [(1, "kv_a"), (2, "kv_a"), (0, "q_b"), (1, "kv_b"), (2, "kv_b"), (0, "q_a")]


def project(core, tokens, sibling, w_row):
    depth = tokens.shape[1]

    def weight_block(j, c):
        kind = lax.rem(j + 1, 3)
        pair = jnp.where((j >= 2) & (j <= 4), 1, 0)
        return (0, 4 * kind + 2 * c[0] + pair)

    whole = lambda rows, width: pl.BlockSpec((rows, width), lambda j, c: (0, 0))
    outs = [(2 * STRIDE, BLOCK), (2 * STRIDE, BLOCK), (STRIDE, BLOCK), (STRIDE, BLOCK)]
    return pl.pallas_call(
        project_kernel,
        grid_spec=pltpu.PrefetchScalarGridSpec(
            num_scalar_prefetch=1,
            grid=(len(PROJECT_ORDER),),
            in_specs=[
                whole(HALF, depth),
                whole(HALF, depth),
                pl.BlockSpec((depth, BLOCK), weight_block),
            ],
            out_specs=[whole(*shape) for shape in outs],
        ),
        out_shape=[jax.ShapeDtypeStruct(shape, jnp.bfloat16) for shape in outs],
        compiler_params=params(),
        cost_estimate=cost(PROJECT_COST),
        name="project",
    )(core, tokens, sibling, w_row)


def score_blocks(query, key_ref, columns, spans):
    return [
        lax.dot_general(
            key_ref[low:high, columns], query, (((1,), (1,)), ((), ())),
            preferred_element_type=jnp.float32,
        )
        for low, high in spans
    ]


def softmax_out(scores, biases, value_t_blocks):
    scores = [s if b is None else s + b for s, b in zip(scores, biases)]
    top = functools.reduce(jnp.maximum, [jnp.max(s, axis=0, keepdims=True) for s in scores])
    expd = [jnp.exp2((s - top) * SCALE2) for s in scores]
    total = sum(jnp.sum(e, axis=0, keepdims=True) for e in expd)
    out = sum(
        jnp.dot(v, e.astype(jnp.bfloat16), preferred_element_type=jnp.float32)
        for v, e in zip(value_t_blocks, expd)
    )
    return out * (1.0 / total), top, total


def pipelined(jobs, ahead, start, finish):
    pending, results = [], {}
    for job in jobs:
        pending.append((job, start(*job)))
        if len(pending) > ahead:
            first, value = pending.pop(0)
            results[first] = finish(*first, value)
    for first, value in pending:
        results[first] = finish(*first, value)
    return results


def split3(value):
    high = value.astype(jnp.bfloat16).astype(jnp.float32)
    rest = value - high
    mid = rest.astype(jnp.bfloat16).astype(jnp.float32)
    return [high, mid, rest - mid]


def band_kernel(earlier, pairs, core_ref, *refs):
    inputs, (same_ref, cross_ref, stat_ref, bias_ref) = refs[: 2 * pairs], refs[2 * pairs :]
    step = pl.program_id(0)
    core = core_ref[0]
    parts = STRIDE // BLOCK
    heads = 2 * pairs

    @pl.when(step == 0)
    def _():
        kpos = lax.broadcasted_iota(jnp.int32, (BLOCK, BLOCK), 0)
        qpos = lax.broadcasted_iota(jnp.int32, (BLOCK, BLOCK), 1)
        allowed = kpos > qpos if earlier else kpos <= qpos
        bias_ref[...] = jnp.where(allowed, 0.0, NEG)

    def spans(part):
        low, high = part * BLOCK, (part + 1) * BLOCK
        rest = (high, STRIDE) if earlier else (0, low)
        return [(low, high)] + ([rest] if rest[0] < rest[1] else [])

    def columns(head):
        return slice(head * HEAD, (head + 1) * HEAD)

    def attend(pair):
        q_ref, kv_ref = inputs[2 * pair : 2 * pair + 2]

        def values_t(head, low, high):
            blocks = [
                kv_ref[STRIDE + at + head * HEAD : STRIDE + at + (head + 1) * HEAD, :]
                for at in range(low, high, BLOCK)
            ]
            return jnp.concatenate(blocks, axis=1)

        def start(part, head):
            query = q_ref[part * BLOCK : (part + 1) * BLOCK, columns(head)]
            return score_blocks(query, kv_ref, columns(head), spans(part))

        def finish(part, head, scores):
            values = [values_t(head, low, high) for low, high in spans(part)]
            out, top, total = softmax_out(scores, [bias_ref[...], None], values)
            return out.astype(jnp.bfloat16), top, total

        jobs = [(part, head) for part in range(parts) for head in range(2)]
        results = pipelined(jobs, 2 if earlier else 4, start, finish)
        for head in range(2):
            stats = [
                jnp.concatenate(
                    split3(results[part, head][1])
                    + split3(results[part, head][2])
                    + [jnp.zeros((2, BLOCK), jnp.float32)],
                    axis=0,
                )
                for part in range(parts)
            ]
            stat_ref[2 * pair + head] = jnp.concatenate(stats, axis=1)
        rows = slice(pair * 2 * HEAD, (pair + 1) * 2 * HEAD)
        for half in range(2):
            piece = jnp.concatenate(
                [
                    jnp.concatenate([results[2 * half + i, head][0] for i in range(2)], axis=1)
                    for head in range(2)
                ],
                axis=0,
            )

            @pl.when(core == half)
            def _():
                same_ref[rows, :] = piece

            @pl.when(core != half)
            def _():
                cross_ref[rows, :] = piece

    for pair in range(pairs):

        @pl.when(step == pair)
        def _():
            attend(pair)

    @pl.when(step == pairs - 1)
    def _():
        stats = jnp.concatenate([stat_ref[h] for h in range(heads)], axis=0).astype(jnp.bfloat16)
        for half in range(2):
            piece = stats[:, half * HALF : (half + 1) * HALF]

            @pl.when(core == half)
            def _():
                same_ref[heads * HEAD :, :] = piece

            @pl.when(core != half)
            def _():
                cross_ref[heads * HEAD :, :] = piece


def band_part(earlier, core, *inputs, estimate):
    pairs = len(inputs) // 2
    payload = 2 * pairs * (HEAD + 8)
    whole = lambda shape: pl.BlockSpec(shape, lambda j, c: (0, 0))
    return pl.pallas_call(
        functools.partial(band_kernel, earlier, pairs),
        grid_spec=pltpu.PrefetchScalarGridSpec(
            num_scalar_prefetch=1,
            grid=(pairs,),
            in_specs=[whole(value.shape) for value in inputs],
            out_specs=[whole((payload, HALF))] * 2,
            scratch_shapes=[
                pltpu.VMEM((2 * pairs, 8, STRIDE), jnp.float32),
                pltpu.VMEM((BLOCK, BLOCK), jnp.float32),
            ],
        ),
        out_shape=[jax.ShapeDtypeStruct((payload, HALF), jnp.bfloat16)] * 2,
        compiler_params=params(),
        cost_estimate=cost(estimate),
        name="band_earlier" if earlier else "band_local",
    )(core, *inputs)


def column_kernel(group, q_ref, k_ref, v_ref, o_ref, bias_ref):
    parts = HALF // BLOCK
    heads = q_ref.shape[1] // HEAD

    @pl.when(pl.program_id(0) == 0)
    def _():
        kpos = lax.broadcasted_iota(jnp.int32, (BLOCK, BLOCK), 0)
        qpos = lax.broadcasted_iota(jnp.int32, (BLOCK, BLOCK), 1)
        column = ((qpos - kpos) & (group - 1)) == 0
        bias_ref[0] = jnp.where(column, 0.0, NEG)
        bias_ref[1] = jnp.where(column & (kpos <= qpos), 0.0, NEG)

    values_t = v_ref[...].astype(jnp.float32).T.astype(jnp.bfloat16)

    def spans(part):
        return [(block * BLOCK, (block + 1) * BLOCK) for block in range(part + 1)]

    def columns(head):
        return slice(head * HEAD, (head + 1) * HEAD)

    def start(part, head):
        query = q_ref[part * BLOCK : (part + 1) * BLOCK, columns(head)]
        return score_blocks(query, k_ref, columns(head), spans(part))

    def finish(part, head, scores):
        values = [values_t[columns(head), low:high] for low, high in spans(part)]
        biases = [bias_ref[1 if block == part else 0] for block in range(part + 1)]
        out = softmax_out(scores, biases, values)[0]
        o_ref[part * BLOCK : (part + 1) * BLOCK, columns(head)] = out.T.astype(jnp.bfloat16)

    pipelined([(part, head) for part in range(parts) for head in range(heads)], 2, start, finish)


def column_attention(projected, group):
    rows = projected.shape[0]
    heads = 4
    steps = HEADS // heads
    spec = lambda third: pl.BlockSpec((rows, heads * HEAD), lambda j: (0, third * steps + j))
    return pl.pallas_call(
        functools.partial(column_kernel, group),
        grid=(steps,),
        in_specs=[spec(0), spec(1), spec(2)],
        out_specs=pl.BlockSpec((rows, heads * HEAD), lambda j: (0, j)),
        out_shape=jax.ShapeDtypeStruct((rows, HEADS * HEAD), jnp.bfloat16),
        scratch_shapes=[pltpu.VMEM((2, BLOCK, BLOCK), jnp.float32)],
        compiler_params=params(),
        cost_estimate=cost(6),
        name="column_attention",
    )(projected, projected, projected)


def merge_kernel(
    flags_ref, local_same, local_cross, same_a, same_b, cross_a, cross_b, o_ref
):
    has_earlier = flags_ref[1] > 0

    def stats(ref, heads, head):
        rows = ref[heads * HEAD :, :].astype(jnp.float32)[8 * head : 8 * head + 8]
        return rows[0:1] + rows[1:2] + rows[2:3], rows[3:4] + rows[4:5] + rows[5:6]

    def merge(local_ref, earlier_refs):
        for head in range(4):
            earlier_ref, index = earlier_refs[head // 2], head % 2
            top_l, sum_l = stats(local_ref, 4, head)
            top_e, sum_e = stats(earlier_ref, 2, index)
            top_e = jnp.where(has_earlier, top_e, NEG)
            top = jnp.maximum(top_l, top_e)
            weight_l = jnp.exp2((top_l - top) * SCALE2) * sum_l
            weight_e = jnp.exp2((top_e - top) * SCALE2) * sum_e
            weight_e = jnp.where(has_earlier, weight_e, 0.0)
            inverse = 1.0 / (weight_l + weight_e)
            columns = slice(head * HEAD, (head + 1) * HEAD)
            out_l = local_ref[columns, :].astype(jnp.float32)
            out_e = earlier_ref[index * HEAD : (index + 1) * HEAD, :].astype(jnp.float32)
            out = out_l * (weight_l * inverse) + out_e * (weight_e * inverse)
            o_ref[:, columns] = out.T.astype(jnp.bfloat16)

    @pl.when(pl.program_id(0) == 0)
    def _():
        merge(local_same, (same_a, same_b))

    @pl.when(pl.program_id(0) == 1)
    def _():
        merge(local_cross, (cross_a, cross_b))


def merge_band(flags, *payloads):
    def out_block(j, c):
        return (0, jnp.where(j == 0, c[0], 1 - c[0]))

    return pl.pallas_call(
        merge_kernel,
        grid_spec=pltpu.PrefetchScalarGridSpec(
            num_scalar_prefetch=1,
            grid=(2,),
            in_specs=[pl.BlockSpec(p.shape, lambda j, c: (0, 0)) for p in payloads],
            out_specs=pl.BlockSpec((HALF, HALF), out_block),
        ),
        out_shape=jax.ShapeDtypeStruct((HALF, 2 * HEADS * HEAD), jnp.bfloat16),
        compiler_params=params(),
        cost_estimate=cost(MERGE_COST),
        name="merge_band",
    )(flags, *payloads)


def place_kernel(columns_ref, _, o_ref):
    o_ref[...] = columns_ref[...]


def place_columns(band_out, col_out):
    width = col_out.shape[1]
    return pl.pallas_call(
        place_kernel,
        grid=(4,),
        in_specs=[
            pl.BlockSpec((HALF // 4, width), lambda j: (j, 0)),
            pl.BlockSpec(memory_space=pl.ANY),
        ],
        out_specs=pl.BlockSpec((HALF // 4, width), lambda j: (j, 1)),
        out_shape=jax.ShapeDtypeStruct(band_out.shape, jnp.bfloat16),
        input_output_aliases={1: 0},
        compiler_params=params(),
        cost_estimate=cost(1),
        name="place_columns",
    )(col_out, band_out)


def in_hbm(value):
    return pltpu.with_memory_space_constraint(value, pltpu.HBM)


def after(value, *others):
    return lax.optimization_barrier((value,) + others)[0]


def on_device(tokens, w_row, w_column):
    count = lax.axis_size("seq")
    chips = count // 2
    rank = lax.axis_index("seq")
    core = (rank % 2).astype(jnp.int32)
    core_arr = core.reshape(1)
    flags = jnp.stack([core, (rank >= 2).astype(jnp.int32)])
    group = HALF // chips
    same_core = [list(range(0, count, 2)), list(range(1, count, 2))]

    def exchange(value):
        width = value.shape[1]
        value = lax.all_to_all(
            value.reshape(chips, group, width), "seq", split_axis=0, concat_axis=0,
            axis_index_groups=same_core, tiled=True,
        )
        return value.reshape(HALF, width)

    def swapped(value):
        return lax.ppermute(value, "seq", [(d, d ^ 1) for d in range(count)])

    def to_next(value):
        return lax.ppermute(value, "seq", [(d, d + 2) for d in range(count - 2)])

    w_row = in_hbm(w_row)
    columns = exchange(tokens)
    sibling = swapped(tokens)
    kv_a, kv_b, q_a, q_b = project(core_arr, tokens, sibling, w_row)
    previous_kv_a = to_next(kv_a)
    next_q_b = lax.ppermute(q_b, "seq", [(d, d - 2) for d in range(2, count)])
    local_same, local_cross = band_part(
        False, core_arr, q_a, kv_a, q_b, kv_b, estimate=LOCAL_COST
    )
    sent_same, sent_cross = band_part(
        True, core_arr, after(next_q_b, local_same), kv_b, estimate=B_COST
    )
    same_b = to_next(sent_same)
    cross_b = lax.ppermute(sent_cross, "seq", [(d, (d + 2) ^ 1) for d in range(count - 2)])
    columns = after(columns, sent_same)
    col_proj = jnp.dot(columns, w_column, preferred_element_type=jnp.float32).astype(jnp.bfloat16)
    col_out = column_attention(col_proj, group)
    same_a, cross_a = band_part(
        True, core_arr, q_a, after(previous_kv_a, col_out, same_b, cross_b), estimate=A_COST
    )
    col_out = exchange(col_out)
    band_out = merge_band(
        flags, local_same, swapped(local_cross), same_a, same_b, swapped(cross_a), cross_b
    )
    return place_columns(band_out, col_out)


def solution(mesh):
    in_specs = (P("seq", None), P(), P())
    out_specs = P("seq", None)
    return jax.shard_map(
        on_device, mesh=mesh, in_specs=in_specs, out_specs=out_specs, check_vma=False
    )
```

```python
import functools
import math

import jax
import jax.numpy as jnp
from jax import lax
from jax.experimental import pallas as pl
from jax.experimental.pallas import tpu as pltpu
from jax.sharding import PartitionSpec as P

HEAD = 128
HEADS = 8
STRIDE = 1024
HALF = 512
BLOCK = 256
SCALE2 = math.log2(math.e) / math.sqrt(HEAD)
NEG = -1e30
VMEM_LIMIT = 28 << 20
PROJECT_COST, LOCAL_COST, B_COST, COMPLETE_COST = 0.5, 0.5, 0.5, 20


def params():
    return pltpu.CompilerParams(vmem_limit_bytes=VMEM_LIMIT)


def cost(us):
    return pl.CostEstimate(flops=int(us * 10**9), bytes_accessed=1 << 14, transcendentals=0)


def project_kernel(core_ref, own_ref, sibling_ref, w_ref, kv_a, kv_b, q_a, q_b):
    core = core_ref[0]
    for step, (kind, ref) in enumerate(PROJECT_ORDER):
        ref = {"kv_a": kv_a, "kv_b": kv_b, "q_a": q_a, "q_b": q_b}[ref]

        @pl.when(pl.program_id(0) == step)
        def _():
            for place, x_ref in ((core, own_ref), (1 - core, sibling_ref)):
                value = jnp.dot(x_ref[...], w_ref[...], preferred_element_type=jnp.float32)
                row = pl.multiple_of(place * HALF, HALF)
                if kind == 2:
                    value = value.T.astype(jnp.bfloat16)
                    for block in range(HALF // BLOCK):
                        rows = pl.ds(STRIDE + row + block * BLOCK, BLOCK)
                        ref[rows, :] = value[:, block * BLOCK : (block + 1) * BLOCK]
                else:
                    ref[pl.ds(row, HALF), :] = value.astype(jnp.bfloat16)


PROJECT_ORDER = [(1, "kv_a"), (2, "kv_a"), (0, "q_b"), (1, "kv_b"), (2, "kv_b"), (0, "q_a")]


def project(core, tokens, sibling, w_row):
    depth = tokens.shape[1]

    def weight_block(j, c):
        kind = lax.rem(j + 1, 3)
        pair = jnp.where((j >= 2) & (j <= 4), 1, 0)
        return (0, 4 * kind + 2 * c[0] + pair)

    whole = lambda rows, width: pl.BlockSpec((rows, width), lambda j, c: (0, 0))
    outs = [(2 * STRIDE, BLOCK), (2 * STRIDE, BLOCK), (STRIDE, BLOCK), (STRIDE, BLOCK)]
    return pl.pallas_call(
        project_kernel,
        grid_spec=pltpu.PrefetchScalarGridSpec(
            num_scalar_prefetch=1,
            grid=(len(PROJECT_ORDER),),
            in_specs=[
                whole(HALF, depth),
                whole(HALF, depth),
                pl.BlockSpec((depth, BLOCK), weight_block),
            ],
            out_specs=[whole(*shape) for shape in outs],
        ),
        out_shape=[jax.ShapeDtypeStruct(shape, jnp.bfloat16) for shape in outs],
        compiler_params=params(),
        cost_estimate=cost(PROJECT_COST),
        name="project",
    )(core, tokens, sibling, w_row)


def score_blocks(query, key_ref, columns, spans):
    return [
        lax.dot_general(
            key_ref[low:high, columns], query, (((1,), (1,)), ((), ())),
            preferred_element_type=jnp.float32,
        )
        for low, high in spans
    ]


def softmax_out(scores, biases, value_t_blocks):
    scores = [s if b is None else s + b for s, b in zip(scores, biases)]
    top = functools.reduce(jnp.maximum, [jnp.max(s, axis=0, keepdims=True) for s in scores])
    expd = [jnp.exp2((s - top) * SCALE2) for s in scores]
    total = sum(jnp.sum(e, axis=0, keepdims=True) for e in expd)
    out = sum(
        jnp.dot(v, e.astype(jnp.bfloat16), preferred_element_type=jnp.float32)
        for v, e in zip(value_t_blocks, expd)
    )
    return out, top, total


def pipelined(jobs, ahead, start, finish):
    pending, results = [], {}
    for job in jobs:
        pending.append((job, start(*job)))
        if len(pending) > ahead:
            first, value = pending.pop(0)
            results[first] = finish(*first, value)
    for first, value in pending:
        results[first] = finish(*first, value)
    return results


def split3(value):
    high = value.astype(jnp.bfloat16).astype(jnp.float32)
    rest = value - high
    mid = rest.astype(jnp.bfloat16).astype(jnp.float32)
    return [high, mid, rest - mid]


def columns_of(head):
    return slice(head * HEAD, (head + 1) * HEAD)


def band_jobs(earlier, ahead, q_ref, kv_ref, bias, finish):
    def spans(part):
        low, high = part * BLOCK, (part + 1) * BLOCK
        rest = (high, STRIDE) if earlier else (0, low)
        return [(low, high)] + ([rest] if rest[0] < rest[1] else [])

    def values_t(head, low, high):
        rows = lambda at: slice(STRIDE + at + head * HEAD, STRIDE + at + (head + 1) * HEAD)
        return jnp.concatenate([kv_ref[rows(at), :] for at in range(low, high, BLOCK)], axis=1)

    def start(part, head):
        query = q_ref[part * BLOCK : (part + 1) * BLOCK, columns_of(head)]
        return score_blocks(query, kv_ref, columns_of(head), spans(part))

    def end(part, head, scores):
        values = [values_t(head, low, high) for low, high in spans(part)]
        return finish(part, head, scores, [bias, None], values)

    jobs = [(part, head) for part in range(STRIDE // BLOCK) for head in range(2)]
    return pipelined(jobs, ahead, start, end)


def band_bias(earlier):
    kpos = lax.broadcasted_iota(jnp.int32, (BLOCK, BLOCK), 0)
    qpos = lax.broadcasted_iota(jnp.int32, (BLOCK, BLOCK), 1)
    return jnp.where(kpos > qpos if earlier else kpos <= qpos, 0.0, NEG)


def band_kernel(earlier, pairs, *refs):
    inputs, (out_ref, stat_ref, bias_ref) = refs[: 2 * pairs], refs[2 * pairs :]
    step = pl.program_id(0)
    heads = 2 * pairs

    @pl.when(step == 0)
    def _():
        bias_ref[...] = band_bias(earlier)

    def attend(pair):
        def finish(part, head, scores, biases, values):
            out, top, total = softmax_out(scores, biases, values)
            queries = slice(part * BLOCK, (part + 1) * BLOCK)
            row = (2 * pair + head) * HEAD
            out = out * (1.0 / total)
            out_ref[row : row + HEAD, queries] = out.astype(jnp.bfloat16)
            stat_ref[2 * pair + head, :, queries] = jnp.concatenate(
                split3(top) + split3(total) + [jnp.zeros((2, BLOCK), jnp.float32)], axis=0
            )

        ahead = 2 if earlier else 4
        band_jobs(earlier, ahead, *inputs[2 * pair : 2 * pair + 2], bias_ref[...], finish)

    for pair in range(pairs):

        @pl.when(step == pair)
        def _():
            attend(pair)

    @pl.when(step == pairs - 1)
    def _():
        stats = jnp.concatenate([stat_ref[h] for h in range(heads)], axis=0)
        out_ref[heads * HEAD :, :] = stats.astype(jnp.bfloat16)


def band_part(earlier, *inputs, estimate):
    pairs = len(inputs) // 2
    payload = (2 * pairs * (HEAD + 8), STRIDE)
    whole = lambda shape: pl.BlockSpec(shape, lambda j: (0, 0))
    return pl.pallas_call(
        functools.partial(band_kernel, earlier, pairs),
        grid=(pairs,),
        in_specs=[whole(value.shape) for value in inputs],
        out_specs=whole(payload),
        scratch_shapes=[
            pltpu.VMEM((2 * pairs, 8, STRIDE), jnp.float32),
            pltpu.VMEM((BLOCK, BLOCK), jnp.float32),
        ],
        out_shape=jax.ShapeDtypeStruct(payload, jnp.bfloat16),
        compiler_params=params(),
        cost_estimate=cost(estimate),
        name="band_earlier" if earlier else "band_local",
    )(*inputs)


def complete_kernel(flags_ref, q_ref, kv_ref, local_ref, earlier_ref, same_ref, cross_ref, bias_ref):
    core = flags_ref[0]
    has_earlier = flags_ref[1] > 0
    bias_ref[...] = band_bias(True)

    def stats(ref, heads, head, queries):
        rows = ref[heads * HEAD :, queries].astype(jnp.float32)[8 * head : 8 * head + 8]
        return rows[0:1] + rows[1:2] + rows[2:3], rows[3:4] + rows[4:5] + rows[5:6]

    def merge(part, head, out_e, top_e, scale_e, sum_e):
        queries = slice(part * BLOCK, (part + 1) * BLOCK)
        top_l, sum_l = stats(local_ref, 4, head, queries)
        top_e = jnp.where(has_earlier, top_e, NEG)
        top = jnp.maximum(top_l, top_e)
        weight_l = jnp.exp2((top_l - top) * SCALE2) * sum_l
        weight_e = jnp.where(has_earlier, jnp.exp2((top_e - top) * SCALE2), 0.0)
        inverse = 1.0 / (weight_l + weight_e * sum_e)
        out_l = local_ref[columns_of(head), queries].astype(jnp.float32)
        out = out_l * (weight_l * inverse) + out_e * (weight_e * scale_e * inverse)
        return out.T.astype(jnp.bfloat16)

    def finish(part, head, scores, biases, values):
        out, top, total = softmax_out(scores, biases, values)
        return merge(part, head, out, top, 1.0, total)

    results = band_jobs(True, 2, q_ref, kv_ref, bias_ref[...], finish)
    for part in range(STRIDE // BLOCK):
        queries = slice(part * BLOCK, (part + 1) * BLOCK)
        for head in range(2):
            top, total = stats(earlier_ref, 2, head, queries)
            out = earlier_ref[columns_of(head), queries].astype(jnp.float32)
            results[part, 2 + head] = merge(part, 2 + head, out, top, total, total)

    def store(ref, half):
        for part in range(2):
            for head in range(4):
                rows = slice(part * BLOCK, (part + 1) * BLOCK)
                ref[rows, columns_of(head)] = results[2 * half + part, head]

    @pl.when(core == 0)
    def _():
        store(same_ref, 0)
        store(cross_ref, 1)

    @pl.when(core == 1)
    def _():
        store(same_ref, 1)
        store(cross_ref, 0)


def complete(flags, query, keyval, local, earlier):
    inputs = [query, keyval, local, earlier]
    return pl.pallas_call(
        complete_kernel,
        grid_spec=pltpu.PrefetchScalarGridSpec(
            num_scalar_prefetch=1,
            grid=(1,),
            in_specs=[pl.BlockSpec(value.shape, lambda j, c: (0, 0)) for value in inputs],
            out_specs=[
                pl.BlockSpec((HALF, HALF), lambda j, c: (0, c[0])),
                pl.BlockSpec((HALF, HALF), lambda j, c: (0, 0)),
            ],
            scratch_shapes=[pltpu.VMEM((BLOCK, BLOCK), jnp.float32)],
        ),
        out_shape=[
            jax.ShapeDtypeStruct((HALF, 2 * HEADS * HEAD), jnp.bfloat16),
            jax.ShapeDtypeStruct((HALF, HALF), jnp.bfloat16),
        ],
        compiler_params=params(),
        cost_estimate=cost(COMPLETE_COST),
        name="complete",
    )(flags, *inputs)


def place_kernel(flags_ref, cross_ref, columns_ref, _, o_ref):
    @pl.when(pl.program_id(0) == 0)
    def _():
        o_ref[...] = cross_ref[...]

    @pl.when(pl.program_id(0) > 0)
    def _():
        o_ref[...] = columns_ref[...]


def place(flags, cross, col_out, result):
    return pl.pallas_call(
        place_kernel,
        grid_spec=pltpu.PrefetchScalarGridSpec(
            num_scalar_prefetch=1,
            grid=(3,),
            in_specs=[
                pl.BlockSpec((HALF, HALF), lambda j, c: (0, 0)),
                pl.BlockSpec((HALF, HALF), lambda j, c: (0, jnp.maximum(j - 1, 0))),
                pl.BlockSpec(memory_space=pl.ANY),
            ],
            out_specs=pl.BlockSpec((HALF, HALF), lambda j, c: (0, jnp.where(j == 0, 1 - c[0], 1 + j))),
        ),
        out_shape=jax.ShapeDtypeStruct(result.shape, jnp.bfloat16),
        input_output_aliases={3: 0},
        compiler_params=params(),
        cost_estimate=cost(1),
        name="place",
    )(flags, cross, col_out, result)


def column_kernel(group, q_ref, k_ref, v_ref, o_ref, bias_ref):
    parts = HALF // BLOCK
    heads = q_ref.shape[1] // HEAD

    @pl.when(pl.program_id(0) == 0)
    def _():
        kpos = lax.broadcasted_iota(jnp.int32, (BLOCK, BLOCK), 0)
        qpos = lax.broadcasted_iota(jnp.int32, (BLOCK, BLOCK), 1)
        column = ((qpos - kpos) & (group - 1)) == 0
        bias_ref[0] = jnp.where(column, 0.0, NEG)
        bias_ref[1] = jnp.where(column & (kpos <= qpos), 0.0, NEG)

    values_t = v_ref[...].astype(jnp.float32).T.astype(jnp.bfloat16)

    def spans(part):
        return [(block * BLOCK, (block + 1) * BLOCK) for block in range(part + 1)]

    def columns(head):
        return slice(head * HEAD, (head + 1) * HEAD)

    def start(part, head):
        query = q_ref[part * BLOCK : (part + 1) * BLOCK, columns(head)]
        return score_blocks(query, k_ref, columns(head), spans(part))

    def finish(part, head, scores):
        values = [values_t[columns(head), low:high] for low, high in spans(part)]
        biases = [bias_ref[1 if block == part else 0] for block in range(part + 1)]
        out, _, total = softmax_out(scores, biases, values)
        out = out * (1.0 / total)
        o_ref[part * BLOCK : (part + 1) * BLOCK, columns(head)] = out.T.astype(jnp.bfloat16)

    pipelined([(part, head) for part in range(parts) for head in range(heads)], 2, start, finish)


def column_attention(projected, group):
    rows = projected.shape[0]
    heads = 4
    steps = HEADS // heads
    spec = lambda third: pl.BlockSpec((rows, heads * HEAD), lambda j: (0, third * steps + j))
    return pl.pallas_call(
        functools.partial(column_kernel, group),
        grid=(steps,),
        in_specs=[spec(0), spec(1), spec(2)],
        out_specs=pl.BlockSpec((rows, heads * HEAD), lambda j: (0, j)),
        out_shape=jax.ShapeDtypeStruct((rows, HEADS * HEAD), jnp.bfloat16),
        scratch_shapes=[pltpu.VMEM((2, BLOCK, BLOCK), jnp.float32)],
        compiler_params=params(),
        cost_estimate=cost(6),
        name="column_attention",
    )(projected, projected, projected)


def in_hbm(value):
    return pltpu.with_memory_space_constraint(value, pltpu.HBM)


def after(value, *others):
    return lax.optimization_barrier((value,) + others)[0]


def on_device(tokens, w_row, w_column):
    count = lax.axis_size("seq")
    chips = count // 2
    rank = lax.axis_index("seq")
    core = (rank % 2).astype(jnp.int32)
    core_arr = core.reshape(1)
    flags = jnp.stack([core, (rank >= 2).astype(jnp.int32)])
    group = HALF // chips
    same_core = [list(range(0, count, 2)), list(range(1, count, 2))]

    def exchange(value):
        width = value.shape[1]
        value = lax.all_to_all(
            value.reshape(chips, group, width), "seq", split_axis=0, concat_axis=0,
            axis_index_groups=same_core, tiled=True,
        )
        return value.reshape(HALF, width)

    def swapped(value):
        return lax.ppermute(value, "seq", [(d, d ^ 1) for d in range(count)])

    def to_next(value):
        return lax.ppermute(value, "seq", [(d, d + 2) for d in range(count - 2)])

    w_row = in_hbm(w_row)
    columns = exchange(tokens)
    sibling = swapped(tokens)
    kv_a, kv_b, q_a, q_b = project(core_arr, tokens, sibling, w_row)
    previous_kv_a = to_next(kv_a)
    next_q_b = lax.ppermute(q_b, "seq", [(d, d - 2) for d in range(2, count)])
    local = band_part(False, q_a, kv_a, q_b, kv_b, estimate=LOCAL_COST)
    columns = after(columns, local)
    col_proj = jnp.dot(columns, w_column, preferred_element_type=jnp.float32).astype(jnp.bfloat16)
    sent_b = band_part(True, after(next_q_b, col_proj), kv_b, estimate=B_COST)
    earlier_b = to_next(sent_b)
    col_out = column_attention(after(col_proj, sent_b), group)
    result, cross = complete(flags, q_a, after(previous_kv_a, col_out), local, earlier_b)
    return place(flags, swapped(cross), exchange(col_out), result)


def solution(mesh):
    in_specs = (P("seq", None), P(), P())
    out_specs = P("seq", None)
    return jax.shard_map(
        on_device, mesh=mesh, in_specs=in_specs, out_specs=out_specs, check_vma=False
    )
```

```python
import functools
import math

import jax
import jax.numpy as jnp
from jax import lax
from jax.experimental import pallas as pl
from jax.experimental.pallas import tpu as pltpu
from jax.sharding import PartitionSpec as P

HEAD = 128
HEADS = 8
STRIDE = 1024
HALF = 512
BLOCK = 256
SCALE2 = math.log2(math.e) / math.sqrt(HEAD)
NEG = -1e30
VMEM_LIMIT = 28 << 20
PROJECT_COST, LOCAL_COST, B_COST, COMPLETE_COST = 0.5, 0.5, 0.5, 20


def params():
    return pltpu.CompilerParams(vmem_limit_bytes=VMEM_LIMIT)


def cost(us):
    return pl.CostEstimate(flops=int(us * 10**9), bytes_accessed=1 << 14, transcendentals=0)


def project_kernel(core_ref, own_ref, sibling_ref, w_ref, kv_a, kv_b, q_a, q_b):
    core = core_ref[0]
    for step, (kind, ref) in enumerate(PROJECT_ORDER):
        ref = {"kv_a": kv_a, "kv_b": kv_b, "q_a": q_a, "q_b": q_b}[ref]

        @pl.when(pl.program_id(0) == step)
        def _():
            for place, x_ref in ((core, own_ref), (1 - core, sibling_ref)):
                value = jnp.dot(x_ref[...], w_ref[...], preferred_element_type=jnp.float32)
                row = pl.multiple_of(place * HALF, HALF)
                if kind == 2:
                    value = value.T.astype(jnp.bfloat16)
                    for block in range(HALF // BLOCK):
                        rows = pl.ds(STRIDE + row + block * BLOCK, BLOCK)
                        ref[rows, :] = value[:, block * BLOCK : (block + 1) * BLOCK]
                else:
                    ref[pl.ds(row, HALF), :] = value.astype(jnp.bfloat16)


PROJECT_ORDER = [(1, "kv_a"), (2, "kv_a"), (0, "q_b"), (1, "kv_b"), (2, "kv_b"), (0, "q_a")]


def project(core, tokens, sibling, w_row):
    depth = tokens.shape[1]

    def weight_block(j, c):
        kind = lax.rem(j + 1, 3)
        pair = jnp.where((j >= 2) & (j <= 4), 1, 0)
        return (0, 4 * kind + 2 * c[0] + pair)

    whole = lambda rows, width: pl.BlockSpec((rows, width), lambda j, c: (0, 0))
    outs = [(2 * STRIDE, BLOCK), (2 * STRIDE, BLOCK), (STRIDE, BLOCK), (STRIDE, BLOCK)]
    return pl.pallas_call(
        project_kernel,
        grid_spec=pltpu.PrefetchScalarGridSpec(
            num_scalar_prefetch=1,
            grid=(len(PROJECT_ORDER),),
            in_specs=[
                whole(HALF, depth),
                whole(HALF, depth),
                pl.BlockSpec((depth, BLOCK), weight_block),
            ],
            out_specs=[whole(*shape) for shape in outs],
        ),
        out_shape=[pltpu.HBM(shape, jnp.bfloat16) for shape in outs],
        compiler_params=params(),
        cost_estimate=cost(PROJECT_COST),
        name="project",
    )(core, tokens, sibling, w_row)


def score_blocks(query, key_ref, columns, spans):
    return [
        lax.dot_general(
            key_ref[low:high, columns], query, (((1,), (1,)), ((), ())),
            preferred_element_type=jnp.float32,
        )
        for low, high in spans
    ]


def softmax_out(scores, biases, value_t_blocks):
    scores = [s if b is None else s + b for s, b in zip(scores, biases)]
    top = functools.reduce(jnp.maximum, [jnp.max(s, axis=0, keepdims=True) for s in scores])
    expd = [jnp.exp2((s - top) * SCALE2) for s in scores]
    total = sum(jnp.sum(e, axis=0, keepdims=True) for e in expd)
    out = sum(
        jnp.dot(v, e.astype(jnp.bfloat16), preferred_element_type=jnp.float32)
        for v, e in zip(value_t_blocks, expd)
    )
    return out, top, total


def pipelined(jobs, ahead, start, finish):
    pending, results = [], {}
    for job in jobs:
        pending.append((job, start(*job)))
        if len(pending) > ahead:
            first, value = pending.pop(0)
            results[first] = finish(*first, value)
    for first, value in pending:
        results[first] = finish(*first, value)
    return results


def split3(value):
    high = value.astype(jnp.bfloat16).astype(jnp.float32)
    rest = value - high
    mid = rest.astype(jnp.bfloat16).astype(jnp.float32)
    return [high, mid, rest - mid]


def columns_of(head):
    return slice(head * HEAD, (head + 1) * HEAD)


def band_jobs(earlier, ahead, q_ref, kv_ref, bias, finish):
    def spans(part):
        low, high = part * BLOCK, (part + 1) * BLOCK
        rest = (high, STRIDE) if earlier else (0, low)
        return [(low, high)] + ([rest] if rest[0] < rest[1] else [])

    def values_t(head, low, high):
        rows = lambda at: slice(STRIDE + at + head * HEAD, STRIDE + at + (head + 1) * HEAD)
        return jnp.concatenate([kv_ref[rows(at), :] for at in range(low, high, BLOCK)], axis=1)

    def start(part, head):
        query = q_ref[part * BLOCK : (part + 1) * BLOCK, columns_of(head)]
        return score_blocks(query, kv_ref, columns_of(head), spans(part))

    def end(part, head, scores):
        values = [values_t(head, low, high) for low, high in spans(part)]
        return finish(part, head, scores, [bias, None], values)

    jobs = [(part, head) for part in range(STRIDE // BLOCK) for head in range(2)]
    return pipelined(jobs, ahead, start, end)


def band_bias(earlier):
    kpos = lax.broadcasted_iota(jnp.int32, (BLOCK, BLOCK), 0)
    qpos = lax.broadcasted_iota(jnp.int32, (BLOCK, BLOCK), 1)
    return jnp.where(kpos > qpos if earlier else kpos <= qpos, 0.0, NEG)


def band_kernel(earlier, pairs, *refs):
    inputs, (out_ref, stat_ref, bias_ref) = refs[: 2 * pairs], refs[2 * pairs :]
    step = pl.program_id(0)
    heads = 2 * pairs

    @pl.when(step == 0)
    def _():
        bias_ref[...] = band_bias(earlier)

    def attend(pair):
        def finish(part, head, scores, biases, values):
            out, top, total = softmax_out(scores, biases, values)
            queries = slice(part * BLOCK, (part + 1) * BLOCK)
            row = (2 * pair + head) * HEAD
            out = out * (1.0 / total)
            out_ref[row : row + HEAD, queries] = out.astype(jnp.bfloat16)
            stat_ref[2 * pair + head, :, queries] = jnp.concatenate(
                split3(top) + split3(total) + [jnp.zeros((2, BLOCK), jnp.float32)], axis=0
            )

        ahead = 2 if earlier else 4
        band_jobs(earlier, ahead, *inputs[2 * pair : 2 * pair + 2], bias_ref[...], finish)

    for pair in range(pairs):

        @pl.when(step == pair)
        def _():
            attend(pair)

    @pl.when(step == pairs - 1)
    def _():
        stats = jnp.concatenate([stat_ref[h] for h in range(heads)], axis=0)
        out_ref[heads * HEAD :, :] = stats.astype(jnp.bfloat16)


def band_part(earlier, *inputs, estimate):
    pairs = len(inputs) // 2
    payload = (2 * pairs * (HEAD + 8), STRIDE)
    whole = lambda shape: pl.BlockSpec(shape, lambda j: (0, 0))
    return pl.pallas_call(
        functools.partial(band_kernel, earlier, pairs),
        grid=(pairs,),
        in_specs=[whole(value.shape) for value in inputs],
        out_specs=whole(payload),
        scratch_shapes=[
            pltpu.VMEM((2 * pairs, 8, STRIDE), jnp.float32),
            pltpu.VMEM((BLOCK, BLOCK), jnp.float32),
        ],
        out_shape=pltpu.HBM(payload, jnp.bfloat16),
        compiler_params=params(),
        cost_estimate=cost(estimate),
        name="band_earlier" if earlier else "band_local",
    )(*inputs)


def complete_kernel(flags_ref, q_ref, kv_ref, local_ref, earlier_ref, same_ref, cross_ref, bias_ref):
    core = flags_ref[0]
    has_earlier = flags_ref[1] > 0
    bias_ref[...] = band_bias(True)

    def stats(ref, heads, head, queries):
        rows = ref[heads * HEAD :, queries].astype(jnp.float32)[8 * head : 8 * head + 8]
        return rows[0:1] + rows[1:2] + rows[2:3], rows[3:4] + rows[4:5] + rows[5:6]

    def merge(part, head, out_e, top_e, scale_e, sum_e):
        queries = slice(part * BLOCK, (part + 1) * BLOCK)
        top_l, sum_l = stats(local_ref, 4, head, queries)
        top_e = jnp.where(has_earlier, top_e, NEG)
        top = jnp.maximum(top_l, top_e)
        weight_l = jnp.exp2((top_l - top) * SCALE2) * sum_l
        weight_e = jnp.where(has_earlier, jnp.exp2((top_e - top) * SCALE2), 0.0)
        inverse = 1.0 / (weight_l + weight_e * sum_e)
        out_l = local_ref[columns_of(head), queries].astype(jnp.float32)
        out = out_l * (weight_l * inverse) + out_e * (weight_e * scale_e * inverse)
        return out.T.astype(jnp.bfloat16)

    def finish(part, head, scores, biases, values):
        out, top, total = softmax_out(scores, biases, values)
        return merge(part, head, out, top, 1.0, total)

    results = band_jobs(True, 2, q_ref, kv_ref, bias_ref[...], finish)
    for part in range(STRIDE // BLOCK):
        queries = slice(part * BLOCK, (part + 1) * BLOCK)
        for head in range(2):
            top, total = stats(earlier_ref, 2, head, queries)
            out = earlier_ref[columns_of(head), queries].astype(jnp.float32)
            results[part, 2 + head] = merge(part, 2 + head, out, top, total, total)

    def store(ref, half):
        for part in range(2):
            for head in range(4):
                rows = slice(part * BLOCK, (part + 1) * BLOCK)
                ref[rows, columns_of(head)] = results[2 * half + part, head]

    @pl.when(core == 0)
    def _():
        store(same_ref, 0)
        store(cross_ref, 1)

    @pl.when(core == 1)
    def _():
        store(same_ref, 1)
        store(cross_ref, 0)


def complete(flags, query, keyval, local, earlier):
    inputs = [query, keyval, local, earlier]
    return pl.pallas_call(
        complete_kernel,
        grid_spec=pltpu.PrefetchScalarGridSpec(
            num_scalar_prefetch=1,
            grid=(1,),
            in_specs=[pl.BlockSpec(value.shape, lambda j, c: (0, 0)) for value in inputs],
            out_specs=[
                pl.BlockSpec((HALF, HALF), lambda j, c: (0, c[0])),
                pl.BlockSpec((HALF, HALF), lambda j, c: (0, 0)),
            ],
            scratch_shapes=[pltpu.VMEM((BLOCK, BLOCK), jnp.float32)],
        ),
        out_shape=[
            jax.ShapeDtypeStruct((HALF, 2 * HEADS * HEAD), jnp.bfloat16),
            jax.ShapeDtypeStruct((HALF, HALF), jnp.bfloat16),
        ],
        compiler_params=params(),
        cost_estimate=cost(COMPLETE_COST),
        name="complete",
    )(flags, *inputs)


def place_kernel(flags_ref, cross_ref, columns_ref, _, o_ref, sems):
    first = pl.multiple_of((1 - flags_ref[0]) * HALF, HALF)
    width = columns_ref.shape[1]
    copies = [
        pltpu.make_async_copy(cross_ref, o_ref.at[:, pl.ds(first, HALF)], sems.at[0]),
        pltpu.make_async_copy(columns_ref, o_ref.at[:, pl.ds(width, width)], sems.at[1]),
    ]
    for copy in copies:
        copy.start()
    for copy in copies:
        copy.wait()


def place(flags, cross, col_out, result):
    anywhere = pl.BlockSpec(memory_space=pl.ANY)
    return pl.pallas_call(
        place_kernel,
        grid_spec=pltpu.PrefetchScalarGridSpec(
            num_scalar_prefetch=1,
            grid=(1,),
            in_specs=[anywhere] * 3,
            out_specs=anywhere,
            scratch_shapes=[pltpu.SemaphoreType.DMA((2,))],
        ),
        out_shape=jax.ShapeDtypeStruct(result.shape, jnp.bfloat16),
        input_output_aliases={3: 0},
        compiler_params=params(),
        cost_estimate=cost(1),
        name="place",
    )(flags, cross, col_out, result)


def column_kernel(group, q_ref, k_ref, v_ref, o_ref, bias_ref):
    parts = HALF // BLOCK
    heads = q_ref.shape[1] // HEAD

    @pl.when(pl.program_id(0) == 0)
    def _():
        qpos = lax.broadcasted_iota(jnp.int32, (BLOCK, BLOCK), 0)
        kpos = lax.broadcasted_iota(jnp.int32, (BLOCK, BLOCK), 1)
        column = ((qpos - kpos) & (group - 1)) == 0
        bias_ref[0] = jnp.where(column, 0.0, NEG)
        bias_ref[1] = jnp.where(column & (kpos <= qpos), 0.0, NEG)

    def rows(block):
        return slice(block * BLOCK, (block + 1) * BLOCK)

    def start(part, head):
        query = q_ref[rows(part), columns_of(head)]
        return [
            lax.dot_general(
                query, k_ref[rows(block), columns_of(head)], (((1,), (1,)), ((), ())),
                preferred_element_type=jnp.float32,
            )
            for block in range(part + 1)
        ]

    def finish(part, head, scores):
        scores = [s + bias_ref[1 if block == part else 0] for block, s in enumerate(scores)]
        top = jnp.max(functools.reduce(jnp.maximum, scores), axis=1, keepdims=True)
        out = 0.0
        for block, s in enumerate(scores):
            values = v_ref[rows(block), columns_of(head)]
            values = jnp.concatenate([values, jnp.ones_like(values)], axis=1)
            expd = jnp.exp2((s - top) * SCALE2).astype(jnp.bfloat16)
            out = out + jnp.dot(expd, values, preferred_element_type=jnp.float32)
        out = out[:, :HEAD] * (1.0 / out[:, HEAD:])
        o_ref[rows(part), columns_of(head)] = out.astype(jnp.bfloat16)

    pipelined([(part, head) for part in range(parts) for head in range(heads)], 4, start, finish)


def column_attention(projected, group):
    rows = projected.shape[0]
    heads = 4
    steps = HEADS // heads
    spec = lambda third: pl.BlockSpec((rows, heads * HEAD), lambda j: (0, third * steps + j))
    return pl.pallas_call(
        functools.partial(column_kernel, group),
        grid=(steps,),
        in_specs=[spec(0), spec(1), spec(2)],
        out_specs=pl.BlockSpec((rows, heads * HEAD), lambda j: (0, j)),
        out_shape=jax.ShapeDtypeStruct((rows, HEADS * HEAD), jnp.bfloat16),
        scratch_shapes=[pltpu.VMEM((2, BLOCK, BLOCK), jnp.float32)],
        compiler_params=params(),
        cost_estimate=cost(6),
        name="column_attention",
    )(projected, projected, projected)


def in_hbm(value):
    return pltpu.with_memory_space_constraint(value, pltpu.HBM)


def after(value, *others):
    return lax.optimization_barrier((value,) + others)[0]


def on_device(tokens, w_row, w_column):
    count = lax.axis_size("seq")
    chips = count // 2
    rank = lax.axis_index("seq")
    core = (rank % 2).astype(jnp.int32)
    core_arr = core.reshape(1)
    flags = jnp.stack([core, (rank >= 2).astype(jnp.int32)])
    group = HALF // chips
    same_core = [list(range(0, count, 2)), list(range(1, count, 2))]

    def exchange(value):
        width = value.shape[1]
        value = lax.all_to_all(
            value.reshape(chips, group, width), "seq", split_axis=0, concat_axis=0,
            axis_index_groups=same_core, tiled=True,
        )
        return value.reshape(HALF, width)

    def swapped(value):
        return lax.ppermute(value, "seq", [(d, d ^ 1) for d in range(count)])

    def to_next(value):
        return lax.ppermute(value, "seq", [(d, d + 2) for d in range(count - 2)])

    w_row = in_hbm(w_row)
    columns = exchange(tokens)
    sibling = swapped(tokens)
    kv_a, kv_b, q_a, q_b = project(core_arr, tokens, sibling, w_row)
    kv_a, kv_b, q_a, q_b = [in_hbm(value) for value in (kv_a, kv_b, q_a, q_b)]
    previous_kv_a = to_next(kv_a)
    next_q_b = lax.ppermute(q_b, "seq", [(d, d - 2) for d in range(2, count)])
    local = band_part(False, q_a, kv_a, q_b, kv_b, estimate=LOCAL_COST)
    columns = after(columns, local)
    col_proj = jnp.dot(columns, w_column, preferred_element_type=jnp.float32).astype(jnp.bfloat16)
    sent_b = band_part(True, after(next_q_b, col_proj), kv_b, estimate=B_COST)
    earlier_b = to_next(sent_b)
    col_out = column_attention(after(col_proj, sent_b), group)
    result, cross = complete(flags, q_a, after(previous_kv_a, col_out), in_hbm(local), earlier_b)
    return place(flags, swapped(cross), exchange(col_out), result)


def solution(mesh):
    in_specs = (P("seq", None), P(), P())
    out_specs = P("seq", None)
    return jax.shard_map(
        on_device, mesh=mesh, in_specs=in_specs, out_specs=out_specs, check_vma=False
    )
```

```python
import functools
import math

import jax
import jax.numpy as jnp
from jax import lax
from jax.experimental import pallas as pl
from jax.experimental.pallas import tpu as pltpu
from jax.sharding import PartitionSpec as P

HEAD = 128
HEADS = 8
STRIDE = 1024
HALF = 512
BLOCK = 256
SCALE2 = math.log2(math.e) / math.sqrt(HEAD)
NEG = -1e30
VMEM_LIMIT = 28 << 20
PROJECT_COST, LOCAL_COST, B_COST, COMPLETE_COST = 0.5, 0.5, 0.5, 20


def params():
    return pltpu.CompilerParams(vmem_limit_bytes=VMEM_LIMIT)


def cost(us):
    return pl.CostEstimate(flops=int(us * 10**9), bytes_accessed=1 << 14, transcendentals=0)


def project_kernel(core_ref, own_ref, sibling_ref, w_ref, kv_a, kv_b, q_a, q_b):
    core = core_ref[0]
    for step, (kind, ref) in enumerate(PROJECT_ORDER):
        ref = {"kv_a": kv_a, "kv_b": kv_b, "q_a": q_a, "q_b": q_b}[ref]

        @pl.when(pl.program_id(0) == step)
        def _():
            for place, x_ref in ((core, own_ref), (1 - core, sibling_ref)):
                value = jnp.dot(x_ref[...], w_ref[...], preferred_element_type=jnp.float32)
                row = pl.multiple_of(place * HALF, HALF)
                if kind == 2:
                    value = value.T.astype(jnp.bfloat16)
                    for block in range(HALF // BLOCK):
                        rows = pl.ds(STRIDE + row + block * BLOCK, BLOCK)
                        ref[rows, :] = value[:, block * BLOCK : (block + 1) * BLOCK]
                else:
                    ref[pl.ds(row, HALF), :] = value.astype(jnp.bfloat16)


PROJECT_ORDER = [(1, "kv_a"), (2, "kv_a"), (0, "q_b"), (1, "kv_b"), (2, "kv_b"), (0, "q_a")]


def project(core, tokens, sibling, w_row):
    depth = tokens.shape[1]

    def weight_block(j, c):
        kind = lax.rem(j + 1, 3)
        pair = jnp.where((j >= 2) & (j <= 4), 1, 0)
        return (0, 4 * kind + 2 * c[0] + pair)

    whole = lambda rows, width: pl.BlockSpec((rows, width), lambda j, c: (0, 0))
    outs = [(2 * STRIDE, BLOCK), (2 * STRIDE, BLOCK), (STRIDE, BLOCK), (STRIDE, BLOCK)]
    return pl.pallas_call(
        project_kernel,
        grid_spec=pltpu.PrefetchScalarGridSpec(
            num_scalar_prefetch=1,
            grid=(len(PROJECT_ORDER),),
            in_specs=[
                whole(HALF, depth),
                whole(HALF, depth),
                pl.BlockSpec((depth, BLOCK), weight_block),
            ],
            out_specs=[whole(*shape) for shape in outs],
        ),
        out_shape=[jax.ShapeDtypeStruct(shape, jnp.bfloat16) for shape in outs],
        compiler_params=params(),
        cost_estimate=cost(PROJECT_COST),
        name="project",
    )(core, tokens, sibling, w_row)


def score_blocks(query, key_ref, columns, spans):
    return [
        lax.dot_general(
            key_ref[low:high, columns], query, (((1,), (1,)), ((), ())),
            preferred_element_type=jnp.float32,
        )
        for low, high in spans
    ]


def softmax_out(scores, biases, value_t_blocks):
    scores = [s if b is None else s + b for s, b in zip(scores, biases)]
    top = functools.reduce(jnp.maximum, [jnp.max(s, axis=0, keepdims=True) for s in scores])
    expd = [jnp.exp2((s - top) * SCALE2) for s in scores]
    total = sum(jnp.sum(e, axis=0, keepdims=True) for e in expd)
    out = sum(
        jnp.dot(v, e.astype(jnp.bfloat16), preferred_element_type=jnp.float32)
        for v, e in zip(value_t_blocks, expd)
    )
    return out, top, total


def pipelined(jobs, ahead, start, finish):
    pending, results = [], {}
    for job in jobs:
        pending.append((job, start(*job)))
        if len(pending) > ahead:
            first, value = pending.pop(0)
            results[first] = finish(*first, value)
    for first, value in pending:
        results[first] = finish(*first, value)
    return results


def split3(value):
    high = value.astype(jnp.bfloat16).astype(jnp.float32)
    rest = value - high
    mid = rest.astype(jnp.bfloat16).astype(jnp.float32)
    return [high, mid, rest - mid]


def columns_of(head):
    return slice(head * HEAD, (head + 1) * HEAD)


def band_jobs(earlier, ahead, q_ref, kv_ref, bias, finish):
    def spans(part):
        low, high = part * BLOCK, (part + 1) * BLOCK
        rest = (high, STRIDE) if earlier else (0, low)
        return [(low, high)] + ([rest] if rest[0] < rest[1] else [])

    def values_t(head, low, high):
        rows = lambda at: slice(STRIDE + at + head * HEAD, STRIDE + at + (head + 1) * HEAD)
        return jnp.concatenate([kv_ref[rows(at), :] for at in range(low, high, BLOCK)], axis=1)

    def start(part, head):
        query = q_ref[part * BLOCK : (part + 1) * BLOCK, columns_of(head)]
        return score_blocks(query, kv_ref, columns_of(head), spans(part))

    def end(part, head, scores):
        values = [values_t(head, low, high) for low, high in spans(part)]
        return finish(part, head, scores, [bias, None], values)

    jobs = [(part, head) for part in range(STRIDE // BLOCK) for head in range(2)]
    return pipelined(jobs, ahead, start, end)


def band_bias(earlier):
    kpos = lax.broadcasted_iota(jnp.int32, (BLOCK, BLOCK), 0)
    qpos = lax.broadcasted_iota(jnp.int32, (BLOCK, BLOCK), 1)
    return jnp.where(kpos > qpos if earlier else kpos <= qpos, 0.0, NEG)


def band_kernel(earlier, pairs, *refs):
    inputs, (out_ref, stat_ref, bias_ref) = refs[: 2 * pairs], refs[2 * pairs :]
    step = pl.program_id(0)
    heads = 2 * pairs

    @pl.when(step == 0)
    def _():
        bias_ref[...] = band_bias(earlier)

    def attend(pair):
        def finish(part, head, scores, biases, values):
            out, top, total = softmax_out(scores, biases, values)
            queries = slice(part * BLOCK, (part + 1) * BLOCK)
            row = (2 * pair + head) * HEAD
            out = out * (1.0 / total)
            out_ref[row : row + HEAD, queries] = out.astype(jnp.bfloat16)
            stat_ref[2 * pair + head, :, queries] = jnp.concatenate(
                split3(top) + split3(total) + [jnp.zeros((2, BLOCK), jnp.float32)], axis=0
            )

        ahead = 2 if earlier else 4
        band_jobs(earlier, ahead, *inputs[2 * pair : 2 * pair + 2], bias_ref[...], finish)

    for pair in range(pairs):

        @pl.when(step == pair)
        def _():
            attend(pair)

    @pl.when(step == pairs - 1)
    def _():
        stats = jnp.concatenate([stat_ref[h] for h in range(heads)], axis=0)
        out_ref[heads * HEAD :, :] = stats.astype(jnp.bfloat16)


def band_part(earlier, *inputs, estimate):
    pairs = len(inputs) // 2
    payload = (2 * pairs * (HEAD + 8), STRIDE)
    whole = lambda shape: pl.BlockSpec(shape, lambda j: (0, 0))
    return pl.pallas_call(
        functools.partial(band_kernel, earlier, pairs),
        grid=(pairs,),
        in_specs=[whole(value.shape) for value in inputs],
        out_specs=whole(payload),
        scratch_shapes=[
            pltpu.VMEM((2 * pairs, 8, STRIDE), jnp.float32),
            pltpu.VMEM((BLOCK, BLOCK), jnp.float32),
        ],
        out_shape=(jax.ShapeDtypeStruct if earlier else pltpu.HBM)(payload, jnp.bfloat16),
        compiler_params=params(),
        cost_estimate=cost(estimate),
        name="band_earlier" if earlier else "band_local",
    )(*inputs)


def complete_kernel(flags_ref, q_ref, kv_ref, local_ref, earlier_ref, same_ref, cross_ref, bias_ref):
    core = flags_ref[0]
    has_earlier = flags_ref[1] > 0
    bias_ref[...] = band_bias(True)

    def stats(ref, heads, head, queries):
        rows = ref[heads * HEAD :, queries].astype(jnp.float32)[8 * head : 8 * head + 8]
        return rows[0:1] + rows[1:2] + rows[2:3], rows[3:4] + rows[4:5] + rows[5:6]

    def merge(part, head, out_e, top_e, scale_e, sum_e):
        queries = slice(part * BLOCK, (part + 1) * BLOCK)
        top_l, sum_l = stats(local_ref, 4, head, queries)
        top_e = jnp.where(has_earlier, top_e, NEG)
        top = jnp.maximum(top_l, top_e)
        weight_l = jnp.exp2((top_l - top) * SCALE2) * sum_l
        weight_e = jnp.where(has_earlier, jnp.exp2((top_e - top) * SCALE2), 0.0)
        inverse = 1.0 / (weight_l + weight_e * sum_e)
        out_l = local_ref[columns_of(head), queries].astype(jnp.float32)
        out = out_l * (weight_l * inverse) + out_e * (weight_e * scale_e * inverse)
        return out.T.astype(jnp.bfloat16)

    def finish(part, head, scores, biases, values):
        out, top, total = softmax_out(scores, biases, values)
        return merge(part, head, out, top, 1.0, total)

    results = band_jobs(True, 2, q_ref, kv_ref, bias_ref[...], finish)
    for part in range(STRIDE // BLOCK):
        queries = slice(part * BLOCK, (part + 1) * BLOCK)
        for head in range(2):
            top, total = stats(earlier_ref, 2, head, queries)
            out = earlier_ref[columns_of(head), queries].astype(jnp.float32)
            results[part, 2 + head] = merge(part, 2 + head, out, top, total, total)

    def store(ref, half):
        for part in range(2):
            for head in range(4):
                rows = slice(part * BLOCK, (part + 1) * BLOCK)
                ref[rows, columns_of(head)] = results[2 * half + part, head]

    @pl.when(core == 0)
    def _():
        store(same_ref, 0)
        store(cross_ref, 1)

    @pl.when(core == 1)
    def _():
        store(same_ref, 1)
        store(cross_ref, 0)


def complete(flags, query, keyval, local, earlier):
    inputs = [query, keyval, local, earlier]
    return pl.pallas_call(
        complete_kernel,
        grid_spec=pltpu.PrefetchScalarGridSpec(
            num_scalar_prefetch=1,
            grid=(1,),
            in_specs=[pl.BlockSpec(value.shape, lambda j, c: (0, 0)) for value in inputs],
            out_specs=[
                pl.BlockSpec((HALF, HALF), lambda j, c: (0, c[0])),
                pl.BlockSpec((HALF, HALF), lambda j, c: (0, 0)),
            ],
            scratch_shapes=[pltpu.VMEM((BLOCK, BLOCK), jnp.float32)],
        ),
        out_shape=[
            jax.ShapeDtypeStruct((HALF, 2 * HEADS * HEAD), jnp.bfloat16),
            jax.ShapeDtypeStruct((HALF, HALF), jnp.bfloat16),
        ],
        compiler_params=params(),
        cost_estimate=cost(COMPLETE_COST),
        name="complete",
    )(flags, *inputs)


def place_kernel(flags_ref, cross_ref, columns_ref, _, o_ref, sems):
    first = pl.multiple_of((1 - flags_ref[0]) * HALF, HALF)
    width = columns_ref.shape[1]
    copies = [
        pltpu.make_async_copy(cross_ref, o_ref.at[:, pl.ds(first, HALF)], sems.at[0]),
        pltpu.make_async_copy(columns_ref, o_ref.at[:, pl.ds(width, width)], sems.at[1]),
    ]
    for copy in copies:
        copy.start()
    for copy in copies:
        copy.wait()


def place(flags, cross, col_out, result):
    anywhere = pl.BlockSpec(memory_space=pl.ANY)
    return pl.pallas_call(
        place_kernel,
        grid_spec=pltpu.PrefetchScalarGridSpec(
            num_scalar_prefetch=1,
            grid=(1,),
            in_specs=[anywhere] * 3,
            out_specs=anywhere,
            scratch_shapes=[pltpu.SemaphoreType.DMA((2,))],
        ),
        out_shape=jax.ShapeDtypeStruct(result.shape, jnp.bfloat16),
        input_output_aliases={3: 0},
        compiler_params=params(),
        cost_estimate=cost(1),
        name="place",
    )(flags, cross, col_out, result)


def column_kernel(group, q_ref, k_ref, v_ref, o_ref, bias_ref):
    parts = HALF // BLOCK
    heads = q_ref.shape[1] // HEAD

    @pl.when(pl.program_id(0) == 0)
    def _():
        qpos = lax.broadcasted_iota(jnp.int32, (BLOCK, BLOCK), 0)
        kpos = lax.broadcasted_iota(jnp.int32, (BLOCK, BLOCK), 1)
        column = ((qpos - kpos) & (group - 1)) == 0
        bias_ref[0] = jnp.where(column, 0.0, NEG)
        bias_ref[1] = jnp.where(column & (kpos <= qpos), 0.0, NEG)

    def rows(block):
        return slice(block * BLOCK, (block + 1) * BLOCK)

    def start(part, head):
        query = q_ref[rows(part), columns_of(head)]
        return [
            lax.dot_general(
                query, k_ref[rows(block), columns_of(head)], (((1,), (1,)), ((), ())),
                preferred_element_type=jnp.float32,
            )
            for block in range(part + 1)
        ]

    def finish(part, head, scores):
        scores = [s + bias_ref[1 if block == part else 0] for block, s in enumerate(scores)]
        top = jnp.max(functools.reduce(jnp.maximum, scores), axis=1, keepdims=True)
        out = 0.0
        for block, s in enumerate(scores):
            values = v_ref[rows(block), columns_of(head)]
            values = jnp.concatenate([values, jnp.ones_like(values)], axis=1)
            expd = jnp.exp2((s - top) * SCALE2).astype(jnp.bfloat16)
            out = out + jnp.dot(expd, values, preferred_element_type=jnp.float32)
        out = out[:, :HEAD] * (1.0 / out[:, HEAD:])
        o_ref[rows(part), columns_of(head)] = out.astype(jnp.bfloat16)

    pipelined([(part, head) for part in range(parts) for head in range(heads)], 4, start, finish)


def column_attention(projected, group):
    rows = projected.shape[0]
    heads = 4
    steps = HEADS // heads
    spec = lambda third: pl.BlockSpec((rows, heads * HEAD), lambda j: (0, third * steps + j))
    return pl.pallas_call(
        functools.partial(column_kernel, group),
        grid=(steps,),
        in_specs=[spec(0), spec(1), spec(2)],
        out_specs=pl.BlockSpec((rows, heads * HEAD), lambda j: (0, j)),
        out_shape=jax.ShapeDtypeStruct((rows, HEADS * HEAD), jnp.bfloat16),
        scratch_shapes=[pltpu.VMEM((2, BLOCK, BLOCK), jnp.float32)],
        compiler_params=params(),
        cost_estimate=cost(6),
        name="column_attention",
    )(projected, projected, projected)


def in_hbm(value):
    return pltpu.with_memory_space_constraint(value, pltpu.HBM)


def after(value, *others):
    return lax.optimization_barrier((value,) + others)[0]


def on_device(tokens, w_row, w_column):
    count = lax.axis_size("seq")
    chips = count // 2
    rank = lax.axis_index("seq")
    core = (rank % 2).astype(jnp.int32)
    core_arr = core.reshape(1)
    flags = jnp.stack([core, (rank >= 2).astype(jnp.int32)])
    group = HALF // chips
    same_core = [list(range(0, count, 2)), list(range(1, count, 2))]

    def exchange(value):
        width = value.shape[1]
        value = lax.all_to_all(
            value.reshape(chips, group, width), "seq", split_axis=0, concat_axis=0,
            axis_index_groups=same_core, tiled=True,
        )
        return value.reshape(HALF, width)

    def swapped(value):
        return lax.ppermute(value, "seq", [(d, d ^ 1) for d in range(count)])

    def to_next(value):
        return lax.ppermute(value, "seq", [(d, d + 2) for d in range(count - 2)])

    w_row = in_hbm(w_row)
    columns = exchange(tokens)
    sibling = swapped(tokens)
    kv_a, kv_b, q_a, q_b = project(core_arr, tokens, sibling, w_row)
    local = band_part(False, q_a, kv_a, q_b, kv_b, estimate=LOCAL_COST)
    previous_kv_a = to_next(after(kv_a, local))
    next_q_b = lax.ppermute(after(q_b, local), "seq", [(d, d - 2) for d in range(2, count)])
    columns = after(columns, local)
    col_proj = jnp.dot(columns, w_column, preferred_element_type=jnp.float32).astype(jnp.bfloat16)
    sent_b = band_part(True, after(next_q_b, col_proj), kv_b, estimate=B_COST)
    earlier_b = to_next(sent_b)
    col_out = column_attention(after(col_proj, sent_b), group)
    result, cross = complete(flags, q_a, after(previous_kv_a, col_out), in_hbm(local), earlier_b)
    return place(flags, swapped(cross), exchange(col_out), result)


def solution(mesh):
    in_specs = (P("seq", None), P(), P())
    out_specs = P("seq", None)
    return jax.shard_map(
        on_device, mesh=mesh, in_specs=in_specs, out_specs=out_specs, check_vma=False
    )
```

```python
import functools
import math

import jax
import jax.numpy as jnp
from jax import lax
from jax.experimental import pallas as pl
from jax.experimental.pallas import tpu as pltpu
from jax.sharding import PartitionSpec as P

HEAD = 128
HEADS = 8
STRIDE = 1024
HALF = 512
BLOCK = 256
SCALE2 = math.log2(math.e) / math.sqrt(HEAD)
NEG = -1e30
VMEM_LIMIT = 28 << 20
PROJECT_COST, LOCAL_COST, B_COST, COMPLETE_COST = 0.5, 0.5, 0.5, 20


def params():
    return pltpu.CompilerParams(vmem_limit_bytes=VMEM_LIMIT)


def cost(us):
    return pl.CostEstimate(flops=int(us * 10**9), bytes_accessed=1 << 14, transcendentals=0)


def project_kernel(core_ref, own_ref, sibling_ref, w_ref, kv_a, kv_b, q_a, q_b):
    core = core_ref[0]
    for step, (kind, ref) in enumerate(PROJECT_ORDER):
        ref = {"kv_a": kv_a, "kv_b": kv_b, "q_a": q_a, "q_b": q_b}[ref]

        @pl.when(pl.program_id(0) == step)
        def _():
            for place, x_ref in ((core, own_ref), (1 - core, sibling_ref)):
                value = jnp.dot(x_ref[...], w_ref[...], preferred_element_type=jnp.float32)
                row = pl.multiple_of(place * HALF, HALF)
                if kind == 2:
                    value = value.T.astype(jnp.bfloat16)
                    for block in range(HALF // BLOCK):
                        rows = pl.ds(STRIDE + row + block * BLOCK, BLOCK)
                        ref[rows, :] = value[:, block * BLOCK : (block + 1) * BLOCK]
                else:
                    ref[pl.ds(row, HALF), :] = value.astype(jnp.bfloat16)


PROJECT_ORDER = [(1, "kv_a"), (2, "kv_a"), (0, "q_b"), (1, "kv_b"), (2, "kv_b"), (0, "q_a")]


def project(core, tokens, sibling, w_row):
    depth = tokens.shape[1]

    def weight_block(j, c):
        kind = lax.rem(j + 1, 3)
        pair = jnp.where((j >= 2) & (j <= 4), 1, 0)
        return (0, 4 * kind + 2 * c[0] + pair)

    whole = lambda rows, width: pl.BlockSpec((rows, width), lambda j, c: (0, 0))
    outs = [(2 * STRIDE, BLOCK), (2 * STRIDE, BLOCK), (STRIDE, BLOCK), (STRIDE, BLOCK)]
    return pl.pallas_call(
        project_kernel,
        grid_spec=pltpu.PrefetchScalarGridSpec(
            num_scalar_prefetch=1,
            grid=(len(PROJECT_ORDER),),
            in_specs=[
                whole(HALF, depth),
                whole(HALF, depth),
                pl.BlockSpec((depth, BLOCK), weight_block),
            ],
            out_specs=[whole(*shape) for shape in outs],
        ),
        out_shape=[jax.ShapeDtypeStruct(shape, jnp.bfloat16) for shape in outs],
        compiler_params=params(),
        cost_estimate=cost(PROJECT_COST),
        name="project",
    )(core, tokens, sibling, w_row)


def score_blocks(query, key_ref, columns, spans):
    return [
        lax.dot_general(
            key_ref[low:high, columns], query, (((1,), (1,)), ((), ())),
            preferred_element_type=jnp.float32,
        )
        for low, high in spans
    ]


def softmax_out(scores, biases, value_t_blocks):
    scores = [s if b is None else s + b for s, b in zip(scores, biases)]
    top = functools.reduce(jnp.maximum, [jnp.max(s, axis=0, keepdims=True) for s in scores])
    expd = [jnp.exp2((s - top) * SCALE2) for s in scores]
    total = sum(jnp.sum(e, axis=0, keepdims=True) for e in expd)
    out = sum(
        jnp.dot(v, e.astype(jnp.bfloat16), preferred_element_type=jnp.float32)
        for v, e in zip(value_t_blocks, expd)
    )
    return out, top, total


def pipelined(jobs, ahead, start, finish):
    pending, results = [], {}
    for job in jobs:
        pending.append((job, start(*job)))
        if len(pending) > ahead:
            first, value = pending.pop(0)
            results[first] = finish(*first, value)
    for first, value in pending:
        results[first] = finish(*first, value)
    return results


def split3(value):
    high = value.astype(jnp.bfloat16).astype(jnp.float32)
    rest = value - high
    mid = rest.astype(jnp.bfloat16).astype(jnp.float32)
    return [high, mid, rest - mid]


def columns_of(head):
    return slice(head * HEAD, (head + 1) * HEAD)


def band_jobs(earlier, ahead, q_ref, kv_ref, bias, finish):
    def spans(part):
        low, high = part * BLOCK, (part + 1) * BLOCK
        rest = (high, STRIDE) if earlier else (0, low)
        return [(low, high)] + ([rest] if rest[0] < rest[1] else [])

    def values_t(head, low, high):
        rows = lambda at: slice(STRIDE + at + head * HEAD, STRIDE + at + (head + 1) * HEAD)
        return jnp.concatenate([kv_ref[rows(at), :] for at in range(low, high, BLOCK)], axis=1)

    def start(part, head):
        query = q_ref[part * BLOCK : (part + 1) * BLOCK, columns_of(head)]
        return score_blocks(query, kv_ref, columns_of(head), spans(part))

    def end(part, head, scores):
        values = [values_t(head, low, high) for low, high in spans(part)]
        return finish(part, head, scores, [bias, None], values)

    jobs = [(part, head) for part in range(STRIDE // BLOCK) for head in range(2)]
    return pipelined(jobs, ahead, start, end)


def band_bias(earlier):
    kpos = lax.broadcasted_iota(jnp.int32, (BLOCK, BLOCK), 0)
    qpos = lax.broadcasted_iota(jnp.int32, (BLOCK, BLOCK), 1)
    return jnp.where(kpos > qpos if earlier else kpos <= qpos, 0.0, NEG)


def band_kernel(earlier, pairs, *refs):
    inputs, (out_ref, stat_ref, bias_ref) = refs[: 2 * pairs], refs[2 * pairs :]
    step = pl.program_id(0)
    heads = 2 * pairs

    @pl.when(step == 0)
    def _():
        bias_ref[...] = band_bias(earlier)

    def attend(pair):
        def finish(part, head, scores, biases, values):
            out, top, total = softmax_out(scores, biases, values)
            queries = slice(part * BLOCK, (part + 1) * BLOCK)
            row = (2 * pair + head) * HEAD
            out = out * (1.0 / total)
            out_ref[row : row + HEAD, queries] = out.astype(jnp.bfloat16)
            stat_ref[2 * pair + head, :, queries] = jnp.concatenate(
                split3(top) + split3(total) + [jnp.zeros((2, BLOCK), jnp.float32)], axis=0
            )

        ahead = 2 if earlier else 4
        band_jobs(earlier, ahead, *inputs[2 * pair : 2 * pair + 2], bias_ref[...], finish)

    for pair in range(pairs):

        @pl.when(step == pair)
        def _():
            attend(pair)

    @pl.when(step == pairs - 1)
    def _():
        stats = jnp.concatenate([stat_ref[h] for h in range(heads)], axis=0)
        out_ref[heads * HEAD :, :] = stats.astype(jnp.bfloat16)


def band_part(earlier, *inputs, estimate):
    pairs = len(inputs) // 2
    payload = (2 * pairs * (HEAD + 8), STRIDE)
    whole = lambda shape: pl.BlockSpec(shape, lambda j: (0, 0))
    return pl.pallas_call(
        functools.partial(band_kernel, earlier, pairs),
        grid=(pairs,),
        in_specs=[whole(value.shape) for value in inputs],
        out_specs=whole(payload),
        scratch_shapes=[
            pltpu.VMEM((2 * pairs, 8, STRIDE), jnp.float32),
            pltpu.VMEM((BLOCK, BLOCK), jnp.float32),
        ],
        out_shape=(jax.ShapeDtypeStruct if earlier else pltpu.HBM)(payload, jnp.bfloat16),
        compiler_params=params(),
        cost_estimate=cost(estimate),
        name="band_earlier" if earlier else "band_local",
    )(*inputs)


def complete_kernel(flags_ref, q_ref, kv_ref, local_ref, earlier_ref, same_ref, cross_ref, bias_ref):
    core = flags_ref[0]
    has_earlier = flags_ref[1] > 0
    bias_ref[...] = band_bias(True)

    def stats(ref, heads, head, queries):
        rows = ref[heads * HEAD :, queries].astype(jnp.float32)[8 * head : 8 * head + 8]
        return rows[0:1] + rows[1:2] + rows[2:3], rows[3:4] + rows[4:5] + rows[5:6]

    def merge(part, head, out_e, top_e, scale_e, sum_e):
        queries = slice(part * BLOCK, (part + 1) * BLOCK)
        top_l, sum_l = stats(local_ref, 4, head, queries)
        top_e = jnp.where(has_earlier, top_e, NEG)
        top = jnp.maximum(top_l, top_e)
        weight_l = jnp.exp2((top_l - top) * SCALE2) * sum_l
        weight_e = jnp.where(has_earlier, jnp.exp2((top_e - top) * SCALE2), 0.0)
        inverse = 1.0 / (weight_l + weight_e * sum_e)
        out_l = local_ref[columns_of(head), queries].astype(jnp.float32)
        out = out_l * (weight_l * inverse) + out_e * (weight_e * scale_e * inverse)
        return out.T.astype(jnp.bfloat16)

    def finish(part, head, scores, biases, values):
        out, top, total = softmax_out(scores, biases, values)
        return merge(part, head, out, top, 1.0, total)

    results = band_jobs(True, 2, q_ref, kv_ref, bias_ref[...], finish)
    for part in range(STRIDE // BLOCK):
        queries = slice(part * BLOCK, (part + 1) * BLOCK)
        for head in range(2):
            top, total = stats(earlier_ref, 2, head, queries)
            out = earlier_ref[columns_of(head), queries].astype(jnp.float32)
            results[part, 2 + head] = merge(part, 2 + head, out, top, total, total)

    def store(ref, half):
        for part in range(2):
            for head in range(4):
                rows = slice(part * BLOCK, (part + 1) * BLOCK)
                ref[rows, columns_of(head)] = results[2 * half + part, head]

    @pl.when(core == 0)
    def _():
        store(same_ref, 0)
        store(cross_ref, 1)

    @pl.when(core == 1)
    def _():
        store(same_ref, 1)
        store(cross_ref, 0)


def complete(flags, query, keyval, local, earlier):
    inputs = [query, keyval, local, earlier]
    return pl.pallas_call(
        complete_kernel,
        grid_spec=pltpu.PrefetchScalarGridSpec(
            num_scalar_prefetch=1,
            grid=(1,),
            in_specs=[pl.BlockSpec(value.shape, lambda j, c: (0, 0)) for value in inputs],
            out_specs=[
                pl.BlockSpec((HALF, HALF), lambda j, c: (0, c[0])),
                pl.BlockSpec((HALF, HALF), lambda j, c: (0, 0)),
            ],
            scratch_shapes=[pltpu.VMEM((BLOCK, BLOCK), jnp.float32)],
        ),
        out_shape=[
            jax.ShapeDtypeStruct((HALF, 2 * HEADS * HEAD), jnp.bfloat16),
            jax.ShapeDtypeStruct((HALF, HALF), jnp.bfloat16),
        ],
        compiler_params=params(),
        cost_estimate=cost(COMPLETE_COST),
        name="complete",
    )(flags, *inputs)


def place_kernel(flags_ref, cross_ref, columns_ref, _, o_ref, sems):
    first = pl.multiple_of((1 - flags_ref[0]) * HALF, HALF)
    width = columns_ref.shape[1]
    copies = [
        pltpu.make_async_copy(cross_ref, o_ref.at[:, pl.ds(first, HALF)], sems.at[0]),
        pltpu.make_async_copy(columns_ref, o_ref.at[:, pl.ds(width, width)], sems.at[1]),
    ]
    for copy in copies:
        copy.start()
    for copy in copies:
        copy.wait()


def place(flags, cross, col_out, result):
    anywhere = pl.BlockSpec(memory_space=pl.ANY)
    return pl.pallas_call(
        place_kernel,
        grid_spec=pltpu.PrefetchScalarGridSpec(
            num_scalar_prefetch=1,
            grid=(1,),
            in_specs=[anywhere] * 3,
            out_specs=anywhere,
            scratch_shapes=[pltpu.SemaphoreType.DMA((2,))],
        ),
        out_shape=jax.ShapeDtypeStruct(result.shape, jnp.bfloat16),
        input_output_aliases={3: 0},
        compiler_params=params(),
        cost_estimate=cost(1),
        name="place",
    )(flags, cross, col_out, result)


def column_kernel(group, q_ref, k_ref, v_ref, o_ref, bias_ref):
    parts = HALF // BLOCK
    heads = q_ref.shape[1] // HEAD

    @pl.when(pl.program_id(0) == 0)
    def _():
        qpos = lax.broadcasted_iota(jnp.int32, (BLOCK, BLOCK), 0)
        kpos = lax.broadcasted_iota(jnp.int32, (BLOCK, BLOCK), 1)
        column = ((qpos - kpos) & (group - 1)) == 0
        bias_ref[0] = jnp.where(column, 0.0, NEG)
        bias_ref[1] = jnp.where(column & (kpos <= qpos), 0.0, NEG)

    def rows(block):
        return slice(block * BLOCK, (block + 1) * BLOCK)

    def start(part, head):
        query = q_ref[rows(part), columns_of(head)]
        return [
            lax.dot_general(
                query, k_ref[rows(block), columns_of(head)], (((1,), (1,)), ((), ())),
                preferred_element_type=jnp.float32,
            )
            for block in range(part + 1)
        ]

    def finish(part, head, scores):
        scores = [s + bias_ref[1 if block == part else 0] for block, s in enumerate(scores)]
        top = jnp.max(functools.reduce(jnp.maximum, scores), axis=1, keepdims=True)
        out = 0.0
        for block, s in enumerate(scores):
            values = v_ref[rows(block), columns_of(head)]
            values = jnp.concatenate([values, jnp.ones_like(values)], axis=1)
            expd = jnp.exp2((s - top) * SCALE2).astype(jnp.bfloat16)
            out = out + jnp.dot(expd, values, preferred_element_type=jnp.float32)
        out = out[:, :HEAD] * (1.0 / out[:, HEAD:])
        o_ref[rows(part), columns_of(head)] = out.astype(jnp.bfloat16)

    pipelined([(part, head) for part in range(parts) for head in range(heads)], 4, start, finish)


def column_attention(projected, group):
    rows = projected.shape[0]
    heads = 4
    steps = HEADS // heads
    spec = lambda third: pl.BlockSpec((rows, heads * HEAD), lambda j: (0, third * steps + j))
    return pl.pallas_call(
        functools.partial(column_kernel, group),
        grid=(steps,),
        in_specs=[spec(0), spec(1), spec(2)],
        out_specs=pl.BlockSpec((rows, heads * HEAD), lambda j: (0, j)),
        out_shape=jax.ShapeDtypeStruct((rows, HEADS * HEAD), jnp.bfloat16),
        scratch_shapes=[pltpu.VMEM((2, BLOCK, BLOCK), jnp.float32)],
        compiler_params=params(),
        cost_estimate=cost(6),
        name="column_attention",
    )(projected, projected, projected)


def in_hbm(value):
    return pltpu.with_memory_space_constraint(value, pltpu.HBM)


def after(value, *others):
    return lax.optimization_barrier((value,) + others)[0]


def on_device(tokens, w_row, w_column):
    count = lax.axis_size("seq")
    chips = count // 2
    rank = lax.axis_index("seq")
    core = (rank % 2).astype(jnp.int32)
    core_arr = core.reshape(1)
    flags = jnp.stack([core, (rank >= 2).astype(jnp.int32)])
    group = HALF // chips
    same_core = [list(range(0, count, 2)), list(range(1, count, 2))]

    def exchange(value):
        width = value.shape[1]
        value = lax.all_to_all(
            value.reshape(chips, group, width), "seq", split_axis=0, concat_axis=0,
            axis_index_groups=same_core, tiled=True,
        )
        return value.reshape(HALF, width)

    def swapped(value):
        return lax.ppermute(value, "seq", [(d, d ^ 1) for d in range(count)])

    def to_next(value):
        return lax.ppermute(value, "seq", [(d, d + 2) for d in range(count - 2)])

    w_row = in_hbm(w_row)
    columns = exchange(tokens)
    sibling = swapped(tokens)
    kv_a, kv_b, q_a, q_b = project(core_arr, tokens, sibling, w_row)
    previous_kv_a = to_next(kv_a)
    next_q_b = lax.ppermute(q_b, "seq", [(d, d - 2) for d in range(2, count)])
    local = band_part(False, q_a, kv_a, q_b, kv_b, estimate=LOCAL_COST)
    columns = after(columns, local)
    col_proj = jnp.dot(columns, w_column, preferred_element_type=jnp.float32).astype(jnp.bfloat16)
    sent_b = band_part(True, after(next_q_b, col_proj), kv_b, estimate=B_COST)
    earlier_b = to_next(sent_b)
    col_out = column_attention(after(col_proj, sent_b), group)
    result, cross = complete(flags, q_a, after(previous_kv_a, col_out), in_hbm(local), earlier_b)
    return place(flags, swapped(cross), exchange(col_out), result)


def solution(mesh):
    in_specs = (P("seq", None), P(), P())
    out_specs = P("seq", None)
    return jax.shard_map(
        on_device, mesh=mesh, in_specs=in_specs, out_specs=out_specs, check_vma=False
    )
```

```python
import functools
import math

import jax
import jax.numpy as jnp
from jax import lax
from jax.experimental import pallas as pl
from jax.experimental.pallas import tpu as pltpu
from jax.sharding import PartitionSpec as P

HEAD = 128
HEADS = 8
STRIDE = 1024
HALF = 512
BLOCK = 256
SCALE2 = math.log2(math.e) / math.sqrt(HEAD)
NEG = -1e30
VMEM_LIMIT = 28 << 20
PROJECT_COST, LOCAL_COST, B_COST, COMPLETE_COST = 0.5, 0.5, 0.5, 20


def params():
    return pltpu.CompilerParams(vmem_limit_bytes=VMEM_LIMIT)


def cost(us):
    return pl.CostEstimate(flops=int(us * 10**9), bytes_accessed=1 << 14, transcendentals=0)


def project_kernel(core_ref, own_ref, sibling_ref, w_ref, kv_a, kv_b, q_a, q_b):
    core = core_ref[0]
    for step, (kind, ref) in enumerate(PROJECT_ORDER):
        ref = {"kv_a": kv_a, "kv_b": kv_b, "q_a": q_a, "q_b": q_b}[ref]

        @pl.when(pl.program_id(0) == step)
        def _():
            for place, x_ref in ((core, own_ref), (1 - core, sibling_ref)):
                value = jnp.dot(x_ref[...], w_ref[...], preferred_element_type=jnp.float32)
                row = pl.multiple_of(place * HALF, HALF)
                if kind == 2:
                    value = value.T.astype(jnp.bfloat16)
                    for block in range(HALF // BLOCK):
                        rows = pl.ds(STRIDE + row + block * BLOCK, BLOCK)
                        ref[rows, :] = value[:, block * BLOCK : (block + 1) * BLOCK]
                else:
                    ref[pl.ds(row, HALF), :] = value.astype(jnp.bfloat16)


PROJECT_ORDER = [(1, "kv_a"), (2, "kv_a"), (0, "q_b"), (1, "kv_b"), (2, "kv_b"), (0, "q_a")]


def project(core, tokens, sibling, w_row):
    depth = tokens.shape[1]

    def weight_block(j, c):
        kind = lax.rem(j + 1, 3)
        pair = jnp.where((j >= 2) & (j <= 4), 1, 0)
        return (0, 4 * kind + 2 * c[0] + pair)

    whole = lambda rows, width: pl.BlockSpec((rows, width), lambda j, c: (0, 0))
    outs = [(2 * STRIDE, BLOCK), (2 * STRIDE, BLOCK), (STRIDE, BLOCK), (STRIDE, BLOCK)]
    return pl.pallas_call(
        project_kernel,
        grid_spec=pltpu.PrefetchScalarGridSpec(
            num_scalar_prefetch=1,
            grid=(len(PROJECT_ORDER),),
            in_specs=[
                whole(HALF, depth),
                whole(HALF, depth),
                pl.BlockSpec((depth, BLOCK), weight_block),
            ],
            out_specs=[whole(*shape) for shape in outs],
        ),
        out_shape=[jax.ShapeDtypeStruct(shape, jnp.bfloat16) for shape in outs],
        compiler_params=params(),
        cost_estimate=cost(PROJECT_COST),
        name="project",
    )(core, tokens, sibling, w_row)


def score_blocks(query, key_ref, columns, spans):
    return [
        lax.dot_general(
            key_ref[low:high, columns], query, (((1,), (1,)), ((), ())),
            preferred_element_type=jnp.float32,
        )
        for low, high in spans
    ]


def softmax_out(scores, biases, value_t_blocks):
    scores = [s if b is None else s + b for s, b in zip(scores, biases)]
    top = functools.reduce(jnp.maximum, [jnp.max(s, axis=0, keepdims=True) for s in scores])
    expd = [jnp.exp2((s - top) * SCALE2) for s in scores]
    total = sum(jnp.sum(e, axis=0, keepdims=True) for e in expd)
    out = sum(
        jnp.dot(v, e.astype(jnp.bfloat16), preferred_element_type=jnp.float32)
        for v, e in zip(value_t_blocks, expd)
    )
    return out, top, total


def pipelined(jobs, ahead, start, finish):
    pending, results = [], {}
    for job in jobs:
        pending.append((job, start(*job)))
        if len(pending) > ahead:
            first, value = pending.pop(0)
            results[first] = finish(*first, value)
    for first, value in pending:
        results[first] = finish(*first, value)
    return results


def split3(value):
    high = value.astype(jnp.bfloat16).astype(jnp.float32)
    rest = value - high
    mid = rest.astype(jnp.bfloat16).astype(jnp.float32)
    return [high, mid, rest - mid]


def columns_of(head):
    return slice(head * HEAD, (head + 1) * HEAD)


def band_jobs(earlier, ahead, q_ref, kv_ref, bias, finish):
    def spans(part):
        low, high = part * BLOCK, (part + 1) * BLOCK
        rest = (high, STRIDE) if earlier else (0, low)
        return [(low, high)] + ([rest] if rest[0] < rest[1] else [])

    def values_t(head, low, high):
        rows = lambda at: slice(STRIDE + at + head * HEAD, STRIDE + at + (head + 1) * HEAD)
        return jnp.concatenate([kv_ref[rows(at), :] for at in range(low, high, BLOCK)], axis=1)

    def start(part, head):
        query = q_ref[part * BLOCK : (part + 1) * BLOCK, columns_of(head)]
        return score_blocks(query, kv_ref, columns_of(head), spans(part))

    def end(part, head, scores):
        values = [values_t(head, low, high) for low, high in spans(part)]
        return finish(part, head, scores, [bias, None], values)

    jobs = [(part, head) for part in range(STRIDE // BLOCK) for head in range(2)]
    return pipelined(jobs, ahead, start, end)


def band_bias(earlier):
    kpos = lax.broadcasted_iota(jnp.int32, (BLOCK, BLOCK), 0)
    qpos = lax.broadcasted_iota(jnp.int32, (BLOCK, BLOCK), 1)
    return jnp.where(kpos > qpos if earlier else kpos <= qpos, 0.0, NEG)


def band_kernel(earlier, pairs, *refs):
    inputs, (out_ref, stat_ref, bias_ref) = refs[: 2 * pairs], refs[2 * pairs :]
    step = pl.program_id(0)
    heads = 2 * pairs

    @pl.when(step == 0)
    def _():
        bias_ref[...] = band_bias(earlier)

    def attend(pair):
        def finish(part, head, scores, biases, values):
            out, top, total = softmax_out(scores, biases, values)
            queries = slice(part * BLOCK, (part + 1) * BLOCK)
            row = (2 * pair + head) * HEAD
            out = out * (1.0 / total)
            out_ref[row : row + HEAD, queries] = out.astype(jnp.bfloat16)
            stat_ref[2 * pair + head, :, queries] = jnp.concatenate(
                split3(top) + split3(total) + [jnp.zeros((2, BLOCK), jnp.float32)], axis=0
            )

        ahead = 2 if earlier else 4
        band_jobs(earlier, ahead, *inputs[2 * pair : 2 * pair + 2], bias_ref[...], finish)

    for pair in range(pairs):

        @pl.when(step == pair)
        def _():
            attend(pair)

    @pl.when(step == pairs - 1)
    def _():
        stats = jnp.concatenate([stat_ref[h] for h in range(heads)], axis=0)
        out_ref[heads * HEAD :, :] = stats.astype(jnp.bfloat16)


def band_part(earlier, *inputs, estimate):
    pairs = len(inputs) // 2
    payload = (2 * pairs * (HEAD + 8), STRIDE)
    whole = lambda shape: pl.BlockSpec(shape, lambda j: (0, 0))
    return pl.pallas_call(
        functools.partial(band_kernel, earlier, pairs),
        grid=(pairs,),
        in_specs=[whole(value.shape) for value in inputs],
        out_specs=whole(payload),
        scratch_shapes=[
            pltpu.VMEM((2 * pairs, 8, STRIDE), jnp.float32),
            pltpu.VMEM((BLOCK, BLOCK), jnp.float32),
        ],
        out_shape=(jax.ShapeDtypeStruct if earlier else pltpu.HBM)(payload, jnp.bfloat16),
        compiler_params=params(),
        cost_estimate=cost(estimate),
        name="band_earlier" if earlier else "band_local",
    )(*inputs)


def complete_kernel(flags_ref, q_ref, kv_ref, local_ref, earlier_ref, same_ref, cross_ref, bias_ref):
    core = flags_ref[0]
    has_earlier = flags_ref[1] > 0
    bias_ref[...] = band_bias(True)

    def stats(ref, heads, head, queries):
        rows = ref[heads * HEAD :, queries].astype(jnp.float32)[8 * head : 8 * head + 8]
        return rows[0:1] + rows[1:2] + rows[2:3], rows[3:4] + rows[4:5] + rows[5:6]

    def merge(part, head, out_e, top_e, scale_e, sum_e):
        queries = slice(part * BLOCK, (part + 1) * BLOCK)
        top_l, sum_l = stats(local_ref, 4, head, queries)
        top_e = jnp.where(has_earlier, top_e, NEG)
        top = jnp.maximum(top_l, top_e)
        weight_l = jnp.exp2((top_l - top) * SCALE2) * sum_l
        weight_e = jnp.where(has_earlier, jnp.exp2((top_e - top) * SCALE2), 0.0)
        inverse = 1.0 / (weight_l + weight_e * sum_e)
        out_l = local_ref[columns_of(head), queries].astype(jnp.float32)
        out = out_l * (weight_l * inverse) + out_e * (weight_e * scale_e * inverse)
        return out.T.astype(jnp.bfloat16)

    def finish(part, head, scores, biases, values):
        out, top, total = softmax_out(scores, biases, values)
        return merge(part, head, out, top, 1.0, total)

    results = band_jobs(True, 2, q_ref, kv_ref, bias_ref[...], finish)
    for part in range(STRIDE // BLOCK):
        queries = slice(part * BLOCK, (part + 1) * BLOCK)
        for head in range(2):
            top, total = stats(earlier_ref, 2, head, queries)
            out = earlier_ref[columns_of(head), queries].astype(jnp.float32)
            results[part, 2 + head] = merge(part, 2 + head, out, top, total, total)

    def store(ref, half):
        for part in range(2):
            for head in range(4):
                rows = slice(part * BLOCK, (part + 1) * BLOCK)
                ref[rows, columns_of(head)] = results[2 * half + part, head]

    @pl.when(core == 0)
    def _():
        store(same_ref, 0)
        store(cross_ref, 1)

    @pl.when(core == 1)
    def _():
        store(same_ref, 1)
        store(cross_ref, 0)


def complete(flags, query, keyval, local, earlier):
    inputs = [query, keyval, local, earlier]
    return pl.pallas_call(
        complete_kernel,
        grid_spec=pltpu.PrefetchScalarGridSpec(
            num_scalar_prefetch=1,
            grid=(1,),
            in_specs=[pl.BlockSpec(value.shape, lambda j, c: (0, 0)) for value in inputs],
            out_specs=[
                pl.BlockSpec((HALF, HALF), lambda j, c: (0, c[0])),
                pl.BlockSpec((HALF, HALF), lambda j, c: (0, 0)),
            ],
            scratch_shapes=[pltpu.VMEM((BLOCK, BLOCK), jnp.float32)],
        ),
        out_shape=[
            jax.ShapeDtypeStruct((HALF, 2 * HEADS * HEAD), jnp.bfloat16),
            jax.ShapeDtypeStruct((HALF, HALF), jnp.bfloat16),
        ],
        compiler_params=params(),
        cost_estimate=cost(COMPLETE_COST),
        name="complete",
    )(flags, *inputs)


def place_kernel(flags_ref, cross_ref, columns_ref, _, o_ref, sems):
    first = pl.multiple_of((1 - flags_ref[0]) * HALF, HALF)
    width = columns_ref.shape[1]
    copies = [
        pltpu.make_async_copy(cross_ref, o_ref.at[:, pl.ds(first, HALF)], sems.at[0]),
        pltpu.make_async_copy(columns_ref, o_ref.at[:, pl.ds(width, width)], sems.at[1]),
    ]
    for copy in copies:
        copy.start()
    for copy in copies:
        copy.wait()


def place(flags, cross, col_out, result):
    anywhere = pl.BlockSpec(memory_space=pl.ANY)
    return pl.pallas_call(
        place_kernel,
        grid_spec=pltpu.PrefetchScalarGridSpec(
            num_scalar_prefetch=1,
            grid=(1,),
            in_specs=[anywhere] * 3,
            out_specs=anywhere,
            scratch_shapes=[pltpu.SemaphoreType.DMA((2,))],
        ),
        out_shape=jax.ShapeDtypeStruct(result.shape, jnp.bfloat16),
        input_output_aliases={3: 0},
        compiler_params=params(),
        cost_estimate=cost(1),
        name="place",
    )(flags, cross, col_out, result)


def column_kernel(group, x_hbm, w_hbm, o_ref, x_ref, w_ref, bias_ref, sems, *projected):
    parts = HALF // BLOCK
    heads = HEADS // 2
    width = heads * HEAD
    load_x = pltpu.make_async_copy(x_hbm, x_ref, sems.at[6])
    load_x.start()
    loads = []
    for index in range(6):
        half, third = divmod(index, 3)
        first = third * HEADS * HEAD + half * width
        load = pltpu.make_async_copy(
            w_hbm.at[:, first : first + width], w_ref.at[index], sems.at[index]
        )
        load.start()
        loads.append(load)

    qpos = lax.broadcasted_iota(jnp.int32, (BLOCK, BLOCK), 0)
    kpos = lax.broadcasted_iota(jnp.int32, (BLOCK, BLOCK), 1)
    column = ((qpos - kpos) & (group - 1)) == 0
    bias_ref[0] = jnp.where(column, 0.0, NEG)
    bias_ref[1] = jnp.where(column & (kpos <= qpos), 0.0, NEG)

    def rows(block):
        return slice(block * BLOCK, (block + 1) * BLOCK)

    def attend(q_ref, k_ref, v_ref, first):
        def start(part, head):
            query = q_ref[rows(part), columns_of(head)]
            return [
                lax.dot_general(
                    query, k_ref[rows(block), columns_of(head)], (((1,), (1,)), ((), ())),
                    preferred_element_type=jnp.float32,
                )
                for block in range(part + 1)
            ]

        def finish(part, head, scores):
            scores = [s + bias_ref[1 if block == part else 0] for block, s in enumerate(scores)]
            top = jnp.max(functools.reduce(jnp.maximum, scores), axis=1, keepdims=True)
            out = 0.0
            for block, s in enumerate(scores):
                values = v_ref[rows(block), columns_of(head)]
                values = jnp.concatenate([values, jnp.ones_like(values)], axis=1)
                expd = jnp.exp2((s - top) * SCALE2).astype(jnp.bfloat16)
                out = out + jnp.dot(expd, values, preferred_element_type=jnp.float32)
            out = out[:, :HEAD] * (1.0 / out[:, HEAD:])
            o_ref[rows(part), columns_of(first + head)] = out.astype(jnp.bfloat16)

        jobs = [(part, head) for part in range(parts) for head in range(heads)]
        pipelined(jobs, 4, start, finish)

    load_x.wait()
    for index, load in enumerate(loads):
        load.wait()
        value = jnp.dot(x_ref[...], w_ref[index], preferred_element_type=jnp.float32)
        projected[index][...] = value.astype(jnp.bfloat16)
        if index == 2:
            attend(*projected[:3], 0)
    attend(*projected[3:], heads)


def column_attention(x, w_column, group):
    rows, depth = x.shape
    width = HEADS // 2 * HEAD
    far = pl.BlockSpec(memory_space=pltpu.HBM)
    return pl.pallas_call(
        functools.partial(column_kernel, group),
        in_specs=[far, far],
        out_specs=pl.BlockSpec(memory_space=pltpu.VMEM),
        out_shape=jax.ShapeDtypeStruct((rows, HEADS * HEAD), jnp.bfloat16),
        scratch_shapes=[
            pltpu.VMEM((rows, depth), jnp.bfloat16),
            pltpu.VMEM((6, depth, width), jnp.bfloat16),
            pltpu.VMEM((2, BLOCK, BLOCK), jnp.float32),
            pltpu.SemaphoreType.DMA((7,)),
        ]
        + [pltpu.VMEM((rows, width), jnp.bfloat16)] * 6,
        compiler_params=pltpu.CompilerParams(vmem_limit_bytes=44 << 20),
        cost_estimate=cost(13),
        name="column_attention",
    )(in_hbm(x), in_hbm(w_column))


def in_hbm(value):
    return pltpu.with_memory_space_constraint(value, pltpu.HBM)


def after(value, *others):
    return lax.optimization_barrier((value,) + others)[0]


def on_device(tokens, w_row, w_column):
    count = lax.axis_size("seq")
    chips = count // 2
    rank = lax.axis_index("seq")
    core = (rank % 2).astype(jnp.int32)
    core_arr = core.reshape(1)
    flags = jnp.stack([core, (rank >= 2).astype(jnp.int32)])
    group = HALF // chips
    same_core = [list(range(0, count, 2)), list(range(1, count, 2))]

    def exchange(value):
        width = value.shape[1]
        value = lax.all_to_all(
            value.reshape(chips, group, width), "seq", split_axis=0, concat_axis=0,
            axis_index_groups=same_core, tiled=True,
        )
        return value.reshape(HALF, width)

    def swapped(value):
        return lax.ppermute(value, "seq", [(d, d ^ 1) for d in range(count)])

    def to_next(value):
        return lax.ppermute(value, "seq", [(d, d + 2) for d in range(count - 2)])

    w_row = in_hbm(w_row)
    columns = exchange(tokens)
    sibling = swapped(tokens)
    kv_a, kv_b, q_a, q_b = project(core_arr, tokens, sibling, w_row)
    previous_kv_a = to_next(kv_a)
    next_q_b = lax.ppermute(q_b, "seq", [(d, d - 2) for d in range(2, count)])
    local = band_part(False, q_a, kv_a, q_b, kv_b, estimate=LOCAL_COST)
    columns = after(columns, local)
    col_out = column_attention(columns, w_column, group)
    sent_b = band_part(True, after(next_q_b, col_out), kv_b, estimate=B_COST)
    earlier_b = to_next(sent_b)
    result, cross = complete(flags, q_a, after(previous_kv_a, col_out), in_hbm(local), earlier_b)
    return place(flags, swapped(cross), exchange(after(col_out, sent_b)), result)


def solution(mesh):
    in_specs = (P("seq", None), P(), P())
    out_specs = P("seq", None)
    return jax.shard_map(
        on_device, mesh=mesh, in_specs=in_specs, out_specs=out_specs, check_vma=False
    )
```

```python
import functools
import math

import jax
import jax.numpy as jnp
from jax import lax
from jax.experimental import pallas as pl
from jax.experimental.pallas import tpu as pltpu
from jax.sharding import PartitionSpec as P

HEAD = 128
HEADS = 8
STRIDE = 1024
HALF = 512
BLOCK = 256
SCALE2 = math.log2(math.e) / math.sqrt(HEAD)
NEG = -1e30
VMEM_LIMIT = 28 << 20
PROJECT_COST, LOCAL_COST, B_COST, COMPLETE_COST = 0.5, 0.5, 0.5, 20


def params():
    return pltpu.CompilerParams(vmem_limit_bytes=VMEM_LIMIT)


def cost(us):
    return pl.CostEstimate(flops=int(us * 10**9), bytes_accessed=1 << 14, transcendentals=0)


def project_kernel(core_ref, own_ref, sibling_ref, w_ref, kv_a, kv_b, q_a, q_b):
    core = core_ref[0]
    for step, (kind, ref) in enumerate(PROJECT_ORDER):
        ref = {"kv_a": kv_a, "kv_b": kv_b, "q_a": q_a, "q_b": q_b}[ref]

        @pl.when(pl.program_id(0) == step)
        def _():
            for place, x_ref in ((core, own_ref), (1 - core, sibling_ref)):
                value = jnp.dot(x_ref[...], w_ref[...], preferred_element_type=jnp.float32)
                row = pl.multiple_of(place * HALF, HALF)
                if kind == 2:
                    value = value.T.astype(jnp.bfloat16)
                    for block in range(HALF // BLOCK):
                        rows = pl.ds(STRIDE + row + block * BLOCK, BLOCK)
                        ref[rows, :] = value[:, block * BLOCK : (block + 1) * BLOCK]
                else:
                    ref[pl.ds(row, HALF), :] = value.astype(jnp.bfloat16)


PROJECT_ORDER = [(1, "kv_a"), (2, "kv_a"), (0, "q_b"), (1, "kv_b"), (2, "kv_b"), (0, "q_a")]


def project(core, tokens, sibling, w_row):
    depth = tokens.shape[1]

    def weight_block(j, c):
        kind = lax.rem(j + 1, 3)
        pair = jnp.where((j >= 2) & (j <= 4), 1, 0)
        return (0, 4 * kind + 2 * c[0] + pair)

    whole = lambda rows, width: pl.BlockSpec((rows, width), lambda j, c: (0, 0))
    outs = [(2 * STRIDE, BLOCK), (2 * STRIDE, BLOCK), (STRIDE, BLOCK), (STRIDE, BLOCK)]
    return pl.pallas_call(
        project_kernel,
        grid_spec=pltpu.PrefetchScalarGridSpec(
            num_scalar_prefetch=1,
            grid=(len(PROJECT_ORDER),),
            in_specs=[
                whole(HALF, depth),
                whole(HALF, depth),
                pl.BlockSpec((depth, BLOCK), weight_block),
            ],
            out_specs=[whole(*shape) for shape in outs],
        ),
        out_shape=[jax.ShapeDtypeStruct(shape, jnp.bfloat16) for shape in outs],
        compiler_params=params(),
        cost_estimate=cost(PROJECT_COST),
        name="project",
    )(core, tokens, sibling, w_row)


def score_blocks(query, key_ref, columns, spans):
    return [
        lax.dot_general(
            key_ref[low:high, columns], query, (((1,), (1,)), ((), ())),
            preferred_element_type=jnp.float32,
        )
        for low, high in spans
    ]


def softmax_out(scores, biases, value_t_blocks):
    scores = [s if b is None else s + b for s, b in zip(scores, biases)]
    top = functools.reduce(jnp.maximum, [jnp.max(s, axis=0, keepdims=True) for s in scores])
    expd = [jnp.exp2((s - top) * SCALE2) for s in scores]
    total = sum(jnp.sum(e, axis=0, keepdims=True) for e in expd)
    out = sum(
        jnp.dot(v, e.astype(jnp.bfloat16), preferred_element_type=jnp.float32)
        for v, e in zip(value_t_blocks, expd)
    )
    return out, top, total


def pipelined(jobs, ahead, start, finish):
    pending, results = [], {}
    for job in jobs:
        pending.append((job, start(*job)))
        if len(pending) > ahead:
            first, value = pending.pop(0)
            results[first] = finish(*first, value)
    for first, value in pending:
        results[first] = finish(*first, value)
    return results


def split3(value):
    high = value.astype(jnp.bfloat16).astype(jnp.float32)
    rest = value - high
    mid = rest.astype(jnp.bfloat16).astype(jnp.float32)
    return [high, mid, rest - mid]


def columns_of(head):
    return slice(head * HEAD, (head + 1) * HEAD)


def band_jobs(earlier, ahead, q_ref, kv_ref, bias, finish):
    def spans(part):
        low, high = part * BLOCK, (part + 1) * BLOCK
        rest = (high, STRIDE) if earlier else (0, low)
        return [(low, high)] + ([rest] if rest[0] < rest[1] else [])

    def values_t(head, low, high):
        rows = lambda at: slice(STRIDE + at + head * HEAD, STRIDE + at + (head + 1) * HEAD)
        return jnp.concatenate([kv_ref[rows(at), :] for at in range(low, high, BLOCK)], axis=1)

    def start(part, head):
        query = q_ref[part * BLOCK : (part + 1) * BLOCK, columns_of(head)]
        return score_blocks(query, kv_ref, columns_of(head), spans(part))

    def end(part, head, scores):
        values = [values_t(head, low, high) for low, high in spans(part)]
        return finish(part, head, scores, [bias, None], values)

    jobs = [(part, head) for part in range(STRIDE // BLOCK) for head in range(2)]
    return pipelined(jobs, ahead, start, end)


def band_bias(earlier):
    kpos = lax.broadcasted_iota(jnp.int32, (BLOCK, BLOCK), 0)
    qpos = lax.broadcasted_iota(jnp.int32, (BLOCK, BLOCK), 1)
    return jnp.where(kpos > qpos if earlier else kpos <= qpos, 0.0, NEG)


def band_kernel(earlier, pairs, *refs):
    inputs, (out_ref, stat_ref, bias_ref) = refs[: 2 * pairs], refs[2 * pairs :]
    step = pl.program_id(0)
    heads = 2 * pairs

    @pl.when(step == 0)
    def _():
        bias_ref[...] = band_bias(earlier)

    def attend(pair):
        def finish(part, head, scores, biases, values):
            out, top, total = softmax_out(scores, biases, values)
            queries = slice(part * BLOCK, (part + 1) * BLOCK)
            row = (2 * pair + head) * HEAD
            out = out * (1.0 / total)
            out_ref[row : row + HEAD, queries] = out.astype(jnp.bfloat16)
            stat_ref[2 * pair + head, :, queries] = jnp.concatenate(
                split3(top) + split3(total) + [jnp.zeros((2, BLOCK), jnp.float32)], axis=0
            )

        ahead = 2 if earlier else 4
        band_jobs(earlier, ahead, *inputs[2 * pair : 2 * pair + 2], bias_ref[...], finish)

    for pair in range(pairs):

        @pl.when(step == pair)
        def _():
            attend(pair)

    @pl.when(step == pairs - 1)
    def _():
        stats = jnp.concatenate([stat_ref[h] for h in range(heads)], axis=0)
        out_ref[heads * HEAD :, :] = stats.astype(jnp.bfloat16)


def band_part(earlier, *inputs, estimate):
    pairs = len(inputs) // 2
    payload = (2 * pairs * (HEAD + 8), STRIDE)
    whole = lambda shape: pl.BlockSpec(shape, lambda j: (0, 0))
    return pl.pallas_call(
        functools.partial(band_kernel, earlier, pairs),
        grid=(pairs,),
        in_specs=[whole(value.shape) for value in inputs],
        out_specs=whole(payload),
        scratch_shapes=[
            pltpu.VMEM((2 * pairs, 8, STRIDE), jnp.float32),
            pltpu.VMEM((BLOCK, BLOCK), jnp.float32),
        ],
        out_shape=(jax.ShapeDtypeStruct if earlier else pltpu.HBM)(payload, jnp.bfloat16),
        compiler_params=params(),
        cost_estimate=cost(estimate),
        name="band_earlier" if earlier else "band_local",
    )(*inputs)


def complete_kernel(flags_ref, q_ref, kv_ref, local_ref, earlier_ref, same_ref, cross_ref, bias_ref):
    core = flags_ref[0]
    has_earlier = flags_ref[1] > 0
    bias_ref[...] = band_bias(True)

    def stats(ref, heads, head, queries):
        rows = ref[heads * HEAD :, queries].astype(jnp.float32)[8 * head : 8 * head + 8]
        return rows[0:1] + rows[1:2] + rows[2:3], rows[3:4] + rows[4:5] + rows[5:6]

    def merge(part, head, out_e, top_e, scale_e, sum_e):
        queries = slice(part * BLOCK, (part + 1) * BLOCK)
        top_l, sum_l = stats(local_ref, 4, head, queries)
        top_e = jnp.where(has_earlier, top_e, NEG)
        top = jnp.maximum(top_l, top_e)
        weight_l = jnp.exp2((top_l - top) * SCALE2) * sum_l
        weight_e = jnp.where(has_earlier, jnp.exp2((top_e - top) * SCALE2), 0.0)
        inverse = 1.0 / (weight_l + weight_e * sum_e)
        out_l = local_ref[columns_of(head), queries].astype(jnp.float32)
        out = out_l * (weight_l * inverse) + out_e * (weight_e * scale_e * inverse)
        return out.T.astype(jnp.bfloat16)

    def finish(part, head, scores, biases, values):
        out, top, total = softmax_out(scores, biases, values)
        return merge(part, head, out, top, 1.0, total)

    results = band_jobs(True, 2, q_ref, kv_ref, bias_ref[...], finish)
    for part in range(STRIDE // BLOCK):
        queries = slice(part * BLOCK, (part + 1) * BLOCK)
        for head in range(2):
            top, total = stats(earlier_ref, 2, head, queries)
            out = earlier_ref[columns_of(head), queries].astype(jnp.float32)
            results[part, 2 + head] = merge(part, 2 + head, out, top, total, total)

    def store(ref, half):
        for part in range(2):
            for head in range(4):
                rows = slice(part * BLOCK, (part + 1) * BLOCK)
                ref[rows, columns_of(head)] = results[2 * half + part, head]

    @pl.when(core == 0)
    def _():
        store(same_ref, 0)
        store(cross_ref, 1)

    @pl.when(core == 1)
    def _():
        store(same_ref, 1)
        store(cross_ref, 0)


def complete(flags, query, keyval, local, earlier):
    inputs = [query, keyval, local, earlier]
    return pl.pallas_call(
        complete_kernel,
        grid_spec=pltpu.PrefetchScalarGridSpec(
            num_scalar_prefetch=1,
            grid=(1,),
            in_specs=[pl.BlockSpec(value.shape, lambda j, c: (0, 0)) for value in inputs],
            out_specs=[
                pl.BlockSpec((HALF, HALF), lambda j, c: (0, c[0])),
                pl.BlockSpec((HALF, HALF), lambda j, c: (0, 0)),
            ],
            scratch_shapes=[pltpu.VMEM((BLOCK, BLOCK), jnp.float32)],
        ),
        out_shape=[
            jax.ShapeDtypeStruct((HALF, 2 * HEADS * HEAD), jnp.bfloat16),
            jax.ShapeDtypeStruct((HALF, HALF), jnp.bfloat16),
        ],
        compiler_params=params(),
        cost_estimate=cost(COMPLETE_COST),
        name="complete",
    )(flags, *inputs)


def place_kernel(flags_ref, cross_ref, columns_ref, _, o_ref, sems):
    first = pl.multiple_of((1 - flags_ref[0]) * HALF, HALF)
    width = columns_ref.shape[1]
    copies = [
        pltpu.make_async_copy(cross_ref, o_ref.at[:, pl.ds(first, HALF)], sems.at[0]),
        pltpu.make_async_copy(columns_ref, o_ref.at[:, pl.ds(width, width)], sems.at[1]),
    ]
    for copy in copies:
        copy.start()
    for copy in copies:
        copy.wait()


def place(flags, cross, col_out, result):
    anywhere = pl.BlockSpec(memory_space=pl.ANY)
    return pl.pallas_call(
        place_kernel,
        grid_spec=pltpu.PrefetchScalarGridSpec(
            num_scalar_prefetch=1,
            grid=(1,),
            in_specs=[anywhere] * 3,
            out_specs=anywhere,
            scratch_shapes=[pltpu.SemaphoreType.DMA((2,))],
        ),
        out_shape=jax.ShapeDtypeStruct(result.shape, jnp.bfloat16),
        input_output_aliases={3: 0},
        compiler_params=params(),
        cost_estimate=cost(1),
        name="place",
    )(flags, cross, col_out, result)


def column_bias(group, bias_ref):
    qpos = lax.broadcasted_iota(jnp.int32, (BLOCK, BLOCK), 0)
    kpos = lax.broadcasted_iota(jnp.int32, (BLOCK, BLOCK), 1)
    column = ((qpos - kpos) & (group - 1)) == 0
    bias_ref[0] = jnp.where(column, 0.0, NEG)
    bias_ref[1] = jnp.where(column & (kpos <= qpos), 0.0, NEG)


def column_attend(q_ref, k_ref, v_ref, bias_ref, o_ref):
    def rows(block):
        return slice(block * BLOCK, (block + 1) * BLOCK)

    def start(part, head):
        query = q_ref[rows(part), columns_of(head)]
        return [
            lax.dot_general(
                query, k_ref[rows(block), columns_of(head)], (((1,), (1,)), ((), ())),
                preferred_element_type=jnp.float32,
            )
            for block in range(part + 1)
        ]

    def finish(part, head, scores):
        scores = [s + bias_ref[1 if block == part else 0] for block, s in enumerate(scores)]
        top = jnp.max(functools.reduce(jnp.maximum, scores), axis=1, keepdims=True)
        out = 0.0
        for block, s in enumerate(scores):
            values = v_ref[rows(block), columns_of(head)]
            values = jnp.concatenate([values, jnp.ones_like(values)], axis=1)
            expd = jnp.exp2((s - top) * SCALE2).astype(jnp.bfloat16)
            out = out + jnp.dot(expd, values, preferred_element_type=jnp.float32)
        out = out[:, :HEAD] * (1.0 / out[:, HEAD:])
        o_ref[rows(part), columns_of(head)] = out.astype(jnp.bfloat16)

    jobs = [(part, head) for part in range(HALF // BLOCK) for head in range(HEADS // 2)]
    pipelined(jobs, 4, start, finish)


def column_kernel(
    group, x_hbm, w_hbm, o_ref, q_ref, k_ref, v_ref, x_ref, w_ref, bias_ref, sems, *projected
):
    width = HEADS // 2 * HEAD
    load_x = pltpu.make_async_copy(x_hbm, x_ref, sems.at[6])
    load_x.start()
    loads = []
    for index in range(6):
        half, third = divmod(index, 3)
        first = third * HEADS * HEAD + half * width
        load = pltpu.make_async_copy(
            w_hbm.at[:, first : first + width], w_ref.at[index], sems.at[index]
        )
        load.start()
        loads.append(load)
    column_bias(group, bias_ref)
    load_x.wait()
    for load, ref, block in zip(loads, projected + (q_ref, k_ref, v_ref), range(6)):
        load.wait()
        value = jnp.dot(x_ref[...], w_ref[block], preferred_element_type=jnp.float32)
        ref[...] = value.astype(jnp.bfloat16)
    column_attend(*projected, bias_ref, o_ref)


def column_first(x, w_column, group):
    rows, depth = x.shape
    width = HEADS // 2 * HEAD
    far = pl.BlockSpec(memory_space=pltpu.HBM)
    half = pl.BlockSpec((rows, width), lambda j: (0, 0))
    part = jax.ShapeDtypeStruct((rows, width), jnp.bfloat16)
    return pl.pallas_call(
        functools.partial(column_kernel, group),
        grid=(1,),
        in_specs=[far, far],
        out_specs=[half] * 4,
        out_shape=[jax.ShapeDtypeStruct((rows, HEADS * HEAD), jnp.bfloat16)] + [part] * 3,
        scratch_shapes=[
            pltpu.VMEM((rows, depth), jnp.bfloat16),
            pltpu.VMEM((6, depth, width), jnp.bfloat16),
            pltpu.VMEM((2, BLOCK, BLOCK), jnp.float32),
            pltpu.SemaphoreType.DMA((7,)),
        ]
        + [pltpu.VMEM((rows, width), jnp.bfloat16)] * 3,
        compiler_params=pltpu.CompilerParams(vmem_limit_bytes=44 << 20),
        cost_estimate=cost(11),
        name="column_first",
    )(in_hbm(x), in_hbm(w_column))


def column_rest_kernel(group, q_ref, k_ref, v_ref, _, o_ref, bias_ref):
    column_bias(group, bias_ref)
    column_attend(q_ref, k_ref, v_ref, bias_ref, o_ref)


def column_rest(query, keys, values, first, group):
    rows, width = query.shape
    whole = pl.BlockSpec((rows, width), lambda j: (0, 0))
    return pl.pallas_call(
        functools.partial(column_rest_kernel, group),
        grid=(1,),
        in_specs=[whole] * 3 + [pl.BlockSpec(memory_space=pl.ANY)],
        out_specs=pl.BlockSpec((rows, width), lambda j: (0, 1)),
        out_shape=jax.ShapeDtypeStruct(first.shape, jnp.bfloat16),
        input_output_aliases={3: 0},
        scratch_shapes=[pltpu.VMEM((2, BLOCK, BLOCK), jnp.float32)],
        compiler_params=params(),
        cost_estimate=cost(6),
        name="column_rest",
    )(query, keys, values, first)


def in_hbm(value):
    return pltpu.with_memory_space_constraint(value, pltpu.HBM)


def after(value, *others):
    return lax.optimization_barrier((value,) + others)[0]


def on_device(tokens, w_row, w_column):
    count = lax.axis_size("seq")
    chips = count // 2
    rank = lax.axis_index("seq")
    core = (rank % 2).astype(jnp.int32)
    core_arr = core.reshape(1)
    flags = jnp.stack([core, (rank >= 2).astype(jnp.int32)])
    group = HALF // chips
    same_core = [list(range(0, count, 2)), list(range(1, count, 2))]

    def exchange(value):
        width = value.shape[1]
        value = lax.all_to_all(
            value.reshape(chips, group, width), "seq", split_axis=0, concat_axis=0,
            axis_index_groups=same_core, tiled=True,
        )
        return value.reshape(HALF, width)

    def swapped(value):
        return lax.ppermute(value, "seq", [(d, d ^ 1) for d in range(count)])

    def to_next(value):
        return lax.ppermute(value, "seq", [(d, d + 2) for d in range(count - 2)])

    w_row = in_hbm(w_row)
    columns = exchange(tokens)
    sibling = swapped(tokens)
    kv_a, kv_b, q_a, q_b = project(core_arr, tokens, sibling, w_row)
    previous_kv_a = to_next(kv_a)
    next_q_b = lax.ppermute(q_b, "seq", [(d, d - 2) for d in range(2, count)])
    local = band_part(False, q_a, kv_a, q_b, kv_b, estimate=LOCAL_COST)
    columns = after(columns, local)
    col_first, *projected = column_first(columns, w_column, group)
    sent_b = band_part(True, after(next_q_b, col_first), kv_b, estimate=B_COST)
    earlier_b = to_next(sent_b)
    col_out = column_rest(after(projected[0], sent_b), *projected[1:], col_first, group)
    result, cross = complete(flags, q_a, after(previous_kv_a, col_out), in_hbm(local), earlier_b)
    return place(flags, swapped(cross), exchange(col_out), result)


def solution(mesh):
    in_specs = (P("seq", None), P(), P())
    out_specs = P("seq", None)
    return jax.shard_map(
        on_device, mesh=mesh, in_specs=in_specs, out_specs=out_specs, check_vma=False
    )
```

```python
import functools
import math

import jax
import jax.numpy as jnp
from jax import lax
from jax.experimental import pallas as pl
from jax.experimental.pallas import tpu as pltpu
from jax.sharding import PartitionSpec as P

HEAD = 128
HEADS = 8
STRIDE = 1024
HALF = 512
BLOCK = 256
SCALE2 = math.log2(math.e) / math.sqrt(HEAD)
NEG = -1e30
VMEM_LIMIT = 28 << 20
PROJECT_COST, LOCAL_COST, B_COST, COMPLETE_COST = 0.5, 0.5, 0.5, 20


def params():
    return pltpu.CompilerParams(vmem_limit_bytes=VMEM_LIMIT)


def cost(us):
    return pl.CostEstimate(flops=int(us * 10**9), bytes_accessed=1 << 14, transcendentals=0)


def project_kernel(core_ref, own_ref, sibling_ref, w_ref, kv_a, kv_b, q_a, q_b):
    core = core_ref[0]
    for step, (kind, ref) in enumerate(PROJECT_ORDER):
        ref = {"kv_a": kv_a, "kv_b": kv_b, "q_a": q_a, "q_b": q_b}[ref]

        @pl.when(pl.program_id(0) == step)
        def _():
            for place, x_ref in ((core, own_ref), (1 - core, sibling_ref)):
                value = jnp.dot(x_ref[...], w_ref[...], preferred_element_type=jnp.float32)
                row = pl.multiple_of(place * HALF, HALF)
                if kind == 2:
                    value = value.T.astype(jnp.bfloat16)
                    for block in range(HALF // BLOCK):
                        rows = pl.ds(STRIDE + row + block * BLOCK, BLOCK)
                        ref[rows, :] = value[:, block * BLOCK : (block + 1) * BLOCK]
                else:
                    ref[pl.ds(row, HALF), :] = value.astype(jnp.bfloat16)


PROJECT_ORDER = [(1, "kv_a"), (2, "kv_a"), (0, "q_b"), (1, "kv_b"), (2, "kv_b"), (0, "q_a")]


def project(core, tokens, sibling, w_row):
    depth = tokens.shape[1]

    def weight_block(j, c):
        kind = lax.rem(j + 1, 3)
        pair = jnp.where((j >= 2) & (j <= 4), 1, 0)
        return (0, 4 * kind + 2 * c[0] + pair)

    whole = lambda rows, width: pl.BlockSpec((rows, width), lambda j, c: (0, 0))
    outs = [(2 * STRIDE, BLOCK), (2 * STRIDE, BLOCK), (STRIDE, BLOCK), (STRIDE, BLOCK)]
    return pl.pallas_call(
        project_kernel,
        grid_spec=pltpu.PrefetchScalarGridSpec(
            num_scalar_prefetch=1,
            grid=(len(PROJECT_ORDER),),
            in_specs=[
                whole(HALF, depth),
                whole(HALF, depth),
                pl.BlockSpec((depth, BLOCK), weight_block),
            ],
            out_specs=[whole(*shape) for shape in outs],
        ),
        out_shape=[jax.ShapeDtypeStruct(shape, jnp.bfloat16) for shape in outs],
        compiler_params=params(),
        cost_estimate=cost(PROJECT_COST),
        name="project",
    )(core, tokens, sibling, w_row)


def score_blocks(query, key_ref, columns, spans):
    return [
        lax.dot_general(
            key_ref[low:high, columns], query, (((1,), (1,)), ((), ())),
            preferred_element_type=jnp.float32,
        )
        for low, high in spans
    ]


def softmax_out(scores, biases, value_t_blocks):
    scores = [s if b is None else s + b for s, b in zip(scores, biases)]
    top = functools.reduce(jnp.maximum, [jnp.max(s, axis=0, keepdims=True) for s in scores])
    expd = [jnp.exp2((s - top) * SCALE2) for s in scores]
    total = sum(jnp.sum(e, axis=0, keepdims=True) for e in expd)
    out = sum(
        jnp.dot(v, e.astype(jnp.bfloat16), preferred_element_type=jnp.float32)
        for v, e in zip(value_t_blocks, expd)
    )
    return out, top, total


def pipelined(jobs, ahead, start, finish):
    pending, results = [], {}
    for job in jobs:
        pending.append((job, start(*job)))
        if len(pending) > ahead:
            first, value = pending.pop(0)
            results[first] = finish(*first, value)
    for first, value in pending:
        results[first] = finish(*first, value)
    return results


def split3(value):
    high = value.astype(jnp.bfloat16).astype(jnp.float32)
    rest = value - high
    mid = rest.astype(jnp.bfloat16).astype(jnp.float32)
    return [high, mid, rest - mid]


def columns_of(head):
    return slice(head * HEAD, (head + 1) * HEAD)


def band_jobs(earlier, ahead, q_ref, kv_ref, bias, finish):
    def spans(part):
        low, high = part * BLOCK, (part + 1) * BLOCK
        rest = (high, STRIDE) if earlier else (0, low)
        return [(low, high)] + ([rest] if rest[0] < rest[1] else [])

    def values_t(head, low, high):
        rows = lambda at: slice(STRIDE + at + head * HEAD, STRIDE + at + (head + 1) * HEAD)
        return jnp.concatenate([kv_ref[rows(at), :] for at in range(low, high, BLOCK)], axis=1)

    def start(part, head):
        query = q_ref[part * BLOCK : (part + 1) * BLOCK, columns_of(head)]
        return score_blocks(query, kv_ref, columns_of(head), spans(part))

    def end(part, head, scores):
        values = [values_t(head, low, high) for low, high in spans(part)]
        return finish(part, head, scores, [bias, None], values)

    jobs = [(part, head) for part in range(STRIDE // BLOCK) for head in range(2)]
    return pipelined(jobs, ahead, start, end)


def band_bias(earlier):
    kpos = lax.broadcasted_iota(jnp.int32, (BLOCK, BLOCK), 0)
    qpos = lax.broadcasted_iota(jnp.int32, (BLOCK, BLOCK), 1)
    return jnp.where(kpos > qpos if earlier else kpos <= qpos, 0.0, NEG)


def band_kernel(earlier, pairs, *refs):
    inputs, (out_ref, stat_ref, bias_ref) = refs[: 2 * pairs], refs[2 * pairs :]
    step = pl.program_id(0)
    heads = 2 * pairs

    @pl.when(step == 0)
    def _():
        bias_ref[...] = band_bias(earlier)

    def attend(pair):
        def finish(part, head, scores, biases, values):
            out, top, total = softmax_out(scores, biases, values)
            queries = slice(part * BLOCK, (part + 1) * BLOCK)
            row = (2 * pair + head) * HEAD
            out = out * (1.0 / total)
            out_ref[row : row + HEAD, queries] = out.astype(jnp.bfloat16)
            stat_ref[2 * pair + head, :, queries] = jnp.concatenate(
                split3(top) + split3(total) + [jnp.zeros((2, BLOCK), jnp.float32)], axis=0
            )

        ahead = 2 if earlier else 4
        band_jobs(earlier, ahead, *inputs[2 * pair : 2 * pair + 2], bias_ref[...], finish)

    for pair in range(pairs):

        @pl.when(step == pair)
        def _():
            attend(pair)

    @pl.when(step == pairs - 1)
    def _():
        stats = jnp.concatenate([stat_ref[h] for h in range(heads)], axis=0)
        out_ref[heads * HEAD :, :] = stats.astype(jnp.bfloat16)


def band_part(earlier, *inputs, estimate):
    pairs = len(inputs) // 2
    payload = (2 * pairs * (HEAD + 8), STRIDE)
    whole = lambda shape: pl.BlockSpec(shape, lambda j: (0, 0))
    return pl.pallas_call(
        functools.partial(band_kernel, earlier, pairs),
        grid=(pairs,),
        in_specs=[whole(value.shape) for value in inputs],
        out_specs=whole(payload),
        scratch_shapes=[
            pltpu.VMEM((2 * pairs, 8, STRIDE), jnp.float32),
            pltpu.VMEM((BLOCK, BLOCK), jnp.float32),
        ],
        out_shape=(jax.ShapeDtypeStruct if earlier else pltpu.HBM)(payload, jnp.bfloat16),
        compiler_params=params(),
        cost_estimate=cost(estimate),
        name="band_earlier" if earlier else "band_local",
    )(*inputs)


def complete_kernel(flags_ref, q_ref, kv_ref, local_ref, earlier_ref, same_ref, cross_ref, bias_ref):
    core = flags_ref[0]
    has_earlier = flags_ref[1] > 0
    bias_ref[...] = band_bias(True)

    def stats(ref, heads, head, queries):
        rows = ref[heads * HEAD :, queries].astype(jnp.float32)[8 * head : 8 * head + 8]
        return rows[0:1] + rows[1:2] + rows[2:3], rows[3:4] + rows[4:5] + rows[5:6]

    def merge(part, head, out_e, top_e, scale_e, sum_e):
        queries = slice(part * BLOCK, (part + 1) * BLOCK)
        top_l, sum_l = stats(local_ref, 4, head, queries)
        top_e = jnp.where(has_earlier, top_e, NEG)
        top = jnp.maximum(top_l, top_e)
        weight_l = jnp.exp2((top_l - top) * SCALE2) * sum_l
        weight_e = jnp.where(has_earlier, jnp.exp2((top_e - top) * SCALE2), 0.0)
        inverse = 1.0 / (weight_l + weight_e * sum_e)
        out_l = local_ref[columns_of(head), queries].astype(jnp.float32)
        out = out_l * (weight_l * inverse) + out_e * (weight_e * scale_e * inverse)
        return out.T.astype(jnp.bfloat16)

    def finish(part, head, scores, biases, values):
        out, top, total = softmax_out(scores, biases, values)
        return merge(part, head, out, top, 1.0, total)

    results = band_jobs(True, 2, q_ref, kv_ref, bias_ref[...], finish)
    for part in range(STRIDE // BLOCK):
        queries = slice(part * BLOCK, (part + 1) * BLOCK)
        for head in range(2):
            top, total = stats(earlier_ref, 2, head, queries)
            out = earlier_ref[columns_of(head), queries].astype(jnp.float32)
            results[part, 2 + head] = merge(part, 2 + head, out, top, total, total)

    def store(ref, half):
        for part in range(2):
            for head in range(4):
                rows = slice(part * BLOCK, (part + 1) * BLOCK)
                ref[rows, columns_of(head)] = results[2 * half + part, head]

    @pl.when(core == 0)
    def _():
        store(same_ref, 0)
        store(cross_ref, 1)

    @pl.when(core == 1)
    def _():
        store(same_ref, 1)
        store(cross_ref, 0)


def complete(flags, query, keyval, local, earlier):
    inputs = [query, keyval, local, earlier]
    return pl.pallas_call(
        complete_kernel,
        grid_spec=pltpu.PrefetchScalarGridSpec(
            num_scalar_prefetch=1,
            grid=(1,),
            in_specs=[pl.BlockSpec(value.shape, lambda j, c: (0, 0)) for value in inputs],
            out_specs=[
                pl.BlockSpec((HALF, HALF), lambda j, c: (0, c[0])),
                pl.BlockSpec((HALF, HALF), lambda j, c: (0, 0)),
            ],
            scratch_shapes=[pltpu.VMEM((BLOCK, BLOCK), jnp.float32)],
        ),
        out_shape=[
            jax.ShapeDtypeStruct((HALF, 2 * HEADS * HEAD), jnp.bfloat16),
            jax.ShapeDtypeStruct((HALF, HALF), jnp.bfloat16),
        ],
        compiler_params=params(),
        cost_estimate=cost(COMPLETE_COST),
        name="complete",
    )(flags, *inputs)


def place_kernel(flags_ref, values_ref, _, o_ref, sems, *, cross):
    width = values_ref.shape[1]
    if cross:
        first = pl.multiple_of((1 - flags_ref[0]) * HALF, HALF)
    else:
        first = width
    count = sems.shape[0]
    rows = [pl.ds(index * (HALF // count), HALF // count) for index in range(count)]
    copies = [
        pltpu.make_async_copy(
            values_ref.at[part, :], o_ref.at[part, pl.ds(first, width)], sems.at[index]
        )
        for index, part in enumerate(rows)
    ]
    for copy in copies:
        copy.start()
    for copy in copies:
        copy.wait()


def place(flags, values, result, cross):
    anywhere = pl.BlockSpec(memory_space=pl.ANY)
    return pl.pallas_call(
        functools.partial(place_kernel, cross=cross),
        grid_spec=pltpu.PrefetchScalarGridSpec(
            num_scalar_prefetch=1,
            grid=(1,),
            in_specs=[anywhere] * 2,
            out_specs=anywhere,
            scratch_shapes=[pltpu.SemaphoreType.DMA((8,))],
        ),
        out_shape=jax.ShapeDtypeStruct(result.shape, jnp.bfloat16),
        input_output_aliases={2: 0},
        compiler_params=params(),
        cost_estimate=cost(1),
        name="place_cross" if cross else "place_columns",
    )(flags, values, result)


def column_kernel(group, q_ref, k_ref, v_ref, o_ref, bias_ref):
    parts = HALF // BLOCK
    heads = q_ref.shape[1] // HEAD

    @pl.when(pl.program_id(0) == 0)
    def _():
        qpos = lax.broadcasted_iota(jnp.int32, (BLOCK, BLOCK), 0)
        kpos = lax.broadcasted_iota(jnp.int32, (BLOCK, BLOCK), 1)
        column = ((qpos - kpos) & (group - 1)) == 0
        bias_ref[0] = jnp.where(column, 0.0, NEG)
        bias_ref[1] = jnp.where(column & (kpos <= qpos), 0.0, NEG)

    def rows(block):
        return slice(block * BLOCK, (block + 1) * BLOCK)

    def start(part, head):
        query = q_ref[rows(part), columns_of(head)]
        return [
            lax.dot_general(
                query, k_ref[rows(block), columns_of(head)], (((1,), (1,)), ((), ())),
                preferred_element_type=jnp.float32,
            )
            for block in range(part + 1)
        ]

    def finish(part, head, scores):
        scores = [s + bias_ref[1 if block == part else 0] for block, s in enumerate(scores)]
        top = jnp.max(functools.reduce(jnp.maximum, scores), axis=1, keepdims=True)
        out = 0.0
        for block, s in enumerate(scores):
            values = v_ref[rows(block), columns_of(head)]
            values = jnp.concatenate([values, jnp.ones_like(values)], axis=1)
            expd = jnp.exp2((s - top) * SCALE2).astype(jnp.bfloat16)
            out = out + jnp.dot(expd, values, preferred_element_type=jnp.float32)
        out = out[:, :HEAD] * (1.0 / out[:, HEAD:])
        o_ref[rows(part), columns_of(head)] = out.astype(jnp.bfloat16)

    pipelined([(part, head) for part in range(parts) for head in range(heads)], 4, start, finish)


def column_attention(projected, group):
    rows = projected.shape[0]
    heads = 4
    steps = HEADS // heads
    spec = lambda third: pl.BlockSpec((rows, heads * HEAD), lambda j: (0, third * steps + j))
    return pl.pallas_call(
        functools.partial(column_kernel, group),
        grid=(steps,),
        in_specs=[spec(0), spec(1), spec(2)],
        out_specs=pl.BlockSpec((rows, heads * HEAD), lambda j: (0, j)),
        out_shape=jax.ShapeDtypeStruct((rows, HEADS * HEAD), jnp.bfloat16),
        scratch_shapes=[pltpu.VMEM((2, BLOCK, BLOCK), jnp.float32)],
        compiler_params=params(),
        cost_estimate=cost(6),
        name="column_attention",
    )(projected, projected, projected)


def in_hbm(value):
    return pltpu.with_memory_space_constraint(value, pltpu.HBM)


def after(value, *others):
    return lax.optimization_barrier((value,) + others)[0]


def on_device(tokens, w_row, w_column):
    count = lax.axis_size("seq")
    chips = count // 2
    rank = lax.axis_index("seq")
    core = (rank % 2).astype(jnp.int32)
    core_arr = core.reshape(1)
    flags = jnp.stack([core, (rank >= 2).astype(jnp.int32)])
    group = HALF // chips
    same_core = [list(range(0, count, 2)), list(range(1, count, 2))]

    def exchange(value):
        width = value.shape[1]
        value = lax.all_to_all(
            value.reshape(chips, group, width), "seq", split_axis=0, concat_axis=0,
            axis_index_groups=same_core, tiled=True,
        )
        return value.reshape(HALF, width)

    def swapped(value):
        return lax.ppermute(value, "seq", [(d, d ^ 1) for d in range(count)])

    def to_next(value):
        return lax.ppermute(value, "seq", [(d, d + 2) for d in range(count - 2)])

    w_row = in_hbm(w_row)
    columns = exchange(tokens)
    sibling = swapped(tokens)
    kv_a, kv_b, q_a, q_b = project(core_arr, tokens, sibling, w_row)
    previous_kv_a = to_next(kv_a)
    next_q_b = lax.ppermute(q_b, "seq", [(d, d - 2) for d in range(2, count)])
    local = band_part(False, q_a, kv_a, q_b, kv_b, estimate=LOCAL_COST)
    columns = after(columns, local)
    col_proj = jnp.dot(columns, w_column, preferred_element_type=jnp.float32).astype(jnp.bfloat16)
    sent_b = band_part(True, after(next_q_b, col_proj), kv_b, estimate=B_COST)
    earlier_b = to_next(sent_b)
    col_out = column_attention(after(col_proj, sent_b), group)
    result, cross = complete(flags, q_a, after(previous_kv_a, col_out), in_hbm(local), earlier_b)
    result = place(flags, swapped(cross), result, True)
    return place(flags, exchange(col_out), result, False)


def solution(mesh):
    in_specs = (P("seq", None), P(), P())
    out_specs = P("seq", None)
    return jax.shard_map(
        on_device, mesh=mesh, in_specs=in_specs, out_specs=out_specs, check_vma=False
    )
```

```python
import functools
import math

import jax
import jax.numpy as jnp
from jax import lax
from jax.experimental import pallas as pl
from jax.experimental.pallas import tpu as pltpu
from jax.sharding import PartitionSpec as P

HEAD = 128
HEADS = 8
STRIDE = 1024
HALF = 512
BLOCK = 256
SCALE2 = math.log2(math.e) / math.sqrt(HEAD)
NEG = -1e30
VMEM_LIMIT = 28 << 20
PROJECT_COST, LOCAL_COST, B_COST, COMPLETE_COST = 0.5, 0.5, 0.5, 20


def params():
    return pltpu.CompilerParams(vmem_limit_bytes=VMEM_LIMIT)


def cost(us):
    return pl.CostEstimate(flops=int(us * 10**9), bytes_accessed=1 << 14, transcendentals=0)


def project_kernel(core_ref, own_ref, sibling_ref, w_ref, kv_a, kv_b, q_a, q_b):
    core = core_ref[0]
    for step, (kind, ref) in enumerate(PROJECT_ORDER):
        ref = {"kv_a": kv_a, "kv_b": kv_b, "q_a": q_a, "q_b": q_b}[ref]

        @pl.when(pl.program_id(0) == step)
        def _():
            for place, x_ref in ((core, own_ref), (1 - core, sibling_ref)):
                value = jnp.dot(x_ref[...], w_ref[...], preferred_element_type=jnp.float32)
                row = pl.multiple_of(place * HALF, HALF)
                if kind == 2:
                    value = value.T.astype(jnp.bfloat16)
                    for block in range(HALF // BLOCK):
                        rows = pl.ds(STRIDE + row + block * BLOCK, BLOCK)
                        ref[rows, :] = value[:, block * BLOCK : (block + 1) * BLOCK]
                else:
                    ref[pl.ds(row, HALF), :] = value.astype(jnp.bfloat16)


PROJECT_ORDER = [(1, "kv_a"), (2, "kv_a"), (0, "q_b"), (1, "kv_b"), (2, "kv_b"), (0, "q_a")]


def project(core, tokens, sibling, w_row):
    depth = tokens.shape[1]

    def weight_block(j, c):
        kind = lax.rem(j + 1, 3)
        pair = jnp.where((j >= 2) & (j <= 4), 1, 0)
        return (0, 4 * kind + 2 * c[0] + pair)

    whole = lambda rows, width: pl.BlockSpec((rows, width), lambda j, c: (0, 0))
    outs = [(2 * STRIDE, BLOCK), (2 * STRIDE, BLOCK), (STRIDE, BLOCK), (STRIDE, BLOCK)]
    return pl.pallas_call(
        project_kernel,
        grid_spec=pltpu.PrefetchScalarGridSpec(
            num_scalar_prefetch=1,
            grid=(len(PROJECT_ORDER),),
            in_specs=[
                whole(HALF, depth),
                whole(HALF, depth),
                pl.BlockSpec((depth, BLOCK), weight_block),
            ],
            out_specs=[whole(*shape) for shape in outs],
        ),
        out_shape=[jax.ShapeDtypeStruct(shape, jnp.bfloat16) for shape in outs],
        compiler_params=params(),
        cost_estimate=cost(PROJECT_COST),
        name="project",
    )(core, tokens, sibling, w_row)


def score_blocks(query, key_ref, columns, spans):
    return [
        lax.dot_general(
            key_ref[low:high, columns], query, (((1,), (1,)), ((), ())),
            preferred_element_type=jnp.float32,
        )
        for low, high in spans
    ]


def softmax_out(scores, biases, value_t_blocks):
    scores = [s if b is None else s + b for s, b in zip(scores, biases)]
    top = functools.reduce(jnp.maximum, [jnp.max(s, axis=0, keepdims=True) for s in scores])
    expd = [jnp.exp2((s - top) * SCALE2) for s in scores]
    total = sum(jnp.sum(e, axis=0, keepdims=True) for e in expd)
    out = sum(
        jnp.dot(v, e.astype(jnp.bfloat16), preferred_element_type=jnp.float32)
        for v, e in zip(value_t_blocks, expd)
    )
    return out, top, total


def pipelined(jobs, ahead, start, finish):
    pending, results = [], {}
    for job in jobs:
        pending.append((job, start(*job)))
        if len(pending) > ahead:
            first, value = pending.pop(0)
            results[first] = finish(*first, value)
    for first, value in pending:
        results[first] = finish(*first, value)
    return results


def split3(value):
    high = value.astype(jnp.bfloat16).astype(jnp.float32)
    rest = value - high
    mid = rest.astype(jnp.bfloat16).astype(jnp.float32)
    return [high, mid, rest - mid]


def columns_of(head):
    return slice(head * HEAD, (head + 1) * HEAD)


def band_jobs(earlier, ahead, q_ref, kv_ref, bias, finish):
    def spans(part):
        low, high = part * BLOCK, (part + 1) * BLOCK
        rest = (high, STRIDE) if earlier else (0, low)
        return [(low, high)] + ([rest] if rest[0] < rest[1] else [])

    def values_t(head, low, high):
        rows = lambda at: slice(STRIDE + at + head * HEAD, STRIDE + at + (head + 1) * HEAD)
        return jnp.concatenate([kv_ref[rows(at), :] for at in range(low, high, BLOCK)], axis=1)

    def start(part, head):
        query = q_ref[part * BLOCK : (part + 1) * BLOCK, columns_of(head)]
        return score_blocks(query, kv_ref, columns_of(head), spans(part))

    def end(part, head, scores):
        values = [values_t(head, low, high) for low, high in spans(part)]
        return finish(part, head, scores, [bias, None], values)

    jobs = [(part, head) for part in range(STRIDE // BLOCK) for head in range(2)]
    return pipelined(jobs, ahead, start, end)


def band_bias(earlier):
    kpos = lax.broadcasted_iota(jnp.int32, (BLOCK, BLOCK), 0)
    qpos = lax.broadcasted_iota(jnp.int32, (BLOCK, BLOCK), 1)
    return jnp.where(kpos > qpos if earlier else kpos <= qpos, 0.0, NEG)


def band_kernel(earlier, pairs, *refs):
    inputs, (out_ref, stat_ref, bias_ref) = refs[: 2 * pairs], refs[2 * pairs :]
    step = pl.program_id(0)
    heads = 2 * pairs

    @pl.when(step == 0)
    def _():
        bias_ref[...] = band_bias(earlier)

    def attend(pair):
        def finish(part, head, scores, biases, values):
            out, top, total = softmax_out(scores, biases, values)
            queries = slice(part * BLOCK, (part + 1) * BLOCK)
            row = (2 * pair + head) * HEAD
            out = out * (1.0 / total)
            out_ref[row : row + HEAD, queries] = out.astype(jnp.bfloat16)
            stat_ref[2 * pair + head, :, queries] = jnp.concatenate(
                split3(top) + split3(total) + [jnp.zeros((2, BLOCK), jnp.float32)], axis=0
            )

        ahead = 2 if earlier else 4
        band_jobs(earlier, ahead, *inputs[2 * pair : 2 * pair + 2], bias_ref[...], finish)

    for pair in range(pairs):

        @pl.when(step == pair)
        def _():
            attend(pair)

    @pl.when(step == pairs - 1)
    def _():
        stats = jnp.concatenate([stat_ref[h] for h in range(heads)], axis=0)
        out_ref[heads * HEAD :, :] = stats.astype(jnp.bfloat16)


def band_part(earlier, *inputs, estimate):
    pairs = len(inputs) // 2
    payload = (2 * pairs * (HEAD + 8), STRIDE)
    whole = lambda shape: pl.BlockSpec(shape, lambda j: (0, 0))
    return pl.pallas_call(
        functools.partial(band_kernel, earlier, pairs),
        grid=(pairs,),
        in_specs=[whole(value.shape) for value in inputs],
        out_specs=whole(payload),
        scratch_shapes=[
            pltpu.VMEM((2 * pairs, 8, STRIDE), jnp.float32),
            pltpu.VMEM((BLOCK, BLOCK), jnp.float32),
        ],
        out_shape=(jax.ShapeDtypeStruct if earlier else pltpu.HBM)(payload, jnp.bfloat16),
        compiler_params=params(),
        cost_estimate=cost(estimate),
        name="band_earlier" if earlier else "band_local",
    )(*inputs)


def complete_kernel(flags_ref, q_ref, kv_ref, local_ref, earlier_ref, same_ref, cross_ref, bias_ref):
    core = flags_ref[0]
    has_earlier = flags_ref[1] > 0
    bias_ref[...] = band_bias(True)

    def stats(ref, heads, head, queries):
        rows = ref[heads * HEAD :, queries].astype(jnp.float32)[8 * head : 8 * head + 8]
        return rows[0:1] + rows[1:2] + rows[2:3], rows[3:4] + rows[4:5] + rows[5:6]

    def merge(part, head, out_e, top_e, scale_e, sum_e):
        queries = slice(part * BLOCK, (part + 1) * BLOCK)
        top_l, sum_l = stats(local_ref, 4, head, queries)
        top_e = jnp.where(has_earlier, top_e, NEG)
        top = jnp.maximum(top_l, top_e)
        weight_l = jnp.exp2((top_l - top) * SCALE2) * sum_l
        weight_e = jnp.where(has_earlier, jnp.exp2((top_e - top) * SCALE2), 0.0)
        inverse = 1.0 / (weight_l + weight_e * sum_e)
        out_l = local_ref[columns_of(head), queries].astype(jnp.float32)
        out = out_l * (weight_l * inverse) + out_e * (weight_e * scale_e * inverse)
        return out.T.astype(jnp.bfloat16)

    def finish(part, head, scores, biases, values):
        out, top, total = softmax_out(scores, biases, values)
        return merge(part, head, out, top, 1.0, total)

    results = band_jobs(True, 2, q_ref, kv_ref, bias_ref[...], finish)
    for part in range(STRIDE // BLOCK):
        queries = slice(part * BLOCK, (part + 1) * BLOCK)
        for head in range(2):
            top, total = stats(earlier_ref, 2, head, queries)
            out = earlier_ref[columns_of(head), queries].astype(jnp.float32)
            results[part, 2 + head] = merge(part, 2 + head, out, top, total, total)

    def store(ref, half):
        for part in range(2):
            for head in range(4):
                rows = slice(part * BLOCK, (part + 1) * BLOCK)
                ref[rows, columns_of(head)] = results[2 * half + part, head]

    @pl.when(core == 0)
    def _():
        store(same_ref, 0)
        store(cross_ref, 1)

    @pl.when(core == 1)
    def _():
        store(same_ref, 1)
        store(cross_ref, 0)


def complete(flags, query, keyval, local, earlier):
    inputs = [query, keyval, local, earlier]
    return pl.pallas_call(
        complete_kernel,
        grid_spec=pltpu.PrefetchScalarGridSpec(
            num_scalar_prefetch=1,
            grid=(1,),
            in_specs=[pl.BlockSpec(value.shape, lambda j, c: (0, 0)) for value in inputs],
            out_specs=[
                pl.BlockSpec((HALF, HALF), lambda j, c: (0, c[0])),
                pl.BlockSpec((HALF, HALF), lambda j, c: (0, 0)),
            ],
            scratch_shapes=[pltpu.VMEM((BLOCK, BLOCK), jnp.float32)],
        ),
        out_shape=[
            jax.ShapeDtypeStruct((HALF, 2 * HEADS * HEAD), jnp.bfloat16),
            jax.ShapeDtypeStruct((HALF, HALF), jnp.bfloat16),
        ],
        compiler_params=params(),
        cost_estimate=cost(COMPLETE_COST),
        name="complete",
    )(flags, *inputs)


def place_kernel(flags_ref, values_ref, _, o_ref, sems, *, cross):
    width = values_ref.shape[1]
    if cross:
        first = pl.multiple_of((1 - flags_ref[0]) * HALF, HALF)
    else:
        first = width
    count = sems.shape[0]
    rows = [pl.ds(index * (HALF // count), HALF // count) for index in range(count)]
    copies = [
        pltpu.make_async_copy(
            values_ref.at[part, :], o_ref.at[part, pl.ds(first, width)], sems.at[index]
        )
        for index, part in enumerate(rows)
    ]
    for copy in copies:
        copy.start()
    for copy in copies:
        copy.wait()


def place(flags, values, result, cross):
    anywhere = pl.BlockSpec(memory_space=pl.ANY)
    return pl.pallas_call(
        functools.partial(place_kernel, cross=cross),
        grid_spec=pltpu.PrefetchScalarGridSpec(
            num_scalar_prefetch=1,
            grid=(1,),
            in_specs=[anywhere] * 2,
            out_specs=anywhere,
            scratch_shapes=[pltpu.SemaphoreType.DMA((8,))],
        ),
        out_shape=jax.ShapeDtypeStruct(result.shape, jnp.bfloat16),
        input_output_aliases={2: 0},
        compiler_params=params(),
        cost_estimate=cost(1),
        name="place_cross" if cross else "place_columns",
    )(flags, values, result)


def column_kernel(group, q_ref, k_ref, v_ref, o_ref, bias_ref):
    parts = HALF // BLOCK
    heads = q_ref.shape[1] // HEAD

    @pl.when(pl.program_id(0) == 0)
    def _():
        qpos = lax.broadcasted_iota(jnp.int32, (BLOCK, BLOCK), 0)
        kpos = lax.broadcasted_iota(jnp.int32, (BLOCK, BLOCK), 1)
        column = ((qpos - kpos) & (group - 1)) == 0
        bias_ref[0] = jnp.where(column, 0.0, NEG)
        bias_ref[1] = jnp.where(column & (kpos <= qpos), 0.0, NEG)

    def rows(block):
        return slice(block * BLOCK, (block + 1) * BLOCK)

    def start(part, head):
        query = q_ref[rows(part), columns_of(head)]
        return [
            lax.dot_general(
                query, k_ref[rows(block), columns_of(head)], (((1,), (1,)), ((), ())),
                preferred_element_type=jnp.float32,
            )
            for block in range(part + 1)
        ]

    def finish(part, head, scores):
        scores = [s + bias_ref[1 if block == part else 0] for block, s in enumerate(scores)]
        top = jnp.max(functools.reduce(jnp.maximum, scores), axis=1, keepdims=True)
        out = 0.0
        for block, s in enumerate(scores):
            values = v_ref[rows(block), columns_of(head)]
            values = jnp.concatenate([values, jnp.ones_like(values)], axis=1)
            expd = jnp.exp2((s - top) * SCALE2).astype(jnp.bfloat16)
            out = out + jnp.dot(expd, values, preferred_element_type=jnp.float32)
        out = out[:, :HEAD] * (1.0 / out[:, HEAD:])
        o_ref[rows(part), columns_of(head)] = out.astype(jnp.bfloat16)

    pipelined([(part, head) for part in range(parts) for head in range(heads)], 4, start, finish)


def column_attention(projected, group):
    rows = projected.shape[0]
    heads = 8
    steps = HEADS // heads
    spec = lambda third: pl.BlockSpec((rows, heads * HEAD), lambda j: (0, third * steps + j))
    return pl.pallas_call(
        functools.partial(column_kernel, group),
        grid=(steps,),
        in_specs=[spec(0), spec(1), spec(2)],
        out_specs=pl.BlockSpec((rows, heads * HEAD), lambda j: (0, j)),
        out_shape=jax.ShapeDtypeStruct((rows, HEADS * HEAD), jnp.bfloat16),
        scratch_shapes=[pltpu.VMEM((2, BLOCK, BLOCK), jnp.float32)],
        compiler_params=params(),
        cost_estimate=cost(6),
        name="column_attention",
    )(projected, projected, projected)


def in_hbm(value):
    return pltpu.with_memory_space_constraint(value, pltpu.HBM)


def after(value, *others):
    return lax.optimization_barrier((value,) + others)[0]


def on_device(tokens, w_row, w_column):
    count = lax.axis_size("seq")
    chips = count // 2
    rank = lax.axis_index("seq")
    core = (rank % 2).astype(jnp.int32)
    core_arr = core.reshape(1)
    flags = jnp.stack([core, (rank >= 2).astype(jnp.int32)])
    group = HALF // chips
    same_core = [list(range(0, count, 2)), list(range(1, count, 2))]

    def exchange(value):
        width = value.shape[1]
        value = lax.all_to_all(
            value.reshape(chips, group, width), "seq", split_axis=0, concat_axis=0,
            axis_index_groups=same_core, tiled=True,
        )
        return value.reshape(HALF, width)

    def swapped(value):
        return lax.ppermute(value, "seq", [(d, d ^ 1) for d in range(count)])

    def to_next(value):
        return lax.ppermute(value, "seq", [(d, d + 2) for d in range(count - 2)])

    w_row = in_hbm(w_row)
    columns = exchange(tokens)
    sibling = swapped(tokens)
    kv_a, kv_b, q_a, q_b = project(core_arr, tokens, sibling, w_row)
    previous_kv_a = to_next(kv_a)
    next_q_b = lax.ppermute(q_b, "seq", [(d, d - 2) for d in range(2, count)])
    local = band_part(False, q_a, kv_a, q_b, kv_b, estimate=LOCAL_COST)
    columns = after(columns, local)
    col_proj = jnp.dot(columns, w_column, preferred_element_type=jnp.float32).astype(jnp.bfloat16)
    sent_b = band_part(True, after(next_q_b, col_proj), kv_b, estimate=B_COST)
    earlier_b = to_next(sent_b)
    col_out = column_attention(after(col_proj, sent_b), group)
    result, cross = complete(flags, q_a, after(previous_kv_a, col_out), in_hbm(local), earlier_b)
    result = place(flags, swapped(cross), result, True)
    return place(flags, exchange(col_out), result, False)


def solution(mesh):
    in_specs = (P("seq", None), P(), P())
    out_specs = P("seq", None)
    return jax.shard_map(
        on_device, mesh=mesh, in_specs=in_specs, out_specs=out_specs, check_vma=False
    )
```
